32 devices in a mesh: fsdp: 4 (over y, x), context: 4 (over z), tensor: 2 (over core).
Axes of the slice: x: 2, y: 2, z: 4, core: 2. Of those that a mesh axis runs over, the one named last changes fastest.
Arguments:
- tokens: bfloat16 [8192, 1536], P(('fsdp', 'context')), may hold values from -6 to 6
- block_order: int32 [4, 4], P('fsdp'), may hold values from 0 to 3, as said below
- norm_one: bfloat16 [1536], P(('fsdp', 'context')), may hold values from 0.5 to 1.5
- w_query: bfloat16 [1536, 1536], P(('fsdp', 'context'), 'tensor'), may hold values from -0.15625 to 0.15625
- b_query: bfloat16 [2, 768], P('tensor', ('fsdp', 'context')), may hold values from -3 to 3
- w_key: bfloat16 [1536, 256], P(('fsdp', 'context'), 'tensor'), may hold values from -0.15625 to 0.15625
- b_key: bfloat16 [2, 128], P('tensor', ('fsdp', 'context')), may hold values from -3 to 3
- w_value: bfloat16 [1536, 256], P(('fsdp', 'context'), 'tensor'), may hold values from -0.15625 to 0.15625
- b_value: bfloat16 [2, 128], P('tensor', ('fsdp', 'context')), may hold values from -3 to 3
- w_out: bfloat16 [1536, 1536], P('tensor', ('fsdp', 'context')), may hold values from -3 to 3
- norm_two: bfloat16 [1536], P(('fsdp', 'context')), may hold values from 0.099609375 to 1.8984375
- w_gate: bfloat16 [1536, 8960], P(('fsdp', 'context'), 'tensor'), may hold values from -0.15625 to 0.15625
- w_up: bfloat16 [1536, 8960], P(('fsdp', 'context'), 'tensor'), may hold values from -0.15625 to 0.15625
- w_down: bfloat16 [8960, 1536], P('tensor', ('fsdp', 'context')), may hold values from -0.25 to 0.25
- cotangent: bfloat16 [8192, 1536], P(('fsdp', 'context')), may hold values from -6 to 6
Outputs:
- result: bfloat16 [8192, 1536], P(('fsdp', 'context'))
- grad_tokens: bfloat16 [8192, 1536], P(('fsdp', 'context'))
- grad_norm_one: float32 [1536], P(('fsdp', 'context'))
- grad_w_query: float32 [1536, 1536], P(('fsdp', 'context'), 'tensor')
- grad_b_query: float32 [2, 768], P('tensor', ('fsdp', 'context'))
- grad_w_key: float32 [1536, 256], P(('fsdp', 'context'), 'tensor')
- grad_b_key: float32 [2, 128], P('tensor', ('fsdp', 'context'))
- grad_w_value: float32 [1536, 256], P(('fsdp', 'context'), 'tensor')
- grad_b_value: float32 [2, 128], P('tensor', ('fsdp', 'context'))
- grad_w_out: float32 [1536, 1536], P('tensor', ('fsdp', 'context'))
- grad_norm_two: float32 [1536], P(('fsdp', 'context'))
- grad_w_gate: float32 [1536, 8960], P(('fsdp', 'context'), 'tensor')
- grad_w_up: float32 [1536, 8960], P(('fsdp', 'context'), 'tensor')
- grad_w_down: float32 [8960, 1536], P('tensor', ('fsdp', 'context'))
The draws below stay inside these ranges and needn't reach their ends.
Inputs may be any that keep to these rules, and one draw needn't show every extreme that they name: Each row of block_order is an ordering of the 4 token blocks 0 to 3 of a group, each once.
All inputs are finite; a program needn't handle non-finite values.
Results may differ from the reference program's by a relative error of at most 0.039.
Values may be sent and summed in bfloat16 or wider, within the bound.
No kernel may reach another device: no remote copies, remote signals or barrier semaphores. Data moves between devices by JAX's collectives and lax.ppermute only.
A program may use at most 256 MiB of HBM per device.

```python
from functools import partial
import jax
import jax.numpy as jnp
from jax import lax

D = 1536
FF = 8960
H = 12
KVH = 2
HD = 128
BLK = 512
QPK = 6
GROUPS = 4
SLOTS = 4
TOKENS = 8192


def draw_block_order(key, part):
    row_keys = jax.random.split(jax.random.fold_in(key, 7), GROUPS)
    return jax.vmap(lambda row_key: jax.random.permutation(row_key, SLOTS))(row_keys).astype(jnp.int32)


def levels(stream_key, shape, cuts, low, largest):
    def one(dim, blocks):
        draws = jax.random.uniform(jax.random.fold_in(jax.random.fold_in(stream_key, 6), dim), (blocks,), jnp.float32, low / len(cuts), largest / len(cuts))
        return jnp.repeat(jnp.exp(draws), shape[dim] // blocks).reshape((-1,) + (1,) * (len(shape) - dim - 1))

    factor_of = one(*cuts[0])
    for cut in cuts[1:]:
        factor_of = factor_of * one(*cut)
    return factor_of


def normal_values(key, dims, spread, reach, pieces=(), kind=jnp.bfloat16):
    entries = jax.random.normal(key, dims, jnp.float32) * spread
    if len(pieces) > 0:
        entries = levels(key, dims, pieces, -0.22, 0.18) * entries
    return jnp.clip(entries, min=-reach, max=reach).astype(kind)


def setup_inputs(seed: int = 0) -> dict:
    key_of = jax.random.split(jax.random.key(seed), 16)
    return {
        "tokens": normal_values(key_of[0], (TOKENS, D), 1.0, 6.0, ((0, 16),)),
        "block_order": draw_block_order(jax.random.fold_in(key_of[15], 71), 0),
        "norm_one": jnp.clip(1.0 + 0.1 * jax.random.normal(key_of[2], (D,), jnp.float32), 0.5, 1.5).astype(jnp.bfloat16),
        "w_query": normal_values(key_of[3], (D, H * HD), D ** -0.5, 0.15625, ((0, 16), (1, 2))),
        "b_query": normal_values(key_of[4], (KVH, QPK * HD), 0.5, 3.0, ((0, 2), (1, 16))),
        "w_key": normal_values(key_of[5], (D, KVH * HD), D ** -0.5, 0.15625, ((0, 16), (1, 2))),
        "b_key": normal_values(key_of[6], (KVH, HD), 0.5, 3.0, ((0, 2), (1, 16))),
        "w_value": normal_values(key_of[7], (D, KVH * HD), D ** -0.5, 0.15625, ((0, 16), (1, 2))),
        "b_value": normal_values(key_of[8], (KVH, HD), 0.5, 3.0, ((0, 2), (1, 16))),
        "w_out": normal_values(key_of[9], (H * HD, D), 4 ** -0.5, 3.0, ((0, 2), (1, 16))),
        "norm_two": jnp.clip(1.0 + 0.18 * jax.random.normal(key_of[10], (D,), jnp.float32), 0.099609375, 1.8984375).astype(jnp.bfloat16),
        "w_gate": normal_values(key_of[11], (D, FF), D ** -0.5, 0.15625, ((0, 16), (1, 2))),
        "w_up": normal_values(key_of[12], (D, FF), D ** -0.5, 0.15625, ((0, 16), (1, 2))),
        "w_down": normal_values(key_of[13], (FF, D), (FF // 16) ** -0.5, 0.25, ((0, 2), (1, 16))),
        "cotangent": normal_values(key_of[14], (TOKENS, D), 1.0, 6.0, ((0, 16),)),
    }


EPSILON = 1e-06
ROPE_BASE = 1000000.0
MASKED = -1e+30

@jax.custom_vjp
def low(v):
    return lax.optimization_barrier(v.astype(jnp.bfloat16)).astype(jnp.float32)

@jax.custom_vjp
def low_back(v):
    return v

def low_keep(v):
    return (low(v), None)

def low_pass(kept, grad):
    return (grad,)

def back_keep(v):
    return (v, None)

def back_low(kept, grad):
    return (low(grad),)
low.defvjp(low_keep, low_pass)
low_back.defvjp(back_keep, back_low)

def tables(positions, head_width):
    ladder = jnp.arange(head_width // 2, dtype=jnp.float32)
    inverse = jnp.exp(-jnp.log(ROPE_BASE) * 2.0 * ladder / head_width)
    angles = positions.astype(jnp.float32)[:, None] * inverse[None, :]
    return (jnp.cos(angles), jnp.sin(angles))

def rotate(field, cosine, sine):
    middle = field.shape[-1] // 2
    first_half = field[..., :middle]
    second_half = field[..., middle:]
    cos_rows = cosine[:, None, :]
    sin_rows = sine[:, None, :]
    return jnp.concatenate([first_half * cos_rows - second_half * sin_rows, second_half * cos_rows + first_half * sin_rows], axis=-1)

def attend_block(query_block, query_pos, query_seg, key_group, value_group, key_pos, key_seg):
    exact = lax.Precision.HIGHEST
    block_rows = query_block.shape[0]
    query_heads = query_block.reshape(block_rows, KVH, QPK, HD)
    scores = jnp.einsum('qgpd,kgd->gpqk', query_heads, key_group, precision=exact) * HD ** (-0.5)
    scores = low_back(scores)
    allowed = (key_pos[None, :] <= query_pos[:, None]) & ((key_seg[None, :] == 0) | (key_seg[None, :] == query_seg[:, None]))
    scores = jnp.where(allowed[None, None], scores, MASKED)
    weights = low(jax.nn.softmax(scores, axis=-1))
    mixed = jnp.einsum('gpqk,kgd->qgpd', weights, value_group, precision=exact)
    return mixed.reshape(block_rows, H * HD)

def rms_norm(values, gain):
    return values * lax.rsqrt(lax.optimization_barrier(jnp.mean(values * values, axis=-1, keepdims=True)) + EPSILON) * gain

def forward(cosine, sine, position, segment, inputs, gain_one, query_w, query_b, key_w, key_b, value_w, value_b, out_w, gain_two, gate_w, up_w, down_w):
    exact = lax.Precision.HIGHEST
    rows_count = inputs.shape[0]
    normed_one = low(rms_norm(inputs, gain_one))
    query_lin = low_back(jnp.dot(normed_one, query_w, precision=exact, preferred_element_type=jnp.float32) + query_b.reshape(-1))
    key_lin = low_back(jnp.dot(normed_one, key_w, precision=exact, preferred_element_type=jnp.float32) + key_b.reshape(-1))
    value_lin = low_back(jnp.dot(normed_one, value_w, precision=exact, preferred_element_type=jnp.float32) + value_b.reshape(-1))
    queries = low(rotate(query_lin.reshape(rows_count, H, HD), cosine, sine))
    keys = low(rotate(key_lin.reshape(rows_count, KVH, HD), cosine, sine))
    values = low(value_lin).reshape(rows_count, KVH, HD)
    span = SLOTS * BLK
    query_groups = queries.reshape(GROUPS, SLOTS, BLK, H, HD)
    key_groups = keys.reshape(GROUPS, span, KVH, HD)
    value_groups = values.reshape(GROUPS, span, KVH, HD)
    checked = jax.checkpoint(attend_block)

    def per_group(group_item):
        query_set, key_set, value_set, pos_set, seg_set = group_item

        def per_block(block_item):
            return checked(block_item[0], block_item[1], block_item[2], key_set, value_set, pos_set, seg_set)
        return lax.map(per_block, (query_set, pos_set.reshape(SLOTS, BLK), seg_set.reshape(SLOTS, BLK)))
    mixed = lax.map(per_group, (query_groups, key_groups, value_groups, position.reshape(GROUPS, span), segment.reshape(GROUPS, span)))
    attn_rows = low(low_back(mixed.reshape(rows_count, H * HD)))
    attn_out = low_back(jnp.dot(attn_rows, out_w, precision=exact, preferred_element_type=jnp.float32))
    hidden_one = inputs + attn_out
    normed_two = low(rms_norm(hidden_one, gain_two))
    gate_lin = low_back(jnp.dot(normed_two, gate_w, precision=exact, preferred_element_type=jnp.float32))
    up_lin = low_back(jnp.dot(normed_two, up_w, precision=exact, preferred_element_type=jnp.float32))
    hidden_low = low(jax.nn.silu(gate_lin) * up_lin)
    return hidden_one + jnp.dot(hidden_low, down_w, precision=exact, preferred_element_type=jnp.float32)

def reference(tokens, block_order, norm_one, w_query, b_query, w_key, b_key, w_value, b_value, w_out, norm_two, w_gate, w_up, w_down, cotangent):
    rows_total = tokens.shape[0]
    row_index = jnp.arange(rows_total, dtype=jnp.int32)
    group_of = (row_index // (SLOTS * BLK)).astype(jnp.int32)
    slot_of = (row_index // BLK % SLOTS).astype(jnp.int32)
    blocks = block_order[group_of, slot_of]
    prompt_slots = SLOTS // 2
    segment = jnp.where(blocks < prompt_slots, 0, blocks - prompt_slots + 1).astype(jnp.int32)
    position = (jnp.where(blocks < prompt_slots, blocks * BLK, prompt_slots * BLK) + row_index % BLK).astype(jnp.int32)
    cosine, sine = tables(position, HD)
    floats = (tokens, norm_one, w_query, b_query, w_key, b_key, w_value, b_value, w_out, norm_two, w_gate, w_up, w_down)
    floats = tuple((item.astype(jnp.float32) for item in floats))
    output, pullback = jax.vjp(partial(forward, cosine, sine, position, segment), *floats)
    grads = pullback(cotangent.astype(jnp.float32))
    return (output.astype(jnp.bfloat16), grads[0].astype(jnp.bfloat16), grads[1], grads[2], grads[3], grads[4], grads[5], grads[6], grads[7], grads[8], grads[9], grads[10], grads[11], grads[12])
```

```python
import jax
import jax.numpy as jnp
from jax import lax
from jax.sharding import PartitionSpec as P

EPSILON = 1e-06
ROPE_BASE = 1000000.0
MASKED = -1e30
LANES = 128
BOTH = ("fsdp", "context")
BF = jnp.bfloat16
F32 = jnp.float32


def tables(positions, head_width):
    ladder = jnp.arange(head_width // 2, dtype=F32)
    inverse = jnp.exp(-jnp.log(ROPE_BASE) * 2.0 * ladder / head_width)
    angles = positions.astype(F32)[:, None] * inverse[None, :]
    return (jnp.cos(angles), jnp.sin(angles))


def rotate(field, cosine, sine):
    middle = field.shape[-1] // 2
    first_half = field[..., :middle]
    second_half = field[..., middle:]
    cos_rows = cosine[:, None, :]
    sin_rows = sine[:, None, :]
    return jnp.concatenate(
        [
            first_half * cos_rows - second_half * sin_rows,
            second_half * cos_rows + first_half * sin_rows,
        ],
        axis=-1,
    )


def unrotate(gradient, cosine, sine):
    return rotate(gradient, cosine, -sine)


def locate(blocks, prompt_slots, block_rows):
    segment = jnp.where(blocks < prompt_slots, 0, blocks - prompt_slots + 1)
    anchor = jnp.where(blocks < prompt_slots, blocks * block_rows, prompt_slots * block_rows)
    return (segment, anchor)


def dot_nn(left, right):
    return lax.dot_general(left, right, (((1,), (0,)), ((), ())), preferred_element_type=F32)


def dot_tn(left, right):
    return lax.dot_general(left, right, (((0,), (0,)), ((), ())), preferred_element_type=F32)


def dot_nt(left, right):
    return lax.dot_general(left, right, (((1,), (1,)), ((), ())), preferred_element_type=F32)


def norm_back(grad_normed, rows_normed, inv_rms, gain):
    grad_rows = grad_normed * gain.astype(F32)
    return inv_rms * (
        grad_rows - rows_normed * jnp.mean(grad_rows * rows_normed, axis=-1, keepdims=True)
    )


class Grid:
    def __init__(self):
        self.nf = lax.axis_size("fsdp")
        self.nc = lax.axis_size("context")
        self.n = self.nf * self.nc
        self.cbits = self.nc.bit_length() - 1
        self.fbits = self.nf.bit_length() - 1
        self.me = lax.axis_index("fsdp") * self.nc + lax.axis_index("context")
        self.my_slot = lax.axis_index("context")
        self.core = lax.axis_index("tensor")

    def bit(self, b):
        return (self.me >> b) & 1

    def xor(self, x, mask):
        return lax.ppermute(x, BOTH, [(i, i ^ mask) for i in range(self.n)])

    def swap(self, x):
        return lax.ppermute(x, "tensor", [(0, 1), (1, 0)])

    def pair(self, b, mine, theirs, axis):
        low = self.bit(b) == 0
        return jnp.stack([jnp.where(low, mine, theirs), jnp.where(low, theirs, mine)], axis)

    def ordered(self, pieces, bits):
        if len(bits) == 0:
            return pieces[0]
        half = len(pieces) // 2
        low = self.ordered(pieces[:half], bits[:-1])
        high = self.ordered(pieces[half:], bits[:-1])
        return self.pair(bits[-1], low, high, 0)

    def gather_all(self, x):
        rows, columns = x.shape
        pieces = [x] + [self.xor(x, r) for r in range(1, self.nc)]
        x = self.ordered(pieces, list(range(self.cbits))).reshape(self.nc * rows, columns)
        rows = self.nc * rows
        if self.fbits == 2:
            xm, ym = self.nc, 2 * self.nc
            gx, gy = self.xor(x, xm), self.xor(x, ym)
            cut = rows // 2
            diagonal = jnp.concatenate([self.xor(gx[:cut], ym), self.xor(gy[cut:], xm)], 0)
            pieces = [x, gx, gy, diagonal]
            x = self.ordered(pieces, [self.cbits, self.cbits + 1])
        else:
            pieces = [x] + [self.xor(x, r * self.nc) for r in range(1, self.nf)]
            x = self.ordered(pieces, [self.cbits + k for k in range(self.fbits)])
        return x.reshape(self.nf * rows, columns)

    def scatter_all(self, x):
        columns = x.shape[1]
        x = x.reshape(self.nf, -1, columns)
        rows = x.shape[1]
        mine = lax.axis_index("fsdp")
        take = lambda r: lax.dynamic_index_in_dim(x, mine ^ r, 0, keepdims=False)
        if self.fbits == 2:
            xm, ym = self.nc, 2 * self.nc
            cut = rows // 2
            far = take(3)
            by_y = self.xor(far[:cut].astype(BF), ym)
            by_x = self.xor(far[cut:].astype(BF), xm)
            px, py = take(1), take(2)
            px = jnp.concatenate([px[:cut].astype(F32) + by_y.astype(F32), px[cut:].astype(F32)], 0)
            py = jnp.concatenate([py[:cut].astype(F32), py[cut:].astype(F32) + by_x.astype(F32)], 0)
            rx = self.xor(px.astype(BF), xm)
            ry = self.xor(py.astype(BF), ym)
            x = take(0).astype(F32) + rx.astype(F32) + ry.astype(F32)
        else:
            parts = [self.xor(take(r).astype(BF), r * self.nc) for r in range(1, self.nf)]
            x = take(0).astype(F32)
            for part in parts:
                x = x + part.astype(F32)
        x = x.astype(BF).reshape(self.nc, -1, columns)
        pick = lambda r: lax.dynamic_index_in_dim(x, self.my_slot ^ r, 0, keepdims=False)
        parts = [self.xor(pick(r), r) for r in range(1, self.nc)]
        total = pick(0).astype(F32)
        for part in parts:
            total = total + part.astype(F32)
        return total

    def scatter_small(self, x):
        columns = x.shape[1]
        x = x.reshape(self.nf, self.nc, columns)
        mine = lax.axis_index("fsdp")
        take = lambda r: lax.dynamic_index_in_dim(x, mine ^ r, 0, keepdims=False)
        total = take(0)
        for part in [self.xor(take(r), r * self.nc) for r in range(1, self.nf)]:
            total = total + part
        pick = lambda r: lax.dynamic_index_in_dim(total, self.my_slot ^ r, 0, keepdims=True)
        final = pick(0)
        for part in [self.xor(pick(r), r) for r in range(1, self.nc)]:
            final = final + part
        return final

    def tokens_in(self, x):
        zm, xm = 1, self.nc
        cut = x.shape[0] // 2
        px, pz = self.xor(x, xm), self.xor(x, zm)
        far = jnp.concatenate([self.xor(px[:cut], zm), self.xor(pz[cut:], xm)], 0)
        pieces = []
        for piece in (x, px, pz, far):
            pieces += [piece, self.swap(piece)]
        return jnp.concatenate(pieces, 0)

    def tokens_out(self, part):
        zm, xm = 1, self.nc
        part = part.reshape(4, 2, part.shape[0] // 8, part.shape[1])
        cut = part.shape[2] // 2

        def joined(k):
            return part[k, 0].astype(F32) + self.swap(part[k, 1]).astype(F32)

        far, px, pz, own = joined(3), joined(1), joined(2), joined(0)
        by_z = self.xor(far[:cut].astype(BF), zm).astype(F32)
        by_x = self.xor(far[cut:].astype(BF), xm).astype(F32)
        px = jnp.concatenate([px[:cut] + by_z, px[cut:]], 0).astype(BF)
        pz = jnp.concatenate([pz[:cut], pz[cut:] + by_x], 0).astype(BF)
        return own + self.xor(px, xm).astype(F32) + self.xor(pz, zm).astype(F32)

    def quarter_masks(self):
        return (0, 1, self.nc, self.nc + 1)

    def my_quarter(self):
        return 2 * self.bit(self.cbits) + self.bit(0)

    def weights_in(self, stack):
        count, rows, width = stack.shape
        width = width // 4
        q = self.my_quarter()
        pieces = []
        for r, mask in enumerate(self.quarter_masks()):
            block = lax.dynamic_slice(stack, (0, 0, (q ^ r) * width), (count, rows, width))
            pieces.append(block if r == 0 else self.xor(block, mask))
        near = self.ordered(pieces, [0, self.cbits])
        near = near.reshape((2, 2) + near.shape[1:]) if near.ndim == 4 else near
        outs = []
        for k in range(count):
            w = near[:, :, k]
            held = [0, self.cbits]
            for b in list(range(1, self.cbits)) + list(range(self.cbits + 1, self.cbits + self.fbits)):
                axis = sum(1 for h in held if h > b)
                w = self.pair(b, w, self.xor(w, 1 << b), axis)
                held.append(b)
            outs.append(w.reshape(self.n * rows, width))
        return outs

    def weights_out(self, grad):
        width = grad.shape[1]
        held = sorted(range(self.cbits + self.fbits), reverse=True)
        g = grad.reshape((2,) * len(held) + (-1, width))
        for b in list(range(self.cbits + self.fbits - 1, self.cbits, -1)) + list(range(self.cbits - 1, 0, -1)):
            axis = held.index(b)
            give = lax.dynamic_index_in_dim(g, 1 - self.bit(b), axis, keepdims=False)
            keep = lax.dynamic_index_in_dim(g, self.bit(b), axis, keepdims=False)
            g = (keep.astype(F32) + self.xor(give, 1 << b).astype(F32)).astype(BF)
            held.remove(b)
        q = self.my_quarter()
        g = g.reshape(4, -1, width)
        pieces = []
        for r, mask in enumerate(self.quarter_masks()):
            block = lax.dynamic_index_in_dim(g, q ^ r, 0, keepdims=False)
            pieces.append(block if r == 0 else self.xor(block, mask))
        full = self.ordered(pieces, [0, self.cbits]).reshape(4, -1, width)
        return full.transpose(1, 0, 2).reshape(-1, 4 * width).astype(F32)


def on_device(
    tokens,
    block_order,
    norm_one,
    w_query,
    b_query,
    w_key,
    b_key,
    w_value,
    b_value,
    w_out,
    norm_two,
    w_gate,
    w_up,
    w_down,
    cotangent,
):
    grid = Grid()
    block_rows, width = tokens.shape
    shard = norm_one.shape[0]
    slot_count = grid.nc
    prompt_slots = slot_count // 2
    head_width = w_key.shape[1]
    query_width = w_query.shape[1]
    head_group = query_width // head_width
    score_scale = head_width ** (-0.5)
    cores = lax.axis_size("tensor")
    own_rows = block_rows // cores
    owners = block_order[0]
    my_block = lax.dynamic_index_in_dim(owners, grid.my_slot, 0, keepdims=False)
    query_anchor = locate(my_block, prompt_slots, block_rows)[1]
    query_pos = query_anchor + jnp.arange(block_rows)

    def own(x):
        return lax.dynamic_slice(x, (grid.core * own_rows, 0), (own_rows, x.shape[1]))

    def both(x):
        other = grid.swap(x)
        first = grid.core == 0
        return jnp.concatenate([jnp.where(first, x, other), jnp.where(first, other, x)], 0)

    def summed(part):
        give = lax.dynamic_slice(part, ((1 - grid.core) * own_rows, 0), (own_rows, width))
        return own(part) + grid.swap(give.astype(BF)).astype(F32)

    bias_shard = b_query.shape[1]
    small_bias = b_key.shape[1]
    vector = jnp.concatenate(
        [norm_one[None], norm_two[None], b_query, b_key, b_value], axis=1
    )
    vectors = grid.gather_all(vector) if False else gather_small(grid, vector)
    gain_one = vectors[:, :shard].reshape(-1)
    gain_two = vectors[:, shard : 2 * shard].reshape(-1)
    start = 2 * shard
    bias = jnp.concatenate(
        [
            vectors[:, start : start + bias_shard].reshape(-1),
            vectors[:, start + bias_shard : start + bias_shard + small_bias].reshape(-1),
            vectors[:, start + bias_shard + small_bias :].reshape(-1),
        ]
    ).astype(F32)

    w_qkv = grid.gather_all(jnp.concatenate([w_query, w_key, w_value], axis=1))
    w_out_t = grid.gather_all(w_out.T)
    hidden = w_gate.shape[1]
    quarter = -(-hidden // (4 * LANES)) * LANES
    pad = ((0, 0), (0, 4 * quarter - hidden))
    stack = jnp.stack([jnp.pad(w_gate, pad), jnp.pad(w_up, pad), jnp.pad(w_down.T, pad)])
    gate_full, up_full, down_full = grid.weights_in(stack)
    grads_in = grid.tokens_in(own(cotangent))

    inputs = tokens.astype(F32)
    inv_one = lax.rsqrt(jnp.mean(inputs * inputs, axis=-1, keepdims=True) + EPSILON)
    rows_one = inputs * inv_one
    normed_one = (rows_one * gain_one.astype(F32)).astype(BF)
    cosine, sine = tables(query_pos, head_width)
    qkv = dot_nn(normed_one, w_qkv) + bias
    queries = rotate(
        qkv[:, :query_width].reshape(block_rows, head_group, head_width), cosine, sine
    ).astype(BF)
    keys = (
        rotate(
            qkv[:, query_width : query_width + head_width].reshape(block_rows, 1, head_width),
            cosine,
            sine,
        )
        .reshape(block_rows, head_width)
        .astype(BF)
    )
    values = qkv[:, query_width + head_width :].astype(BF)
    pair = jnp.concatenate([keys, values], axis=1)
    pairs = [pair] + [grid.xor(pair, r) for r in range(1, slot_count)]
    stacked = jnp.stack(pairs)
    piece_block = owners[grid.my_slot ^ jnp.arange(slot_count)]
    seen = (piece_block < prompt_slots) & (piece_block < my_block)
    causal = jnp.arange(block_rows)[None, :] <= jnp.arange(block_rows)[:, None]

    def keep_state(running):
        return running

    def attend(state, current):
        piece, first, visible = current
        key_blk, value_blk = piece[:, :head_width], piece[:, head_width:]
        allowed = causal | jnp.logical_not(first)

        def update_block(inner):
            run_peak, run_total, run_sum = inner
            scores = (
                jnp.einsum("qhd,kd->hqk", queries, key_blk, preferred_element_type=F32)
                * score_scale
            )
            scores = jnp.where(allowed[None], scores, MASKED)
            new_peak = jnp.maximum(run_peak, jnp.max(scores, axis=-1))
            shrink = jnp.exp(run_peak - new_peak)
            attn_probs = jnp.exp(scores - new_peak[..., None])
            new_total = run_total * shrink + jnp.sum(attn_probs, axis=-1)
            new_sum = run_sum * shrink[..., None] + jnp.einsum(
                "hqk,kd->hqd", attn_probs.astype(BF), value_blk, preferred_element_type=F32
            )
            return (new_peak, new_total, new_sum)

        return (lax.cond(visible, update_block, keep_state, state), None)

    start_state = (
        jnp.full((head_group, block_rows), MASKED, F32),
        jnp.zeros((head_group, block_rows), F32),
        jnp.zeros((head_group, block_rows, head_width), F32),
    )
    is_first = jnp.arange(slot_count) == 0
    meta = (is_first, is_first | seen)
    running, unused = lax.scan(attend, start_state, (stacked,) + meta)
    run_peak, run_total, run_sum = running
    log_total = run_peak + jnp.log(run_total)
    attn_heads = run_sum / run_total[..., None]
    out_low = attn_heads.transpose(1, 0, 2).reshape(block_rows, query_width).astype(BF)
    hidden_one = own(tokens).astype(F32) + summed(dot_nt(out_low, w_out_t))

    inv_two = lax.rsqrt(jnp.mean(hidden_one * hidden_one, axis=-1, keepdims=True) + EPSILON)
    rows_two = hidden_one * inv_two
    normed_two = (rows_two * gain_two.astype(F32)).astype(BF)
    normed_in = grid.tokens_in(normed_two)
    gate_lin = dot_nn(normed_in, gate_full)
    up_lin = dot_nn(normed_in, up_full)
    sigmoid_gate = jax.nn.sigmoid(gate_lin)
    silu_gate = gate_lin * sigmoid_gate
    act = (silu_gate * up_lin).astype(BF)
    grad_act = dot_nn(grads_in, down_full)
    grad_gate = (
        grad_act * up_lin * sigmoid_gate * (1.0 + gate_lin * (1.0 - sigmoid_gate))
    ).astype(BF)
    grad_up = (grad_act * silu_gate).astype(BF)
    grad_normed_two = grid.tokens_out(
        (dot_nt(grad_gate, gate_full) + dot_nt(grad_up, up_full)).astype(BF)
    )
    grad_wdown = grid.weights_out(dot_tn(grads_in, act).astype(BF))
    grad_wgate = grid.weights_out(dot_tn(normed_in, grad_gate).astype(BF))
    grad_wup = grid.weights_out(dot_tn(normed_in, grad_up).astype(BF))
    mlp_total = grid.tokens_out(dot_nt(act, down_full).astype(BF))
    result = both((hidden_one + mlp_total).astype(BF))

    grad_gain_two = jnp.sum(grad_normed_two * rows_two, axis=0)
    grad_hidden_one = own(cotangent).astype(F32) + norm_back(
        grad_normed_two, rows_two, inv_two, gain_two
    )

    grad_low = both(grad_hidden_one.astype(BF))
    grad_wout = grid.scatter_all(dot_tn(grad_low, out_low).astype(BF))
    grad_heads = (
        dot_nn(grad_low, w_out_t).astype(BF).reshape(block_rows, head_group, head_width)
    )
    delta_rows = jnp.einsum("qhd,hqd->hq", grad_heads.astype(F32), attn_heads)

    def attend_back(grad_in, current):
        piece, first, visible = current
        key_blk, value_blk = piece[:, :head_width], piece[:, head_width:]
        allowed = causal | jnp.logical_not(first)

        def update_block(grad_now):
            scores = (
                jnp.einsum("qhd,kd->hqk", queries, key_blk, preferred_element_type=F32)
                * score_scale
            )
            attn_probs = jnp.where(allowed[None], jnp.exp(scores - log_total[..., None]), 0.0)
            grad_value_blk = jnp.einsum(
                "hqk,qhd->kd", attn_probs.astype(BF), grad_heads, preferred_element_type=F32
            )
            grad_probs = jnp.einsum(
                "qhd,kd->hqk", grad_heads, value_blk, preferred_element_type=F32
            )
            grad_scores = (attn_probs * (grad_probs - delta_rows[..., None])).astype(BF)
            grad_next = grad_now + score_scale * jnp.einsum(
                "hqk,kd->qhd", grad_scores, key_blk, preferred_element_type=F32
            )
            grad_key_blk = score_scale * jnp.einsum(
                "hqk,qhd->kd", grad_scores, queries, preferred_element_type=F32
            )
            return (grad_next, jnp.concatenate([grad_key_blk, grad_value_blk], axis=1).astype(BF))

        def skip_block(grad_now):
            return (grad_now, jnp.zeros((block_rows, 2 * head_width), BF))

        return lax.cond(visible, update_block, skip_block, grad_in)

    grad_query = jnp.zeros((block_rows, head_group, head_width), F32)
    grad_query, grad_pairs = lax.scan(attend_back, grad_query, (stacked,) + meta)
    grad_pair = grad_pairs[0].astype(F32)
    for r in range(1, slot_count):
        grad_pair = grad_pair + grid.xor(grad_pairs[r], r).astype(F32)
    grad_query_lin = unrotate(grad_query, cosine, sine).reshape(block_rows, query_width)
    grad_key_lin = unrotate(
        grad_pair[:, :head_width].reshape(block_rows, 1, head_width), cosine, sine
    ).reshape(block_rows, head_width)
    grad_qkv = jnp.concatenate(
        [grad_query_lin, grad_key_lin, grad_pair[:, head_width:]], axis=1
    ).astype(BF)
    grad_wqkv = grid.scatter_all(dot_tn(normed_one, grad_qkv).astype(BF))
    grad_bias = jnp.sum(grad_qkv.astype(F32), axis=0)
    grad_normed_one = summed(dot_nt(grad_qkv, w_qkv))
    rows_own = own(rows_one)
    inv_own = own(inv_one)
    grad_gain_one = jnp.sum(grad_normed_one * rows_own, axis=0)
    grad_inputs = grad_hidden_one + norm_back(grad_normed_one, rows_own, inv_own, gain_one)
    grad_tokens = both(grad_inputs.astype(BF))

    gains = jnp.concatenate(
        [grad_gain_one.reshape(-1, shard), grad_gain_two.reshape(-1, shard)], axis=1
    )
    gains = gains + grid.swap(gains)
    small = jnp.concatenate(
        [
            gains,
            grad_bias[:query_width].reshape(-1, bias_shard),
            grad_bias[query_width : query_width + head_width].reshape(-1, small_bias),
            grad_bias[query_width + head_width :].reshape(-1, small_bias),
        ],
        axis=1,
    )
    small = grid.scatter_small(small)
    return (
        result,
        grad_tokens,
        small[0, :shard],
        grad_wqkv[:, :query_width],
        small[:, start : start + bias_shard],
        grad_wqkv[:, query_width : query_width + head_width],
        small[:, start + bias_shard : start + bias_shard + small_bias],
        grad_wqkv[:, query_width + head_width :],
        small[:, start + bias_shard + small_bias :],
        grad_wout.T,
        small[0, shard : 2 * shard],
        grad_wgate[:, :hidden],
        grad_wup[:, :hidden],
        grad_wdown[:, :hidden].T,
    )


def gather_small(grid, x):
    pieces = [x] + [grid.xor(x, r) for r in range(1, grid.nc)]
    x = grid.ordered(pieces, list(range(grid.cbits))).reshape(grid.nc, -1)
    pieces = [x] + [grid.xor(x, r * grid.nc) for r in range(1, grid.nf)]
    x = grid.ordered(pieces, [grid.cbits + k for k in range(grid.fbits)])
    return x.reshape(grid.n, -1)


def solution(mesh):
    rows = P(("fsdp", "context"), None)
    split = P(("fsdp", "context"))
    into = P(("fsdp", "context"), "tensor")
    back = P("tensor", ("fsdp", "context"))
    return jax.shard_map(
        on_device,
        mesh=mesh,
        in_specs=(
            rows,
            P("fsdp", None),
            split,
            into,
            back,
            into,
            back,
            into,
            back,
            back,
            split,
            into,
            into,
            back,
            rows,
        ),
        out_specs=(
            rows,
            rows,
            split,
            into,
            back,
            into,
            back,
            into,
            back,
            back,
            split,
            into,
            into,
            back,
        ),
        check_vma=False,
    )
```

```python
import functools

import jax
import jax.numpy as jnp
from jax import lax
from jax.experimental import pallas as pl
from jax.experimental.pallas import tpu as pltpu
from jax.sharding import PartitionSpec as P

EPSILON = 1e-06
ROPE_BASE = 1000000.0
MASKED = -1e30
LANES = 128
BOTH = ("fsdp", "context")
KERNEL_BYTES = 56 << 20
BF = jnp.bfloat16
F32 = jnp.float32


def tables(positions, head_width):
    ladder = jnp.arange(head_width // 2, dtype=F32)
    inverse = jnp.exp(-jnp.log(ROPE_BASE) * 2.0 * ladder / head_width)
    angles = positions.astype(F32)[:, None] * inverse[None, :]
    return (jnp.cos(angles), jnp.sin(angles))


def rotate(field, cosine, sine):
    middle = field.shape[-1] // 2
    first_half = field[..., :middle]
    second_half = field[..., middle:]
    cos_rows = cosine[:, None, :]
    sin_rows = sine[:, None, :]
    return jnp.concatenate(
        [
            first_half * cos_rows - second_half * sin_rows,
            second_half * cos_rows + first_half * sin_rows,
        ],
        axis=-1,
    )


def unrotate(gradient, cosine, sine):
    return rotate(gradient, cosine, -sine)


def locate(blocks, prompt_slots, block_rows):
    segment = jnp.where(blocks < prompt_slots, 0, blocks - prompt_slots + 1)
    anchor = jnp.where(blocks < prompt_slots, blocks * block_rows, prompt_slots * block_rows)
    return (segment, anchor)


def dot_nn(left, right):
    return lax.dot_general(left, right, (((1,), (0,)), ((), ())), preferred_element_type=F32)


def dot_tn(left, right):
    return lax.dot_general(left, right, (((0,), (0,)), ((), ())), preferred_element_type=F32)


def dot_nt(left, right):
    return lax.dot_general(left, right, (((1,), (1,)), ((), ())), preferred_element_type=F32)


def norm_back(grad_normed, rows_normed, inv_rms, gain):
    grad_rows = grad_normed * gain.astype(F32)
    return inv_rms * (
        grad_rows - rows_normed * jnp.mean(grad_rows * rows_normed, axis=-1, keepdims=True)
    )


def attend_kernel(count, scale, seen, q_ref, *refs):
    pairs = refs[:count]
    out_ref, low_ref, lse_ref, peak_ref, total_ref, sum_ref = refs[count:]
    wide = q_ref.shape[1]
    query = q_ref[...]

    def piece(r):
        scores = dot_nt(pairs[r][:, :wide], query) * scale
        if r == 0:
            rows = lax.broadcasted_iota(jnp.int32, scores.shape, 0)
            columns = lax.broadcasted_iota(jnp.int32, scores.shape, 1)
            scores = jnp.where(rows <= columns, scores, MASKED)
            peak = jnp.max(scores, axis=0, keepdims=True)
        else:
            old = peak_ref[...]
            peak = jnp.maximum(old, jnp.max(scores, axis=0, keepdims=True))
        probs = jnp.exp(scores - peak)
        total = jnp.sum(probs, axis=0, keepdims=True)
        mixed = dot_tn(pairs[r][:, wide:], probs.astype(BF))
        if r:
            shrink = jnp.exp(old - peak)
            total = total + total_ref[...] * shrink
            mixed = mixed + sum_ref[...] * shrink
        peak_ref[...] = peak
        total_ref[...] = total
        sum_ref[...] = mixed

    piece(0)
    for r in range(1, count):
        pl.when(seen[r] != 0)(functools.partial(piece, r))
    total = total_ref[...]
    out = jnp.transpose(sum_ref[...] / total)
    out_ref[...] = out
    low_ref[...] = out.astype(BF)
    lse_ref[...] = (peak_ref[...] + jnp.log(total))[None]


def attend(seen, queries, pairs, heads, scale):
    rows = queries.shape[0]
    wide = queries.shape[1] // heads
    count = len(pairs)
    head = pl.BlockSpec((rows, wide), lambda h, seen: (0, h))
    whole = pl.BlockSpec(pairs[0].shape, lambda h, seen: (0, 0))
    return pl.pallas_call(
        functools.partial(attend_kernel, count, scale),
        grid_spec=pltpu.PrefetchScalarGridSpec(
            num_scalar_prefetch=1,
            grid=(heads,),
            in_specs=[head] + [whole] * count,
            out_specs=[head, head, pl.BlockSpec((1, 1, rows), lambda h, seen: (h, 0, 0))],
            scratch_shapes=[
                pltpu.VMEM((1, rows), F32),
                pltpu.VMEM((1, rows), F32),
                pltpu.VMEM((wide, rows), F32),
            ],
        ),
        out_shape=[
            jax.ShapeDtypeStruct(queries.shape, F32),
            jax.ShapeDtypeStruct(queries.shape, BF),
            jax.ShapeDtypeStruct((heads, 1, rows), F32),
        ],
        compiler_params=pltpu.CompilerParams(vmem_limit_bytes=KERNEL_BYTES),
        cost_estimate=pl.CostEstimate(
            flops=100 * rows * queries.size, bytes_accessed=8 * queries.size, transcendentals=0
        ),
    )(seen, queries, *pairs)


def attend_back_kernel(count, scale, seen, q_ref, g_ref, out_ref, lse_ref, *refs):
    pairs = refs[:count]
    dq_ref = refs[count]
    grads = refs[count + 1 : 2 * count + 1]
    held, sum_ref = refs[2 * count + 1 :]
    wide = q_ref.shape[1]
    step = pl.program_id(0)
    query = q_ref[...]
    grad = g_ref[...]
    delta = jnp.sum(grad.astype(F32) * out_ref[...], axis=1, keepdims=True)
    delta = jnp.transpose(jnp.broadcast_to(delta, q_ref.shape))[:1]
    lse = lse_ref[0]

    @pl.when(step == 0)
    def _():
        held[...] = jnp.zeros_like(held)

    def piece(r):
        key = pairs[r][:, :wide]
        probs = jnp.exp(dot_nt(key, query) * scale - lse)
        if r == 0:
            rows = lax.broadcasted_iota(jnp.int32, probs.shape, 0)
            columns = lax.broadcasted_iota(jnp.int32, probs.shape, 1)
            probs = jnp.where(rows <= columns, probs, 0.0)
        grad_scores = (probs * (dot_nt(pairs[r][:, wide:], grad) - delta)).astype(BF)
        held[r, :, wide:] += dot_nn(probs.astype(BF), grad)
        held[r, :, :wide] += dot_nn(grad_scores, query) * scale
        term = dot_tn(key, grad_scores)
        sum_ref[...] = term if r == 0 else sum_ref[...] + term

    piece(0)
    for r in range(1, count):
        pl.when(seen[r] != 0)(functools.partial(piece, r))
    dq_ref[...] = jnp.transpose(sum_ref[...]) * scale

    @pl.when(step == pl.num_programs(0) - 1)
    def _():
        for r in range(count):
            grads[r][...] = held[r].astype(grads[r].dtype)


def attend_back(seen, queries, grads, outs, lse, pairs, heads, scale):
    rows = queries.shape[0]
    wide = queries.shape[1] // heads
    count = len(pairs)
    head = pl.BlockSpec((rows, wide), lambda h, seen: (0, h))
    whole = pl.BlockSpec(pairs[0].shape, lambda h, seen: (0, 0))
    results = pl.pallas_call(
        functools.partial(attend_back_kernel, count, scale),
        grid_spec=pltpu.PrefetchScalarGridSpec(
            num_scalar_prefetch=1,
            grid=(heads,),
            in_specs=[head] * 3
            + [pl.BlockSpec((1, 1, rows), lambda h, seen: (h, 0, 0))]
            + [whole] * count,
            out_specs=[head] + [whole] * count,
            scratch_shapes=[
                pltpu.VMEM((count,) + pairs[0].shape, F32),
                pltpu.VMEM((wide, rows), F32),
            ],
        ),
        out_shape=[jax.ShapeDtypeStruct(queries.shape, F32)]
        + [jax.ShapeDtypeStruct(pairs[0].shape, F32 if r == 0 else BF) for r in range(count)],
        compiler_params=pltpu.CompilerParams(vmem_limit_bytes=KERNEL_BYTES),
        cost_estimate=pl.CostEstimate(
            flops=150 * rows * queries.size, bytes_accessed=16 * queries.size, transcendentals=0
        ),
    )(seen, queries, grads, outs, lse, *pairs)
    return results[0], results[1:]


def hidden_kernel(n_ref, d_ref, wg_ref, wu_ref, wd_ref, act_ref, dg_ref, du_ref):
    gate = dot_nn(n_ref[...], wg_ref[...])
    up = dot_nn(n_ref[...], wu_ref[...])
    sigmoid = jax.nn.sigmoid(gate)
    silu = gate * sigmoid
    act_ref[...] = (silu * up).astype(BF)
    grad = dot_nn(d_ref[...], wd_ref[...])
    du_ref[...] = (grad * silu).astype(BF)
    dg_ref[...] = (grad * up * (sigmoid + silu * (1.0 - sigmoid))).astype(BF)


def hidden_units(normed, grads, gate_w, up_w, down_w):
    tokens, depth = normed.shape
    units = gate_w.shape[1]
    tm = min(tokens, 256)
    rows = pl.BlockSpec((tm, depth), lambda m: (m, 0))
    weight = pl.BlockSpec((depth, units), lambda m: (0, 0))
    out = pl.BlockSpec((tm, units), lambda m: (m, 0))
    flops = 6 * tokens * depth * units
    return pl.pallas_call(
        hidden_kernel,
        grid=(tokens // tm,),
        in_specs=[rows, rows, weight, weight, weight],
        out_specs=[out] * 3,
        out_shape=[jax.ShapeDtypeStruct((tokens, units), BF)] * 3,
        compiler_params=pltpu.CompilerParams(vmem_limit_bytes=KERNEL_BYTES),
        cost_estimate=pl.CostEstimate(
            flops=flops, bytes_accessed=2 * units * (depth + tokens) * 3, transcendentals=0
        ),
    )(normed, grads, gate_w, up_w, down_w)


def back_kernel(dg_ref, du_ref, wg_ref, wu_ref, out_ref):
    out_ref[...] = (
        dot_nt(dg_ref[...], wg_ref[...]) + dot_nt(du_ref[...], wu_ref[...])
    ).astype(BF)


def hidden_back(grad_gate, grad_up, gate_w, up_w):
    tokens, units = grad_gate.shape
    depth = gate_w.shape[0]
    tm = min(tokens, 512)
    rows = pl.BlockSpec((tm, units), lambda m: (m, 0))
    weight = pl.BlockSpec((depth, units), lambda m: (0, 0))
    return pl.pallas_call(
        back_kernel,
        grid=(tokens // tm,),
        in_specs=[rows, rows, weight, weight],
        out_specs=pl.BlockSpec((tm, depth), lambda m: (m, 0)),
        out_shape=jax.ShapeDtypeStruct((tokens, depth), BF),
        compiler_params=pltpu.CompilerParams(vmem_limit_bytes=KERNEL_BYTES),
        cost_estimate=pl.CostEstimate(
            flops=4 * tokens * depth * units,
            bytes_accessed=4 * units * (depth + tokens),
            transcendentals=0,
        ),
    )(grad_gate, grad_up, gate_w, up_w)


def after(x, *earlier):
    return lax.optimization_barrier((x,) + earlier)[0]


class Grid:
    def __init__(self):
        self.nf = lax.axis_size("fsdp")
        self.nc = lax.axis_size("context")
        self.n = self.nf * self.nc
        self.cbits = self.nc.bit_length() - 1
        self.fbits = self.nf.bit_length() - 1
        self.me = lax.axis_index("fsdp") * self.nc + lax.axis_index("context")
        self.my_slot = lax.axis_index("context")
        self.core = lax.axis_index("tensor")
        self.last = {}
        self.zm = 1
        self.xm = self.nc
        self.deep = list(range(1, self.cbits)) + list(range(self.cbits + 1, self.cbits + self.fbits))

    def bit(self, b):
        return (self.me >> b) & 1

    def lanes(self, mask):
        found = set()
        for b in range(self.cbits + self.fbits):
            if mask >> b & 1:
                if b == 0:
                    found.add("near")
                elif b < self.cbits:
                    found.add("far")
                elif b == self.cbits:
                    found.add("x")
                else:
                    found.add("y")
        return found

    def xor(self, x, mask):
        return lax.ppermute(x, BOTH, [(i, i ^ mask) for i in range(self.n)])

    def send(self, pairs, free=False, wait=None):
        lanes = set().union(*[self.lanes(mask) for _, mask in pairs])
        earlier = []
        if wait is not None:
            earlier = list(wait)
        elif not free:
            for lane in sorted(lanes):
                earlier += self.last.get(lane, [])
        outs = []
        for x, mask in pairs:
            outs.append(self.xor(after(x, *earlier) if earlier else x, mask))
        for lane in lanes:
            self.last[lane] = list(outs)
        return outs

    def one(self, x, mask, free=False):
        return self.send([(x, mask)], free)[0]

    def swap(self, x):
        return lax.ppermute(x, "tensor", [(0, 1), (1, 0)])

    def pair(self, b, mine, theirs, axis):
        low = self.bit(b) == 0
        return jnp.stack([jnp.where(low, mine, theirs), jnp.where(low, theirs, mine)], axis)

    def ordered(self, pieces, bits):
        if len(bits) == 0:
            return pieces[0]
        half = len(pieces) // 2
        low = self.ordered(pieces[:half], bits[:-1])
        high = self.ordered(pieces[half:], bits[:-1])
        return self.pair(bits[-1], low, high, 0)

    def gather_context(self, x, bits):
        rows, columns = x.shape
        w, held = x[None], []
        w = x
        for b in bits:
            w = self.pair(b, w, self.one(w, 1 << b), 0) if not held else self.deepen(w, held, b)
            if not held:
                held.append(b)
        return w, held

    def gather_fsdp(self, x):
        rows, columns = x.shape
        if self.fbits == 2:
            xm, ym = self.xm, 2 * self.xm
            gx, gy = self.one(x, xm), self.one(x, ym)
            cut = rows // 2
            by_y, by_x = self.one(gx[:cut], ym), self.one(gy[cut:], xm)
            pieces = [x, gx, gy, jnp.concatenate([by_y, by_x], 0)]
            x = self.ordered(pieces, [self.cbits, self.cbits + 1])
        else:
            pieces = [x] + self.send([(x, r * self.nc) for r in range(1, self.nf)])
            x = self.ordered(pieces, [self.cbits + k for k in range(self.fbits)])
        return x.reshape(self.nf * rows, columns)

    def scatter_fsdp(self, x):
        columns = x.shape[1]
        x = x.reshape(self.nf, -1, columns)
        rows = x.shape[1]
        mine = lax.axis_index("fsdp")
        take = lambda r: lax.dynamic_index_in_dim(x, mine ^ r, 0, keepdims=False)
        if self.fbits == 2:
            xm, ym = self.xm, 2 * self.xm
            cut = rows // 2
            far = take(3)
            by_y, by_x = self.one(far[:cut], ym), self.one(far[cut:], xm)
            px, py = take(1), take(2)
            px = jnp.concatenate([px[:cut].astype(F32) + by_y.astype(F32), px[cut:].astype(F32)], 0)
            py = jnp.concatenate([py[:cut].astype(F32), py[cut:].astype(F32) + by_x.astype(F32)], 0)
            rx = self.one(px.astype(BF), xm)
            ry = self.one(py.astype(BF), ym)
            x = take(0).astype(F32) + rx.astype(F32) + ry.astype(F32)
        else:
            parts = self.send([(take(r), r * self.nc) for r in range(1, self.nf)])
            x = take(0).astype(F32)
            for part in parts:
                x = x + part.astype(F32)
        return x.astype(BF)

    def scatter_context(self, x):
        columns = x.shape[1]
        x = x.reshape(self.nc, -1, columns)
        pick = lambda r: lax.dynamic_index_in_dim(x, self.my_slot ^ r, 0, keepdims=False)
        parts = self.send([(pick(r), r) for r in range(1, self.nc)])
        total = pick(0).astype(F32)
        for part in parts:
            total = total + part.astype(F32)
        return total

    def scatter_small(self, x):
        columns = x.shape[1]
        x = x.reshape(self.nf, self.nc, columns)
        mine = lax.axis_index("fsdp")
        take = lambda r: lax.dynamic_index_in_dim(x, mine ^ r, 0, keepdims=False)
        total = take(0)
        for part in [self.xor(take(r), r * self.nc) for r in range(1, self.nf)]:
            total = total + part
        pick = lambda r: lax.dynamic_index_in_dim(total, self.my_slot ^ r, 0, keepdims=True)
        final = pick(0)
        for part in [self.xor(pick(r), r) for r in range(1, self.nc)]:
            final = final + part
        return final

    def tokens_in(self, x, other=None):
        zm, xm = self.zm, self.xm
        cut = x.shape[0] // 2
        if other is None:
            other = self.swap(x)
        px, pz = self.one(x, xm), self.one(x, zm)
        by_z, by_x = self.one(px[:cut], zm), self.one(pz[cut:], xm)
        got = jnp.concatenate([px, pz, by_z, by_x], 0)
        return jnp.concatenate([x, got, other, self.swap(got)], 0)

    def tokens_out(self, part):
        zm, xm = self.zm, self.xm
        rows = part.shape[0] // 8
        cut = rows // 2
        part = part[: 4 * rows].astype(F32) + self.swap(part[4 * rows :]).astype(F32)
        own, px, pz, far = [part[k * rows : (k + 1) * rows] for k in range(4)]
        by_z = self.one(far[:cut].astype(BF), zm)
        by_x = self.one(far[cut:].astype(BF), xm)
        px = jnp.concatenate([px[:cut] + by_z.astype(F32), px[cut:]], 0).astype(BF)
        pz = jnp.concatenate([pz[:cut], pz[cut:] + by_x.astype(F32)], 0).astype(BF)
        total = own + self.one(px, xm).astype(F32) + self.one(pz, zm).astype(F32)
        return total, (by_z, by_x)

    def quarter_masks(self):
        return (0, self.zm, self.xm, self.xm + self.zm)

    def my_quarter(self):
        return 2 * self.bit(self.cbits) + self.bit(0)

    def quarters_in(self, w, wait):
        rows, width = w.shape[0], w.shape[1] // 4
        q = self.my_quarter()
        blocks = [lax.dynamic_slice(w, (0, (q ^ r) * width), (rows, width)) for r in range(4)]
        got = self.send(list(zip(blocks[1:], self.quarter_masks()[1:])), wait=wait)
        return self.ordered(blocks[:1] + got, [0, self.cbits])

    def quarter_x(self, w):
        half = w.shape[1] // 2
        take = lambda k: lax.dynamic_slice(w, (0, k * half), (w.shape[0], half))
        xb = self.bit(self.cbits)
        return self.pair(self.cbits, take(xb), self.one(take(1 - xb), self.xm), 0)

    def quarter_z(self, w):
        half = w.shape[2] // 2
        take = lambda k: lax.dynamic_slice(w, (0, 0, k * half), w.shape[:2] + (half,))
        zb = self.bit(0)
        return self.pair(0, take(zb), self.one(take(1 - zb), self.zm), 1)

    def quarters_out(self, g):
        rows, width = g.shape[2:]
        g = g.reshape(4, rows, width)
        q = self.my_quarter()
        blocks = [lax.dynamic_index_in_dim(g, q ^ r, 0, keepdims=False) for r in range(4)]
        got = self.send(list(zip(blocks[1:], self.quarter_masks()[1:])))
        full = self.ordered(blocks[:1] + got, [0, self.cbits]).reshape(4, rows, width)
        return full.transpose(1, 0, 2).reshape(rows, 4 * width).astype(F32)

    def deepen(self, w, held, b):
        axis = sum(1 for h in held if h > b)
        held.append(b)
        got = self.one(w, 1 << b)
        self.got = got
        return self.pair(b, w, got, axis)

    def fold(self, g, held, b):
        axis = held.index(b)
        held.remove(b)
        give = lax.dynamic_index_in_dim(g, 1 - self.bit(b), axis, keepdims=False)
        keep = lax.dynamic_index_in_dim(g, self.bit(b), axis, keepdims=False)
        return (keep.astype(F32) + self.one(give, 1 << b).astype(F32)).astype(BF)


def on_device(
    tokens,
    block_order,
    norm_one,
    w_query,
    b_query,
    w_key,
    b_key,
    w_value,
    b_value,
    w_out,
    norm_two,
    w_gate,
    w_up,
    w_down,
    cotangent,
):
    grid = Grid()
    block_rows, width = tokens.shape
    shard = norm_one.shape[0]
    slot_count = grid.nc
    prompt_slots = slot_count // 2
    head_width = w_key.shape[1]
    query_width = w_query.shape[1]
    head_group = query_width // head_width
    score_scale = head_width ** (-0.5)
    cores = lax.axis_size("tensor")
    own_rows = block_rows // cores
    owners = block_order[0]
    my_block = lax.dynamic_index_in_dim(owners, grid.my_slot, 0, keepdims=False)
    query_anchor = locate(my_block, prompt_slots, block_rows)[1]
    query_pos = query_anchor + jnp.arange(block_rows)

    def own(x):
        return lax.dynamic_slice(x, (grid.core * own_rows, 0), (own_rows, x.shape[1]))

    def others(x):
        return lax.dynamic_slice(x, ((1 - grid.core) * own_rows, 0), (own_rows, x.shape[1]))

    def both(x):
        other = grid.swap(x)
        first = grid.core == 0
        return jnp.concatenate([jnp.where(first, x, other), jnp.where(first, other, x)], 0)

    def summed(part):
        give = lax.dynamic_slice(part, ((1 - grid.core) * own_rows, 0), (own_rows, width))
        return own(part) + grid.swap(give.astype(BF)).astype(F32)

    bias_shard = b_query.shape[1]
    small_bias = b_key.shape[1]
    vector = jnp.concatenate([norm_one[None], norm_two[None], b_query, b_key, b_value], axis=1)
    columns = query_width + 2 * head_width
    vector = jnp.pad(vector, ((0, 7), (0, columns - vector.shape[1])))
    packed = jnp.concatenate(
        [jnp.concatenate([w_query, w_key, w_value], axis=1), vector], axis=0
    )
    hidden = w_gate.shape[1]
    quarter = -(-hidden // (4 * LANES)) * LANES
    pad = ((0, 0), (0, 4 * quarter - hidden))
    w_out_t = lax.all_gather(w_out.T, BOTH, axis=0, tiled=True)

    context_deep = [b for b in grid.deep if b < grid.cbits]
    fsdp_deep = [b for b in grid.deep if b > grid.cbits]
    deep_first = context_deep[::-1]
    packed, held = grid.gather_context(packed, deep_first)
    w_one = grid.quarters_in(jnp.pad(w_gate, pad), wait=[])
    grid.last["near"] = []
    packed = grid.deepen(packed, held, 0).reshape(grid.nc * (shard + 8), columns)
    w_two = grid.quarter_x(jnp.pad(w_up, pad))
    grid.last["x"] = []
    w_two = grid.quarter_z(w_two)
    packed = grid.gather_fsdp(packed).reshape(grid.n, shard + 8, columns)
    w_qkv = packed[:, :shard].reshape(grid.n * shard, columns)
    vectors = packed[:, shard]
    gain_one = vectors[:, :shard].reshape(-1)
    gain_two = vectors[:, shard : 2 * shard].reshape(-1)
    start = 2 * shard
    bias = jnp.concatenate(
        [
            vectors[:, start : start + bias_shard].reshape(-1),
            vectors[:, start + bias_shard : start + bias_shard + small_bias].reshape(-1),
            vectors[
                :, start + bias_shard + small_bias : start + bias_shard + 2 * small_bias
            ].reshape(-1),
        ]
    ).astype(F32)
    held_one, held_two, held_three = [[0, grid.cbits] for _ in range(3)]
    grid.last["far"] = []
    for b in context_deep:
        w_one = grid.deepen(w_one, held_one, b)
    for b in context_deep:
        w_two = grid.deepen(w_two, held_two, b)
    second_deep = grid.last["far"]
    for b in fsdp_deep:
        w_one = grid.deepen(w_one, held_one, b)

    inputs = tokens.astype(F32)
    inv_one = lax.rsqrt(jnp.mean(inputs * inputs, axis=-1, keepdims=True) + EPSILON)
    rows_one = inputs * inv_one
    normed_one = (rows_one * gain_one.astype(F32)).astype(BF)
    cosine, sine = tables(query_pos, head_width)
    qkv = dot_nn(normed_one, w_qkv) + bias
    queries = (
        rotate(qkv[:, :query_width].reshape(block_rows, head_group, head_width), cosine, sine)
        .reshape(block_rows, query_width)
        .astype(BF)
    )
    keys = (
        rotate(
            qkv[:, query_width : query_width + head_width].reshape(block_rows, 1, head_width),
            cosine,
            sine,
        )
        .reshape(block_rows, head_width)
        .astype(BF)
    )
    values = qkv[:, query_width + head_width :].astype(BF)
    pair = jnp.concatenate([keys, values], axis=1)
    pairs = [pair] + grid.send([(pair, r) for r in range(1, slot_count)], wait=[])
    grid.last["far"] = second_deep
    grid.last["near"] = pairs[1:]
    w_three = grid.quarter_z(grid.quarter_x(jnp.pad(after(w_down, w_qkv).T, pad)))
    grads_in = grid.tokens_in(own(cotangent), others(cotangent))
    for b in fsdp_deep:
        w_two = grid.deepen(w_two, held_two, b)
    for b in context_deep + fsdp_deep:
        w_three = grid.deepen(w_three, held_three, b)
    gate_full, up_full, down_full = [
        w.reshape(grid.n * shard, quarter) for w in (w_one, w_two, w_three)
    ]
    piece_block = owners[grid.my_slot ^ jnp.arange(slot_count)]
    seen = ((piece_block < prompt_slots) & (piece_block < my_block)).astype(jnp.int32)
    attn_heads, out_low, log_total = attend(seen, queries, pairs, head_group, score_scale)
    hidden_one = own(tokens).astype(F32) + summed(dot_nt(after(out_low, *second_deep), w_out_t))

    inv_two = lax.rsqrt(jnp.mean(hidden_one * hidden_one, axis=-1, keepdims=True) + EPSILON)
    rows_two = hidden_one * inv_two
    normed_two = (rows_two * gain_two.astype(F32)).astype(BF)
    normed_in = grid.tokens_in(normed_two)
    act, grad_gate, grad_up = hidden_units(normed_in, grads_in, gate_full, up_full, down_full)
    top = sorted(range(grid.cbits + grid.fbits), reverse=True)
    shape = (2,) * len(top) + (shard, quarter)
    helds = [list(top) for _ in range(3)]
    down_first = fsdp_deep[::-1] + context_deep[::-1]
    grad_wdown = dot_tn(grads_in, act).astype(BF)
    grad_normed_two = hidden_back(after(grad_gate, grad_wdown), grad_up, gate_full, up_full)
    grad_normed_parts = grad_normed_two
    grad_wdown = grad_wdown.reshape(shape)
    for b in fsdp_deep[::-1]:
        grad_wdown = grid.fold(grad_wdown, helds[0], b)
    grad_normed_two, started = grid.tokens_out(grad_normed_two)
    grad_wgate = dot_tn(normed_in, after(grad_gate, grad_normed_parts)).astype(BF)
    grad_wup = dot_tn(normed_in, after(grad_up, grad_wgate, *started)).astype(BF).reshape(shape)
    grad_wgate = grad_wgate.reshape(shape)
    for b in context_deep[::-1]:
        grad_wdown = grid.fold(grad_wdown, helds[0], b)
    for b in fsdp_deep[::-1]:
        grad_wgate = grid.fold(grad_wgate, helds[1], b)
    for b in context_deep[::-1]:
        grad_wgate = grid.fold(grad_wgate, helds[1], b)
    for b in fsdp_deep[::-1]:
        grad_wup = grid.fold(grad_wup, helds[2], b)

    grad_gain_two = jnp.sum(grad_normed_two * rows_two, axis=0)
    grad_hidden_one = own(cotangent).astype(F32) + norm_back(
        grad_normed_two, rows_two, inv_two, gain_two
    )

    grad_low = both(grad_hidden_one.astype(BF))
    grad_wout = dot_tn(grad_low, out_low).astype(BF)
    grad_heads = dot_nn(grad_low, w_out_t).astype(BF)
    grad_query, grad_pairs = attend_back(
        seen, queries, grad_heads, attn_heads, log_total, pairs, head_group, score_scale
    )
    grad_query_lin = (
        unrotate(grad_query.reshape(block_rows, head_group, head_width), cosine, sine)
        .reshape(block_rows, query_width)
        .astype(BF)
    )
    grad_pair = grad_pairs[0]
    mlp_part = dot_nt(after(act, grad_wup, grad_heads), down_full).astype(BF)
    for part in grid.send([(grad_pairs[r], r) for r in range(1, slot_count)]):
        grad_pair = grad_pair + part.astype(F32)
    grad_wquery = dot_tn(normed_one, grad_query_lin).astype(BF)
    grad_attn = grid.scatter_fsdp(jnp.concatenate([grad_wquery, grad_wout], axis=1))
    for b in context_deep[::-1]:
        grad_wup = grid.fold(grad_wup, helds[2], b)
    grad_key_lin = unrotate(
        grad_pair[:, :head_width].reshape(block_rows, 1, head_width), cosine, sine
    ).reshape(block_rows, head_width)
    grad_kv = jnp.concatenate([grad_key_lin, grad_pair[:, head_width:]], axis=1).astype(BF)
    mlp_total, _ = grid.tokens_out(mlp_part)
    result = both((after(hidden_one, grad_query) + mlp_total).astype(BF))
    grad_wkv = grid.scatter_fsdp(dot_tn(normed_one, grad_kv).astype(BF))
    grad_dg = grid.quarters_out(jnp.concatenate([grad_wdown, grad_wgate], axis=2))
    grad_wdown, grad_wgate = grad_dg[:shard], grad_dg[shard:]
    grad_attn = grid.scatter_context(jnp.concatenate([grad_attn, grad_wkv], axis=1))
    grad_wup = grid.quarters_out(grad_wup)
    grad_qkv = jnp.concatenate([grad_query_lin, grad_kv], axis=1)
    grad_bias = jnp.sum(grad_qkv.astype(F32), axis=0)
    grad_normed_one = summed(dot_nt(grad_qkv, w_qkv))
    rows_own = own(rows_one)
    inv_own = own(inv_one)
    grad_gain_one = jnp.sum(grad_normed_one * rows_own, axis=0)
    grad_inputs = grad_hidden_one + norm_back(grad_normed_one, rows_own, inv_own, gain_one)
    grad_tokens = both(grad_inputs.astype(BF))

    gains = jnp.concatenate(
        [grad_gain_one.reshape(-1, shard), grad_gain_two.reshape(-1, shard)], axis=1
    )
    gains = gains + grid.swap(gains)
    small = jnp.concatenate(
        [
            gains,
            grad_bias[:query_width].reshape(-1, bias_shard),
            grad_bias[query_width : query_width + head_width].reshape(-1, small_bias),
            grad_bias[query_width + head_width :].reshape(-1, small_bias),
        ],
        axis=1,
    )
    small = grid.scatter_small(small)
    return (
        result,
        grad_tokens,
        small[0, :shard],
        grad_attn[:, :query_width],
        small[:, start : start + bias_shard],
        grad_attn[:, 2 * query_width : 2 * query_width + head_width],
        small[:, start + bias_shard : start + bias_shard + small_bias],
        grad_attn[:, 2 * query_width + head_width :],
        small[:, start + bias_shard + small_bias :],
        grad_attn[:, query_width : 2 * query_width].T,
        small[0, shard : 2 * shard],
        grad_wgate[:, :hidden],
        grad_wup[:, :hidden],
        grad_wdown[:, :hidden].T,
    )


def solution(mesh):
    rows = P(("fsdp", "context"), None)
    split = P(("fsdp", "context"))
    into = P(("fsdp", "context"), "tensor")
    back = P("tensor", ("fsdp", "context"))
    return jax.shard_map(
        on_device,
        mesh=mesh,
        in_specs=(
            rows,
            P("fsdp", None),
            split,
            into,
            back,
            into,
            back,
            into,
            back,
            back,
            split,
            into,
            into,
            back,
            rows,
        ),
        out_specs=(
            rows,
            rows,
            split,
            into,
            back,
            into,
            back,
            into,
            back,
            back,
            split,
            into,
            into,
            back,
        ),
        check_vma=False,
    )
```

```python
import functools

import jax
import jax.numpy as jnp
from jax import lax
from jax.experimental import pallas as pl
from jax.experimental.pallas import tpu as pltpu
from jax.sharding import PartitionSpec as P

EPSILON = 1e-06
ROPE_BASE = 1000000.0
MASKED = -1e30
LANES = 128
BOTH = ("fsdp", "context")
KERNEL_BYTES = 56 << 20
BF = jnp.bfloat16
F32 = jnp.float32


def tables(positions, head_width):
    ladder = jnp.arange(head_width // 2, dtype=F32)
    inverse = jnp.exp(-jnp.log(ROPE_BASE) * 2.0 * ladder / head_width)
    angles = positions.astype(F32)[:, None] * inverse[None, :]
    cosine, sine = jnp.cos(angles), jnp.sin(angles)
    return (
        jnp.concatenate([cosine, cosine], axis=1),
        jnp.concatenate([-sine, sine], axis=1),
    )


def swap_halves(x):
    middle = x.shape[1] // 2
    return jnp.concatenate([x[:, middle:], x[:, :middle]], axis=1)


def locate(blocks, prompt_slots, block_rows):
    segment = jnp.where(blocks < prompt_slots, 0, blocks - prompt_slots + 1)
    anchor = jnp.where(blocks < prompt_slots, blocks * block_rows, prompt_slots * block_rows)
    return (segment, anchor)


def dot_nn(left, right):
    return lax.dot_general(left, right, (((1,), (0,)), ((), ())), preferred_element_type=F32)


def dot_tn(left, right):
    return lax.dot_general(left, right, (((0,), (0,)), ((), ())), preferred_element_type=F32)


def dot_nt(left, right):
    return lax.dot_general(left, right, (((1,), (1,)), ((), ())), preferred_element_type=F32)


def norm_back(grad_normed, rows_normed, inv_rms, gain):
    grad_rows = grad_normed * gain.astype(F32)
    return inv_rms * (
        grad_rows - rows_normed * jnp.mean(grad_rows * rows_normed, axis=-1, keepdims=True)
    )


def turn(x, cosine, sine):
    return x * cosine + pltpu.roll(x, x.shape[1] // 2, 1) * sine


def attend_kernel(count, scale, seen, lin_ref, cos_ref, sin_ref, *refs):
    pairs = refs[:count]
    q_ref, out_ref, low_ref, lse_ref, peak_ref, total_ref, sum_ref = refs[count:]
    wide = lin_ref.shape[1]
    query = turn(lin_ref[...], cos_ref[...], sin_ref[...]).astype(BF)
    q_ref[...] = query

    def piece(r):
        scores = dot_nt(pairs[r][:, :wide], query) * scale
        if r == 0:
            rows = lax.broadcasted_iota(jnp.int32, scores.shape, 0)
            columns = lax.broadcasted_iota(jnp.int32, scores.shape, 1)
            scores = jnp.where(rows <= columns, scores, MASKED)
            peak = jnp.max(scores, axis=0, keepdims=True)
        else:
            old = peak_ref[...]
            peak = jnp.maximum(old, jnp.max(scores, axis=0, keepdims=True))
        probs = jnp.exp(scores - peak)
        total = jnp.sum(probs, axis=0, keepdims=True)
        mixed = dot_tn(pairs[r][:, wide:], probs.astype(BF))
        if r:
            shrink = jnp.exp(old - peak)
            total = total + total_ref[...] * shrink
            mixed = mixed + sum_ref[...] * shrink
        peak_ref[...] = peak
        total_ref[...] = total
        sum_ref[...] = mixed

    piece(0)
    for r in range(1, count):
        pl.when(seen[r] != 0)(functools.partial(piece, r))
    total = total_ref[...]
    out = jnp.transpose(sum_ref[...] / total)
    out_ref[...] = out
    low_ref[...] = out.astype(BF)
    lse_ref[...] = (peak_ref[...] + jnp.log(total))[None]


def attend(seen, lin, cosine, sine, pairs, heads, scale):
    rows, wide = cosine.shape
    count = len(pairs)
    every = pl.BlockSpec((rows, wide), lambda h, seen: (0, 0))
    head = pl.BlockSpec((rows, wide), lambda h, seen: (0, h))
    whole = pl.BlockSpec(pairs[0].shape, lambda h, seen: (0, 0))
    return pl.pallas_call(
        functools.partial(attend_kernel, count, scale),
        grid_spec=pltpu.PrefetchScalarGridSpec(
            num_scalar_prefetch=1,
            grid=(heads,),
            in_specs=[head, every, every] + [whole] * count,
            out_specs=[head, head, head, pl.BlockSpec((1, 1, rows), lambda h, seen: (h, 0, 0))],
            scratch_shapes=[
                pltpu.VMEM((1, rows), F32),
                pltpu.VMEM((1, rows), F32),
                pltpu.VMEM((wide, rows), F32),
            ],
        ),
        out_shape=[
            jax.ShapeDtypeStruct((rows, heads * wide), BF),
            jax.ShapeDtypeStruct((rows, heads * wide), F32),
            jax.ShapeDtypeStruct((rows, heads * wide), BF),
            jax.ShapeDtypeStruct((heads, 1, rows), F32),
        ],
        compiler_params=pltpu.CompilerParams(vmem_limit_bytes=KERNEL_BYTES),
        cost_estimate=pl.CostEstimate(flops=1, bytes_accessed=1, transcendentals=0),
    )(seen, lin, cosine, sine, *pairs)


def attend_back_kernel(
    count, scale, seen, q_ref, g_ref, out_ref, lse_ref, cos_ref, sin_ref, *refs
):
    pairs = refs[:count]
    dq_ref = refs[count]
    grads = refs[count + 1 : 2 * count + 1]
    held, sum_ref = refs[2 * count + 1 :]
    wide = q_ref.shape[1]
    step = pl.program_id(0)
    query = q_ref[...]
    grad = g_ref[...]
    delta = jnp.sum(grad.astype(F32) * out_ref[...], axis=1, keepdims=True)
    delta = jnp.transpose(jnp.broadcast_to(delta, q_ref.shape))[:1]
    lse = lse_ref[0]

    @pl.when(step == 0)
    def _():
        held[...] = jnp.zeros_like(held)

    def piece(r):
        key = pairs[r][:, :wide]
        probs = jnp.exp(dot_nt(key, query) * scale - lse)
        if r == 0:
            rows = lax.broadcasted_iota(jnp.int32, probs.shape, 0)
            columns = lax.broadcasted_iota(jnp.int32, probs.shape, 1)
            probs = jnp.where(rows <= columns, probs, 0.0)
        grad_scores = (probs * (dot_nt(pairs[r][:, wide:], grad) - delta)).astype(BF)
        held[r, :, wide:] += dot_nn(probs.astype(BF), grad)
        held[r, :, :wide] += dot_nn(grad_scores, query) * scale
        term = dot_tn(key, grad_scores)
        sum_ref[...] = term if r == 0 else sum_ref[...] + term

    piece(0)
    for r in range(1, count):
        pl.when(seen[r] != 0)(functools.partial(piece, r))
    grad_query = jnp.transpose(sum_ref[...]) * scale
    dq_ref[...] = turn(grad_query, cos_ref[...], -sin_ref[...]).astype(BF)

    @pl.when(step == pl.num_programs(0) - 1)
    def _():
        for r in range(count):
            grads[r][...] = held[r].astype(grads[r].dtype)


def attend_back(seen, queries, grads, outs, lse, cosine, sine, pairs, heads, scale):
    rows = queries.shape[0]
    wide = queries.shape[1] // heads
    count = len(pairs)
    head = pl.BlockSpec((rows, wide), lambda h, seen: (0, h))
    whole = pl.BlockSpec(pairs[0].shape, lambda h, seen: (0, 0))
    results = pl.pallas_call(
        functools.partial(attend_back_kernel, count, scale),
        grid_spec=pltpu.PrefetchScalarGridSpec(
            num_scalar_prefetch=1,
            grid=(heads,),
            in_specs=[head] * 3
            + [pl.BlockSpec((1, 1, rows), lambda h, seen: (h, 0, 0))]
            + [pl.BlockSpec((rows, wide), lambda h, seen: (0, 0))] * 2
            + [whole] * count,
            out_specs=[head] + [whole] * count,
            scratch_shapes=[
                pltpu.VMEM((count,) + pairs[0].shape, F32),
                pltpu.VMEM((wide, rows), F32),
            ],
        ),
        out_shape=[jax.ShapeDtypeStruct(queries.shape, BF)]
        + [jax.ShapeDtypeStruct(pairs[0].shape, F32 if r == 0 else BF) for r in range(count)],
        compiler_params=pltpu.CompilerParams(vmem_limit_bytes=KERNEL_BYTES),
        cost_estimate=pl.CostEstimate(flops=1, bytes_accessed=1, transcendentals=0),
    )(seen, queries, grads, outs, lse, cosine, sine, *pairs)
    return results[0], results[1:]


def products_kernel(a_ref, b_ref, c_ref, d_ref, out_ref):
    wide = b_ref.shape[1]
    out_ref[:, :wide] = dot_tn(a_ref[...], b_ref[...]).astype(BF)
    out_ref[:, wide:] = dot_tn(c_ref[...], d_ref[...]).astype(BF)


def products(a, b, c, d):
    tokens, depth = a.shape
    tile = depth // 3 if depth % (3 * LANES) == 0 else depth
    left = pl.BlockSpec((tokens, tile), lambda m: (0, m))
    right = pl.BlockSpec(b.shape, lambda m: (0, 0))
    return pl.pallas_call(
        products_kernel,
        grid=(depth // tile,),
        in_specs=[left, right, left, right],
        out_specs=pl.BlockSpec((tile, 2 * b.shape[1]), lambda m: (m, 0)),
        out_shape=jax.ShapeDtypeStruct((depth, 2 * b.shape[1]), BF),
        compiler_params=pltpu.CompilerParams(vmem_limit_bytes=KERNEL_BYTES),
        cost_estimate=pl.CostEstimate(flops=1, bytes_accessed=1, transcendentals=0),
    )(a, b, c, d)


def hidden_kernel(n_ref, wg_ref, wu_ref, act_ref, by_gate_ref, by_up_ref):
    gate = dot_nn(n_ref[...], wg_ref[...])
    up = dot_nn(n_ref[...], wu_ref[...])
    sigmoid = jax.nn.sigmoid(gate)
    silu = gate * sigmoid
    act_ref[...] = (silu * up).astype(BF)
    by_gate_ref[...] = (up * (sigmoid + silu * (1.0 - sigmoid))).astype(BF)
    by_up_ref[...] = silu.astype(BF)


def hidden_units(normed, gate_w, up_w):
    tokens, depth = normed.shape
    units = gate_w.shape[1]
    tm = min(tokens, 256)
    rows = pl.BlockSpec((tm, depth), lambda m: (m, 0))
    weight = pl.BlockSpec((depth, units), lambda m: (0, 0))
    out = pl.BlockSpec((tm, units), lambda m: (m, 0))
    return pl.pallas_call(
        hidden_kernel,
        grid=(tokens // tm,),
        in_specs=[rows, weight, weight],
        out_specs=[out] * 3,
        out_shape=[jax.ShapeDtypeStruct((tokens, units), BF)] * 3,
        compiler_params=pltpu.CompilerParams(vmem_limit_bytes=KERNEL_BYTES),
        cost_estimate=pl.CostEstimate(flops=1, bytes_accessed=1, transcendentals=0),
    )(normed, gate_w, up_w)


def hidden_grad_kernel(d_ref, wd_ref, by_gate_ref, by_up_ref, dg_ref, du_ref):
    grad = dot_nn(d_ref[...], wd_ref[...])
    dg_ref[...] = (grad * by_gate_ref[...].astype(F32)).astype(BF)
    du_ref[...] = (grad * by_up_ref[...].astype(F32)).astype(BF)


def hidden_grads(grads, down_w, by_gate, by_up):
    tokens, depth = grads.shape
    units = down_w.shape[1]
    tm = min(tokens, 256)
    out = pl.BlockSpec((tm, units), lambda m: (m, 0))
    return pl.pallas_call(
        hidden_grad_kernel,
        grid=(tokens // tm,),
        in_specs=[
            pl.BlockSpec((tm, depth), lambda m: (m, 0)),
            pl.BlockSpec((depth, units), lambda m: (0, 0)),
            out,
            out,
        ],
        out_specs=[out] * 2,
        out_shape=[jax.ShapeDtypeStruct((tokens, units), BF)] * 2,
        compiler_params=pltpu.CompilerParams(vmem_limit_bytes=KERNEL_BYTES),
        cost_estimate=pl.CostEstimate(flops=1, bytes_accessed=1, transcendentals=0),
    )(grads, down_w, by_gate, by_up)


def back_kernel(count, half, *refs):
    lefts, rights = refs[:count], refs[count : 2 * count]
    first, second = refs[2 * count :]
    total = dot_nt(lefts[0][...], rights[0][...])
    for left, right in zip(lefts[1:], rights[1:]):
        total = total + dot_nt(left[...], right[...])
    step = pl.program_id(0)

    @pl.when(step < half)
    def _():
        first[...] = total.astype(BF)

    @pl.when(step >= half)
    def _():
        second[...] = total.astype(BF)


def hidden_back(lefts, rights):
    tokens, units = lefts[0].shape
    depth = rights[0].shape[0]
    count = len(lefts)
    tm = min(tokens // 2, 512)
    half = tokens // 2 // tm
    rows = pl.BlockSpec((tm, units), lambda m: (m, 0))
    weight = pl.BlockSpec((depth, units), lambda m: (0, 0))
    return pl.pallas_call(
        functools.partial(back_kernel, count, half),
        grid=(tokens // tm,),
        in_specs=[rows] * count + [weight] * count,
        out_specs=[
            pl.BlockSpec((tm, depth), lambda m: (jnp.minimum(m, half - 1), 0)),
            pl.BlockSpec((tm, depth), lambda m: (jnp.maximum(m - half, 0), 0)),
        ],
        out_shape=[jax.ShapeDtypeStruct((tokens // 2, depth), BF)] * 2,
        compiler_params=pltpu.CompilerParams(vmem_limit_bytes=KERNEL_BYTES),
        cost_estimate=pl.CostEstimate(flops=1, bytes_accessed=1, transcendentals=0),
    )(*lefts, *rights)


def after(x, *earlier):
    return lax.optimization_barrier((x,) + earlier)[0]


class Pending:
    def __init__(self, got, finish):
        self.got = got
        self.finish = finish


class Grid:
    def __init__(self):
        self.nf = lax.axis_size("fsdp")
        self.nc = lax.axis_size("context")
        self.n = self.nf * self.nc
        self.cbits = self.nc.bit_length() - 1
        self.fbits = self.nf.bit_length() - 1
        self.me = lax.axis_index("fsdp") * self.nc + lax.axis_index("context")
        self.my_slot = lax.axis_index("context")
        self.core = lax.axis_index("tensor")
        self.done = ()
        self.zm = 1
        self.xm = self.nc
        self.deep = list(range(1, self.cbits)) + list(range(self.cbits + 1, self.cbits + self.fbits))

    def bit(self, b):
        return (self.me >> b) & 1

    def fence(self, *xs):
        return lax.optimization_barrier(xs + self.done)[: len(xs)]

    def close(self, *xs):
        raw = lax.optimization_barrier(
            tuple(x.got if isinstance(x, Pending) else x for x in xs)
        )
        self.done = raw
        outs = [x.finish(r) if isinstance(x, Pending) else r for x, r in zip(xs, raw)]
        return outs[0] if len(outs) == 1 else outs

    def one(self, x, mask, pin=()):
        if pin:
            x = after(x, *pin)
        return lax.ppermute(x, BOTH, [(i, i ^ mask) for i in range(self.n)])

    def swap(self, x):
        return lax.ppermute(x, "tensor", [(0, 1), (1, 0)])

    def pair(self, b, mine, theirs, axis):
        low = self.bit(b) == 0
        return jnp.stack([jnp.where(low, mine, theirs), jnp.where(low, theirs, mine)], axis)

    def ordered(self, pieces, bits):
        if len(bits) == 0:
            return pieces[0]
        half = len(pieces) // 2
        low = self.ordered(pieces[:half], bits[:-1])
        high = self.ordered(pieces[half:], bits[:-1])
        return self.pair(bits[-1], low, high, 0)

    def fsdp_take(self, x, r):
        x = x.reshape(self.nf, -1, x.shape[1])
        return lax.dynamic_index_in_dim(x, lax.axis_index("fsdp") ^ r, 0, keepdims=False)

    def fsdp_far(self, x):
        far = self.fsdp_take(x, 3)
        cut = far.shape[0] // 2
        return far[:cut], far[cut:]

    def fsdp_near(self, x, by_y, by_x):
        px, py = self.fsdp_take(x, 1), self.fsdp_take(x, 2)
        cut = px.shape[0] // 2
        px = jnp.concatenate([px[:cut].astype(F32) + by_y.astype(F32), px[cut:].astype(F32)], 0)
        py = jnp.concatenate([py[:cut].astype(F32), py[cut:].astype(F32) + by_x.astype(F32)], 0)
        return px.astype(BF), py.astype(BF)

    def fsdp_end(self, x, rx, ry):
        return (self.fsdp_take(x, 0).astype(F32) + rx.astype(F32) + ry.astype(F32)).astype(BF)

    def over_x(self, x):
        return self.one(x, self.xm)

    def over_y(self, x):
        return self.one(x, 2 * self.xm)

    def over_z(self, x):
        return self.one(x, self.zm)

    def context_pick(self, x, r):
        x = x.reshape(self.nc, -1, x.shape[1])
        return lax.dynamic_index_in_dim(x, self.my_slot ^ r, 0, keepdims=False)

    def scatter_context(self, x):
        gives = self.fence(*[self.context_pick(x, r) for r in range(1, self.nc)])
        total = self.context_pick(x, 0).astype(F32)
        for r in range(1, self.nc):
            total = total + self.one(gives[r - 1], r).astype(F32)
        return total

    def tokens_near(self, x, pin_x=(), pin_z=()):
        return self.one(x, self.xm, pin_x), self.one(x, self.zm, pin_z)

    def tokens_far(self, nears):
        cut = nears[0][0].shape[0] // 2
        by_z = self.one(jnp.concatenate([px[:cut] for px, _ in nears], 0), self.zm)
        by_x = self.one(jnp.concatenate([pz[cut:] for _, pz in nears], 0), self.xm)
        parts = []
        for k, (px, pz) in enumerate(nears):
            here = slice(k * cut, (k + 1) * cut)
            parts.append(jnp.concatenate([px, pz, by_z[here], by_x[here]], 0))
        return parts

    def tokens_split(self, part, other):
        rows = part.shape[0] // 4
        cut = rows // 2
        here = [slice(k * rows, (k + 1) * rows) for k in range(4)]
        own, px, pz, far = [part[k].astype(F32) + other[k].astype(F32) for k in here]
        return own, px, pz, far[:cut].astype(BF), far[cut:].astype(BF)

    def tokens_add(self, px, pz, by_z, by_x):
        cut = by_z.shape[0]
        px = jnp.concatenate([px[:cut] + by_z.astype(F32), px[cut:]], 0).astype(BF)
        pz = jnp.concatenate([pz[:cut], pz[cut:] + by_x.astype(F32)], 0).astype(BF)
        return px, pz

    def quarter_masks(self):
        return (0, self.zm, self.xm, self.xm + self.zm)

    def my_quarter(self):
        return 2 * self.bit(self.cbits) + self.bit(0)

    def quarter_groups(self):
        masks = (0, self.zm, self.xm, self.xm + self.zm)
        return [[i | m for m in masks] for i in range(self.n) if i & masks[3] == 0]

    def quarters_in(self, w):
        return lax.all_to_all(w, BOTH, 0, 0, axis_index_groups=self.quarter_groups())

    def quarters_out(self, g):
        return lax.all_to_all(g, BOTH, 0, 0, axis_index_groups=self.quarter_groups())

    def deepen(self, w, held, bits):
        for b in bits[:-1]:
            w = self.pair(b, w, self.one(w, 1 << b), sum(1 for h in held if h > b))
            held.append(b)
        b = bits[-1]
        axis = sum(1 for h in held if h > b)
        held.append(b)
        return Pending(self.one(w, 1 << b), lambda got: self.pair(b, w, got, axis))

    def fold(self, g, held, bits):
        def step(g, b):
            axis = held.index(b)
            held.remove(b)
            give = lax.dynamic_index_in_dim(g, 1 - self.bit(b), axis, keepdims=False)
            keep = lax.dynamic_index_in_dim(g, self.bit(b), axis, keepdims=False)
            finish = lambda got: (keep.astype(F32) + got.astype(F32)).astype(BF)
            return Pending(self.one(give, 1 << b), finish)

        for b in bits[:-1]:
            pending = step(g, b)
            g = pending.finish(pending.got)
        return step(g, bits[-1])


def on_device(
    tokens,
    block_order,
    norm_one,
    w_query,
    b_query,
    w_key,
    b_key,
    w_value,
    b_value,
    w_out,
    norm_two,
    w_gate,
    w_up,
    w_down,
    cotangent,
):
    grid = Grid()
    block_rows, width = tokens.shape
    shard = norm_one.shape[0]
    slot_count = grid.nc
    prompt_slots = slot_count // 2
    head_width = w_key.shape[1]
    query_width = w_query.shape[1]
    head_group = query_width // head_width
    score_scale = head_width ** (-0.5)
    cores = lax.axis_size("tensor")
    own_rows = block_rows // cores
    owners = block_order[0]
    my_block = lax.dynamic_index_in_dim(owners, grid.my_slot, 0, keepdims=False)
    query_anchor = locate(my_block, prompt_slots, block_rows)[1]
    query_pos = query_anchor + jnp.arange(block_rows)

    def own(x):
        return lax.dynamic_slice(x, (grid.core * own_rows, 0), (own_rows, x.shape[1]))

    def others(x):
        return lax.dynamic_slice(x, ((1 - grid.core) * own_rows, 0), (own_rows, x.shape[1]))

    def both(x):
        other = grid.swap(x)
        first = grid.core == 0
        return jnp.concatenate([jnp.where(first, x, other), jnp.where(first, other, x)], 0)

    def summed(part):
        give = lax.dynamic_slice(part, ((1 - grid.core) * own_rows, 0), (own_rows, width))
        return own(part) + grid.swap(give.astype(BF)).astype(F32)

    bias_shard = b_query.shape[1]
    small_bias = b_key.shape[1]
    vector = jnp.concatenate([norm_one[None], norm_two[None], b_query, b_key, b_value], axis=1)
    columns = query_width + 2 * head_width
    vector = jnp.pad(vector, ((0, 7), (0, columns - vector.shape[1])))
    packed = jnp.concatenate(
        [jnp.concatenate([w_query, w_key, w_value], axis=1), vector], axis=0
    )
    hidden = w_gate.shape[1]
    quarter = -(-hidden // (4 * LANES)) * LANES
    pad = ((0, 0), (0, 4 * quarter - hidden))
    w_out_t = lax.all_gather(w_out.T, BOTH, axis=0, tiled=True)

    context_deep = [b for b in grid.deep if b < grid.cbits]
    fsdp_deep = [b for b in grid.deep if b > grid.cbits]

    def quarters(w):
        return w.reshape(shard, 4, quarter).transpose(1, 0, 2)

    def deep_z(w):
        return grid.deepen(w, [0], context_deep)

    def deep_y(w):
        return grid.deepen(w, [0] + context_deep, fsdp_deep)

    def whole(halves):
        return jnp.stack(halves, len(fsdp_deep)).reshape(grid.n * shard, quarter)

    held = []
    gate_near = grid.quarters_in(quarters(jnp.pad(w_gate, pad)))
    packed = grid.deepen(packed, held, context_deep[::-1])
    gate_near, packed = grid.close(gate_near, packed)

    gate_near = gate_near.reshape(2, 2, shard, quarter)
    packed = grid.close(grid.deepen(packed, held, [0]))

    packed = packed.reshape(grid.nc * (shard + 8), columns)
    (gate_0,) = grid.fence(gate_near[0])
    gx, gy, gate_0 = grid.close(grid.over_x(packed), grid.over_y(packed), deep_z(gate_0))

    cut = gx.shape[0] // 2
    gate_1, up_in = grid.fence(gate_near[1], quarters(jnp.pad(w_up, pad)))
    by_y, by_x = grid.over_y(gx[:cut]), grid.over_x(gy[cut:])
    by_y, by_x, gate_1, up_near = grid.close(
        by_y, by_x, deep_z(gate_1), grid.quarters_in(up_in)
    )

    up_near = up_near.reshape(2, 2, shard, quarter)
    pieces = [packed, gx, gy, jnp.concatenate([by_y, by_x], 0)]
    pieces = [x.reshape(grid.nc, shard + 8, columns) for x in pieces]
    sources = [grid.cbits, grid.cbits + 1]
    w_qkv = grid.ordered([x[:, :shard] for x in pieces], sources)
    w_qkv = w_qkv.reshape(grid.n * shard, columns)
    vectors = grid.ordered([x[:, shard] for x in pieces], sources).reshape(grid.n, columns)
    gain_one = vectors[:, :shard].reshape(-1)
    gain_two = vectors[:, shard : 2 * shard].reshape(-1)
    start = 2 * shard
    bias = jnp.concatenate(
        [
            vectors[:, start : start + bias_shard].reshape(-1),
            vectors[:, start + bias_shard : start + bias_shard + small_bias].reshape(-1),
            vectors[
                :, start + bias_shard + small_bias : start + bias_shard + 2 * small_bias
            ].reshape(-1),
        ]
    ).astype(F32)

    inputs = tokens.astype(F32)
    inv_one = lax.rsqrt(jnp.mean(inputs * inputs, axis=-1, keepdims=True) + EPSILON)
    rows_one = inputs * inv_one
    normed_one = (rows_one * gain_one.astype(F32)).astype(BF)
    cosine, sine = tables(query_pos, head_width)
    grads_own, grads_other = own(cotangent), others(cotangent)
    gate_0, grads_pz = grid.fence(gate_0, grads_own)
    gate_0, grads_pz = deep_y(gate_0), grid.over_z(grads_pz)
    qkv = dot_nn(normed_one, w_qkv) + bias
    keys = qkv[:, query_width : query_width + head_width]
    keys = keys * cosine + swap_halves(keys) * sine
    pair = jnp.concatenate([keys, qkv[:, query_width + head_width :]], axis=1).astype(BF)
    pair, qkv, gate_0, grads_pz = grid.close(pair, qkv, gate_0, grads_pz)

    gate_1, grads_px = grid.fence(gate_1, grads_own)
    met = [grid.one(pair, r) for r in range(1, slot_count)]
    gate_1, grads_px, *met = grid.close(deep_y(gate_1), grid.over_x(grads_px), *met)
    pairs = [pair] + met

    piece_block = owners[grid.my_slot ^ jnp.arange(slot_count)]
    seen = ((piece_block < prompt_slots) & (piece_block < my_block)).astype(jnp.int32)
    up_0, down_in = grid.fence(up_near[0], quarters(jnp.pad(w_down.T, pad)))
    up_0, down_near = deep_z(up_0), grid.quarters_in(down_in)
    queries, attn_heads, out_low, log_total = attend(
        seen, qkv, cosine, sine, pairs, head_group, score_scale
    )
    out_low, up_0, down_near = grid.close(out_low, up_0, down_near)

    down_near = down_near.reshape(2, 2, shard, quarter)
    hidden_one = own(tokens).astype(F32) + summed(dot_nt(out_low, w_out_t))

    inv_two = lax.rsqrt(jnp.mean(hidden_one * hidden_one, axis=-1, keepdims=True) + EPSILON)
    rows_two = hidden_one * inv_two
    normed_two = (rows_two * gain_two.astype(F32)).astype(BF)
    normed_two = grid.close(normed_two)

    up_0, up_1 = grid.fence(up_0, up_near[1])
    px, pz, normed_other, up_1, up_0 = grid.close(
        grid.over_x(normed_two),
        grid.over_z(normed_two),
        grid.swap(normed_two),
        deep_z(up_1),
        deep_y(up_0),
    )

    cut = px.shape[0] // 2
    (down_0,) = grid.fence(down_near[0])
    by_z, by_x, up_1, down_0 = grid.close(
        grid.over_z(px[:cut]), grid.over_x(pz[cut:]), deep_y(up_1), deep_z(down_0)
    )

    normed_got = jnp.concatenate([px, pz, by_z, by_x], 0)
    gate_0, gate_1, up_0 = grid.fence(gate_0, gate_1, up_0)
    gate_full, up_full = whole([gate_0, gate_1]), whole([up_0, up_1])
    normed_far, gate_full, up_full = grid.close(grid.swap(normed_got), gate_full, up_full)

    normed_in = jnp.concatenate([normed_two, normed_got, normed_other, normed_far], 0)
    far_z, far_x, down_0, down_1 = grid.fence(
        grads_px[:cut], grads_pz[cut:], down_0, down_near[1]
    )
    by_z, by_x = grid.over_z(far_z), grid.over_x(far_x)
    down_0, down_1 = deep_y(down_0), deep_z(down_1)
    act, by_gate, by_up = hidden_units(normed_in, gate_full, up_full)
    act, by_z, by_x, down_0, down_1 = grid.close(act, by_z, by_x, down_0, down_1)

    grads_got = jnp.concatenate([grads_px, grads_pz, by_z, by_x], 0)
    down_1 = deep_y(down_1)
    grads_in = jnp.concatenate(
        [grads_own, grads_got, grads_other, grid.swap(grads_got)], 0
    )
    grad_wdown = dot_tn(grads_in, act).astype(BF)
    grad_wdown, down_1 = grid.close(grad_wdown, down_1)

    top = sorted(range(grid.cbits + grid.fbits), reverse=True)
    shape = (2,) * len(top) + (shard, quarter)
    y_back, z_back = fsdp_deep[::-1], context_deep[::-1]

    def half(grad, h):
        return lax.index_in_dim(grad.reshape(shape), h, top.index(grid.cbits), keepdims=False)

    def fold_y(grad):
        return grid.fold(grad, [b for b in top if b != grid.cbits], y_back)

    def fold_z(grad):
        return grid.fold(grad, [b for b in top if b not in fsdp_deep and b != grid.cbits], z_back)

    def joined(first, second):
        return jnp.stack([first, second], 0).reshape(4, shard, quarter)

    down_full = whole([down_0, down_1])
    down_0 = fold_y(half(grad_wdown, 0))
    grad_gate, grad_up = hidden_grads(grads_in, down_full, by_gate, by_up)
    down_0, grad_gate, grad_up = grid.close(down_0, grad_gate, grad_up)

    (down_1,) = grid.fence(half(grad_wdown, 1))
    down_0, down_1 = fold_z(down_0), fold_y(down_1)
    part, give = hidden_back((grad_gate, grad_up), (gate_full, up_full))
    down_0, down_1, part, give = grid.close(down_0, down_1, part, give)

    other = grid.swap(give)
    (up_in,) = grid.fence(grad_up)
    grad_wup = dot_tn(normed_in, up_in).astype(BF)
    other, grad_wup = grid.close(other, grad_wup)

    part_own, px, pz, far_z, far_x = grid.tokens_split(part, other)
    down_1, gate_in = grid.fence(down_1, grad_gate)
    by_z, by_x = grid.over_z(far_z), grid.over_x(far_x)
    down_1, up_0 = fold_z(down_1), fold_y(half(grad_wup, 0))
    grad_wgate = dot_tn(normed_in, gate_in).astype(BF)
    by_z, by_x, down_1, up_0, grad_wgate = grid.close(by_z, by_x, down_1, up_0, grad_wgate)

    px, pz = grid.tokens_add(px, pz, by_z, by_x)
    up_1, act_in = grid.fence(half(grad_wup, 1), act)
    px, pz = grid.over_x(px), grid.over_z(pz)
    up_0, up_1 = fold_z(up_0), fold_y(up_1)
    mlp_part, mlp_give = hidden_back((act_in,), (down_full,))
    px, pz, up_0, up_1, mlp_part, mlp_give = grid.close(
        px, pz, up_0, up_1, mlp_part, mlp_give
    )

    (down_in,) = grid.fence(joined(down_0, down_1))
    grad_wdown = grid.quarters_out(down_in)
    mlp_other = grid.swap(mlp_give)
    grad_normed_two = part_own + px.astype(F32) + pz.astype(F32)
    grad_gain_two = jnp.sum(grad_normed_two * rows_two, axis=0)
    grad_hidden_one = own(cotangent).astype(F32) + norm_back(
        grad_normed_two, rows_two, inv_two, gain_two
    )
    grad_low = both(grad_hidden_one.astype(BF))
    grad_heads = dot_nn(grad_low, w_out_t).astype(BF)
    grad_heads, mlp_other, grad_wdown = grid.close(grad_heads, mlp_other, grad_wdown)

    mlp_own, mx, mz, far_z, far_x = grid.tokens_split(mlp_part, mlp_other)
    gate_0, up_1 = grid.fence(half(grad_wgate, 0), up_1)
    by_z, by_x = grid.over_z(far_z), grid.over_x(far_x)
    gate_0, up_1 = fold_y(gate_0), fold_z(up_1)
    grad_query, grad_pairs = attend_back(
        seen,
        queries,
        grad_heads,
        attn_heads,
        log_total,
        cosine,
        sine,
        pairs,
        head_group,
        score_scale,
    )
    by_z, by_x, gate_0, up_1, grad_query, *grad_pairs = grid.close(
        by_z, by_x, gate_0, up_1, grad_query, *grad_pairs
    )

    grad_got = [grid.one(x, r + 1) for r, x in enumerate(grad_pairs[1:])]
    mx, mz = grid.tokens_add(mx, mz, by_z, by_x)
    (gate_1,) = grid.fence(half(grad_wgate, 1))
    mx, gate_1 = grid.over_x(mx), fold_y(gate_1)
    grad_attn = products(normed_one, grad_query, grad_low, out_low)
    mx, gate_1, grad_attn, *grad_got = grid.close(mx, gate_1, grad_attn, *grad_got)

    far_y, far_x = grid.fsdp_far(grad_attn)
    mz, grad_query = grid.fence(mz, grad_query)
    by_y, by_x = grid.over_y(far_y), grid.over_x(far_x)
    gate_0, mz = fold_z(gate_0), grid.over_z(mz)
    grad_pair = grad_pairs[0]
    for x in grad_got:
        grad_pair = grad_pair + x.astype(F32)
    grad_keys = grad_pair[:, :head_width]
    grad_keys = grad_keys * cosine - swap_halves(grad_keys) * sine
    grad_kv = jnp.concatenate([grad_keys, grad_pair[:, head_width:]], axis=1).astype(BF)
    grad_qkv = jnp.concatenate([grad_query, grad_kv], axis=1)
    grad_bias = jnp.sum(grad_qkv.astype(F32), axis=0)
    grad_normed_one = summed(dot_nt(grad_qkv, w_qkv))
    rows_own = own(rows_one)
    inv_own = own(inv_one)
    grad_gain_one = jnp.sum(grad_normed_one * rows_own, axis=0)
    gains = jnp.concatenate(
        [grad_gain_one.reshape(-1, shard), grad_gain_two.reshape(-1, shard)], axis=1
    )
    gains = gains + grid.swap(gains)
    small = jnp.concatenate(
        [
            gains,
            grad_bias[:query_width].reshape(-1, bias_shard),
            grad_bias[query_width : query_width + head_width].reshape(-1, small_bias),
            grad_bias[query_width + head_width :].reshape(-1, small_bias),
        ],
        axis=1,
    )
    wide = 2 * head_width
    small = jnp.pad(small[:, None], ((0, 0), (0, 7), (0, max(wide - small.shape[1], 0))))
    grad_wkv = dot_tn(normed_one, grad_kv).reshape(grid.n, shard, wide)
    grad_wkv = jnp.concatenate([grad_wkv, small], axis=1).astype(BF)
    grad_wkv = grad_wkv.reshape(grid.n * (shard + 8), wide)
    by_y, by_x, gate_0, mz, grad_wkv, grad_normed_one = grid.close(
        by_y, by_x, gate_0, mz, grad_wkv, grad_normed_one
    )

    ax, ay = grid.fsdp_near(grad_attn, by_y, by_x)
    far_y, far_x = grid.fsdp_far(grad_wkv)
    (gate_1,) = grid.fence(gate_1)
    ax, ay = grid.over_x(ax), grid.over_y(ay)
    by_y, by_x, gate_1 = grid.over_y(far_y), grid.over_x(far_x), fold_z(gate_1)
    grad_inputs = grad_hidden_one + norm_back(grad_normed_one, rows_own, inv_own, gain_one)
    result = (hidden_one + mlp_own + mx.astype(F32) + mz.astype(F32)).astype(BF)
    ax, ay, by_y, by_x, gate_1, grad_tokens, result = grid.close(
        ax, ay, by_y, by_x, gate_1, grad_inputs.astype(BF), result
    )

    kx, ky = grid.fsdp_near(grad_wkv, by_y, by_x)
    (up_in,) = grid.fence(joined(up_0, up_1))
    kx, ky = grid.over_x(kx), grid.over_y(ky)
    grad_wup = grid.quarters_out(up_in)
    grad_tokens = both(grad_tokens)
    kx, ky, grad_wup = grid.close(kx, ky, grad_wup)

    (gate_in,) = grid.fence(joined(gate_0, gate_1))
    grad_wgate = grid.quarters_out(gate_in)
    grad_attn = grid.fsdp_end(grad_attn, ax, ay)
    grad_wkv = grid.fsdp_end(grad_wkv, kx, ky)
    grad_attn = jnp.pad(
        grad_attn.reshape(-1, shard, 2 * query_width), ((0, 0), (0, 8), (0, 0))
    )
    grad_attn = jnp.concatenate([grad_attn, grad_wkv.reshape(-1, shard + 8, wide)], axis=2)
    grad_attn = grid.scatter_context(grad_attn.reshape(-1, 2 * query_width + wide))
    result = both(result)
    small = grad_attn[shard : shard + 1, 2 * query_width :]
    grad_attn = grad_attn[:shard]
    grad_wdown, grad_wup, grad_wgate = [
        g.transpose(1, 0, 2).reshape(shard, 4 * quarter).astype(F32)
        for g in (grad_wdown, grad_wup, grad_wgate)
    ]
    grad_wkv = grad_attn[:, 2 * query_width :]
    return (
        result,
        grad_tokens,
        small[0, :shard],
        grad_attn[:, :query_width],
        small[:, start : start + bias_shard],
        grad_wkv[:, :head_width],
        small[:, start + bias_shard : start + bias_shard + small_bias],
        grad_wkv[:, head_width:],
        small[:, start + bias_shard + small_bias : start + bias_shard + 2 * small_bias],
        grad_attn[:, query_width : 2 * query_width].T,
        small[0, shard : 2 * shard],
        grad_wgate[:, :hidden],
        grad_wup[:, :hidden],
        grad_wdown[:, :hidden].T,
    )


def solution(mesh):
    rows = P(("fsdp", "context"), None)
    split = P(("fsdp", "context"))
    into = P(("fsdp", "context"), "tensor")
    back = P("tensor", ("fsdp", "context"))
    return jax.shard_map(
        on_device,
        mesh=mesh,
        in_specs=(
            rows,
            P("fsdp", None),
            split,
            into,
            back,
            into,
            back,
            into,
            back,
            back,
            split,
            into,
            into,
            back,
            rows,
        ),
        out_specs=(
            rows,
            rows,
            split,
            into,
            back,
            into,
            back,
            into,
            back,
            back,
            split,
            into,
            into,
            back,
        ),
        check_vma=False,
    )
```

```python
import functools

import jax
import jax.numpy as jnp
from jax import lax
from jax.experimental import pallas as pl
from jax.experimental.pallas import tpu as pltpu
from jax.sharding import PartitionSpec as P

EPSILON = 1e-06
ROPE_BASE = 1000000.0
MASKED = -1e30
LANES = 128
PARTS = 4
BOTH = ("fsdp", "context")
KERNEL_BYTES = 56 << 20
BF = jnp.bfloat16
F32 = jnp.float32


def tables(positions, head_width):
    ladder = jnp.arange(head_width // 2, dtype=F32)
    inverse = jnp.exp(-jnp.log(ROPE_BASE) * 2.0 * ladder / head_width)
    angles = positions.astype(F32)[:, None] * inverse[None, :]
    cosine, sine = jnp.cos(angles), jnp.sin(angles)
    return (
        jnp.concatenate([cosine, cosine], axis=1),
        jnp.concatenate([-sine, sine], axis=1),
    )


def swap_halves(x):
    middle = x.shape[1] // 2
    return jnp.concatenate([x[:, middle:], x[:, :middle]], axis=1)


def locate(blocks, prompt_slots, block_rows):
    segment = jnp.where(blocks < prompt_slots, 0, blocks - prompt_slots + 1)
    anchor = jnp.where(blocks < prompt_slots, blocks * block_rows, prompt_slots * block_rows)
    return (segment, anchor)


def dot_nn(left, right):
    return lax.dot_general(left, right, (((1,), (0,)), ((), ())), preferred_element_type=F32)


def dot_tn(left, right):
    return lax.dot_general(left, right, (((0,), (0,)), ((), ())), preferred_element_type=F32)


def dot_nt(left, right):
    return lax.dot_general(left, right, (((1,), (1,)), ((), ())), preferred_element_type=F32)


def norm_back(grad_normed, rows_normed, inv_rms, gain):
    grad_rows = grad_normed * gain.astype(F32)
    return inv_rms * (
        grad_rows - rows_normed * jnp.mean(grad_rows * rows_normed, axis=-1, keepdims=True)
    )


def turn(x, cosine, sine):
    return x * cosine + pltpu.roll(x, x.shape[1] // 2, 1) * sine


def attend_kernel(count, scale, seen, lin_ref, cos_ref, sin_ref, *refs):
    pairs = refs[:count]
    q_ref, out_ref, low_ref, lse_ref, peak_ref, total_ref, sum_ref = refs[count:]
    wide = lin_ref.shape[1]
    query = turn(lin_ref[...], cos_ref[...], sin_ref[...]).astype(BF)
    q_ref[...] = query

    def piece(r):
        scores = dot_nt(pairs[r][:, :wide], query) * scale
        if r == 0:
            rows = lax.broadcasted_iota(jnp.int32, scores.shape, 0)
            columns = lax.broadcasted_iota(jnp.int32, scores.shape, 1)
            scores = jnp.where(rows <= columns, scores, MASKED)
            peak = jnp.max(scores, axis=0, keepdims=True)
        else:
            old = peak_ref[...]
            peak = jnp.maximum(old, jnp.max(scores, axis=0, keepdims=True))
        probs = jnp.exp(scores - peak)
        total = jnp.sum(probs, axis=0, keepdims=True)
        mixed = dot_tn(pairs[r][:, wide:], probs.astype(BF))
        if r:
            shrink = jnp.exp(old - peak)
            total = total + total_ref[...] * shrink
            mixed = mixed + sum_ref[...] * shrink
        peak_ref[...] = peak
        total_ref[...] = total
        sum_ref[...] = mixed

    piece(0)
    for r in range(1, count):
        pl.when(seen[r] != 0)(functools.partial(piece, r))
    total = total_ref[...]
    out = jnp.transpose(sum_ref[...] / total)
    out_ref[...] = out
    low_ref[...] = out.astype(BF)
    lse_ref[...] = (peak_ref[...] + jnp.log(total))[None]


def attend(seen, lin, cosine, sine, pairs, heads, scale):
    rows, wide = cosine.shape
    count = len(pairs)
    every = pl.BlockSpec((rows, wide), lambda h, seen: (0, 0))
    head = pl.BlockSpec((rows, wide), lambda h, seen: (0, h))
    whole = pl.BlockSpec(pairs[0].shape, lambda h, seen: (0, 0))
    return pl.pallas_call(
        functools.partial(attend_kernel, count, scale),
        grid_spec=pltpu.PrefetchScalarGridSpec(
            num_scalar_prefetch=1,
            grid=(heads,),
            in_specs=[head, every, every] + [whole] * count,
            out_specs=[head, head, head, pl.BlockSpec((1, 1, rows), lambda h, seen: (h, 0, 0))],
            scratch_shapes=[
                pltpu.VMEM((1, rows), F32),
                pltpu.VMEM((1, rows), F32),
                pltpu.VMEM((wide, rows), F32),
            ],
        ),
        out_shape=[
            jax.ShapeDtypeStruct((rows, heads * wide), BF),
            jax.ShapeDtypeStruct((rows, heads * wide), F32),
            jax.ShapeDtypeStruct((rows, heads * wide), BF),
            jax.ShapeDtypeStruct((heads, 1, rows), F32),
        ],
        compiler_params=pltpu.CompilerParams(vmem_limit_bytes=KERNEL_BYTES),
        cost_estimate=pl.CostEstimate(flops=1, bytes_accessed=1, transcendentals=0),
    )(seen, lin, cosine, sine, *pairs)


def attend_back_kernel(
    count, scale, seen, q_ref, g_ref, out_ref, lse_ref, cos_ref, sin_ref, *refs
):
    pairs = refs[:count]
    dq_ref = refs[count]
    grads = refs[count + 1 : 2 * count + 1]
    held, sum_ref = refs[2 * count + 1 :]
    wide = q_ref.shape[1]
    step = pl.program_id(0)
    query = q_ref[...]
    grad = g_ref[...]
    delta = jnp.sum(grad.astype(F32) * out_ref[...], axis=1, keepdims=True)
    delta = jnp.transpose(jnp.broadcast_to(delta, q_ref.shape))[:1]
    lse = lse_ref[0]

    @pl.when(step == 0)
    def _():
        held[...] = jnp.zeros_like(held)

    def piece(r):
        key = pairs[r][:, :wide]
        probs = jnp.exp(dot_nt(key, query) * scale - lse)
        if r == 0:
            rows = lax.broadcasted_iota(jnp.int32, probs.shape, 0)
            columns = lax.broadcasted_iota(jnp.int32, probs.shape, 1)
            probs = jnp.where(rows <= columns, probs, 0.0)
        grad_scores = (probs * (dot_nt(pairs[r][:, wide:], grad) - delta)).astype(BF)
        held[r, :, wide:] += dot_nn(probs.astype(BF), grad)
        held[r, :, :wide] += dot_nn(grad_scores, query) * scale
        term = dot_tn(key, grad_scores)
        sum_ref[...] = term if r == 0 else sum_ref[...] + term

    piece(0)
    for r in range(1, count):
        pl.when(seen[r] != 0)(functools.partial(piece, r))
    grad_query = jnp.transpose(sum_ref[...]) * scale
    dq_ref[...] = turn(grad_query, cos_ref[...], -sin_ref[...]).astype(BF)

    @pl.when(step == pl.num_programs(0) - 1)
    def _():
        for r in range(count):
            grads[r][...] = held[r].astype(grads[r].dtype)


def attend_back(seen, queries, grads, outs, lse, cosine, sine, pairs, heads, scale):
    rows = queries.shape[0]
    wide = queries.shape[1] // heads
    count = len(pairs)
    head = pl.BlockSpec((rows, wide), lambda h, seen: (0, h))
    whole = pl.BlockSpec(pairs[0].shape, lambda h, seen: (0, 0))
    results = pl.pallas_call(
        functools.partial(attend_back_kernel, count, scale),
        grid_spec=pltpu.PrefetchScalarGridSpec(
            num_scalar_prefetch=1,
            grid=(heads,),
            in_specs=[head] * 3
            + [pl.BlockSpec((1, 1, rows), lambda h, seen: (h, 0, 0))]
            + [pl.BlockSpec((rows, wide), lambda h, seen: (0, 0))] * 2
            + [whole] * count,
            out_specs=[head] + [whole] * count,
            scratch_shapes=[
                pltpu.VMEM((count,) + pairs[0].shape, F32),
                pltpu.VMEM((wide, rows), F32),
            ],
        ),
        out_shape=[jax.ShapeDtypeStruct(queries.shape, BF)]
        + [jax.ShapeDtypeStruct(pairs[0].shape, F32 if r == 0 else BF) for r in range(count)],
        compiler_params=pltpu.CompilerParams(vmem_limit_bytes=KERNEL_BYTES),
        cost_estimate=pl.CostEstimate(flops=1, bytes_accessed=1, transcendentals=0),
    )(seen, queries, grads, outs, lse, cosine, sine, *pairs)
    return results[0], results[1:]


def products_kernel(a_ref, b_ref, c_ref, d_ref, out_ref):
    wide = b_ref.shape[1]
    out_ref[:, :wide] = dot_tn(a_ref[...], b_ref[...]).astype(BF)
    out_ref[:, wide:] = dot_tn(c_ref[...], d_ref[...]).astype(BF)


def products(a, b, c, d):
    tokens, depth = a.shape
    tile = depth // 3 if depth % (3 * LANES) == 0 else depth
    left = pl.BlockSpec((tokens, tile), lambda m: (0, m))
    right = pl.BlockSpec(b.shape, lambda m: (0, 0))
    return pl.pallas_call(
        products_kernel,
        grid=(depth // tile,),
        in_specs=[left, right, left, right],
        out_specs=pl.BlockSpec((tile, 2 * b.shape[1]), lambda m: (m, 0)),
        out_shape=jax.ShapeDtypeStruct((depth, 2 * b.shape[1]), BF),
        compiler_params=pltpu.CompilerParams(vmem_limit_bytes=KERNEL_BYTES),
        cost_estimate=pl.CostEstimate(flops=1, bytes_accessed=1, transcendentals=0),
    )(a, b, c, d)


def fetch(side, parts, held, sems):
    @pl.when(pl.program_id(0) == 0)
    def _():
        copies = []
        for k, dst in enumerate(held):
            for p in range(PARTS):
                src = parts[PARTS * k + p]
                rows = src.shape[0]
                high = side[0] if p < 2 else 1 - side[0]
                first = pl.multiple_of((2 * high + p % 2) * rows, rows)
                copies.append(
                    pltpu.make_async_copy(src, dst.at[pl.ds(first, rows)], sems.at[k, p])
                )
        for copy in copies:
            copy.start()
        for copy in copies:
            copy.wait()


def with_weights(body, grid, in_specs, weights, out_specs, out_shape):
    rows, units = weights[0][0].shape
    count = len(weights)
    first = 1 + len(in_specs)
    last = first + PARTS * count

    def kernel(*refs):
        held, sems = refs[-count - 1 : -1], refs[-1]
        fetch(refs[0], refs[first:last], held, sems)
        body(*refs[1:first], *held, *refs[last : -count - 1])

    return pl.pallas_call(
        kernel,
        grid=grid,
        in_specs=[pl.BlockSpec(memory_space=pltpu.SMEM)]
        + in_specs
        + [pl.BlockSpec(memory_space=pl.ANY)] * (PARTS * count),
        out_specs=out_specs,
        out_shape=out_shape,
        scratch_shapes=[pltpu.VMEM((PARTS * rows, units), BF)] * count
        + [pltpu.SemaphoreType.DMA((count, PARTS))],
        compiler_params=pltpu.CompilerParams(vmem_limit_bytes=KERNEL_BYTES),
        cost_estimate=pl.CostEstimate(flops=1, bytes_accessed=1, transcendentals=0),
    )


def hidden_kernel(n_ref, wg_ref, wu_ref, act_ref, by_gate_ref, by_up_ref):
    gate = dot_nn(n_ref[...], wg_ref[...])
    up = dot_nn(n_ref[...], wu_ref[...])
    sigmoid = jax.nn.sigmoid(gate)
    silu = gate * sigmoid
    act_ref[...] = (silu * up).astype(BF)
    by_gate_ref[...] = (up * (sigmoid + silu * (1.0 - sigmoid))).astype(BF)
    by_up_ref[...] = silu.astype(BF)


def hidden_units(side, normed, gate_w, up_w):
    tokens, depth = normed.shape
    units = gate_w[0].shape[1]
    tm = min(tokens, 256)
    rows = pl.BlockSpec((tm, depth), lambda m: (m, 0))
    out = pl.BlockSpec((tm, units), lambda m: (m, 0))
    shape = jax.ShapeDtypeStruct((tokens, units), BF)
    call = with_weights(
        hidden_kernel, (tokens // tm,), [rows], (gate_w, up_w), [out] * 3, [shape] * 3
    )
    return call(side, normed, *gate_w, *up_w)


def hidden_grad_kernel(d_ref, by_gate_ref, by_up_ref, wd_ref, dg_ref, du_ref):
    grad = dot_nn(d_ref[...], wd_ref[...])
    dg_ref[...] = (grad * by_gate_ref[...].astype(F32)).astype(BF)
    du_ref[...] = (grad * by_up_ref[...].astype(F32)).astype(BF)


def hidden_grads(side, grads, down_w, by_gate, by_up):
    tokens, depth = grads.shape
    units = down_w[0].shape[1]
    tm = min(tokens, 256)
    rows = pl.BlockSpec((tm, depth), lambda m: (m, 0))
    out = pl.BlockSpec((tm, units), lambda m: (m, 0))
    shape = jax.ShapeDtypeStruct((tokens, units), BF)
    call = with_weights(
        hidden_grad_kernel, (tokens // tm,), [rows, out, out], (down_w,), [out] * 2, [shape] * 2
    )
    return call(side, grads, by_gate, by_up, *down_w)


def back_kernel(count, half, *refs):
    lefts, rights = refs[:count], refs[count : 2 * count]
    first, second = refs[2 * count :]
    total = dot_nt(lefts[0][...], rights[0][...])
    for left, right in zip(lefts[1:], rights[1:]):
        total = total + dot_nt(left[...], right[...])
    step = pl.program_id(0)

    @pl.when(step < half)
    def _():
        first[...] = total.astype(BF)

    @pl.when(step >= half)
    def _():
        second[...] = total.astype(BF)


def hidden_back(side, lefts, rights):
    tokens, units = lefts[0].shape
    depth = PARTS * rights[0][0].shape[0]
    count = len(lefts)
    tm = min(tokens // 2, 512)
    half = tokens // 2 // tm
    rows = pl.BlockSpec((tm, units), lambda m: (m, 0))
    out_specs = [
        pl.BlockSpec((tm, depth), lambda m: (jnp.minimum(m, half - 1), 0)),
        pl.BlockSpec((tm, depth), lambda m: (jnp.maximum(m - half, 0), 0)),
    ]
    call = with_weights(
        functools.partial(back_kernel, count, half),
        (tokens // tm,),
        [rows] * count,
        rights,
        out_specs,
        [jax.ShapeDtypeStruct((tokens // 2, depth), BF)] * 2,
    )
    return call(side, *lefts, *[x for w in rights for x in w])


def after(x, *earlier):
    return lax.optimization_barrier((x,) + earlier)[0]


class Pending:
    def __init__(self, got, finish):
        self.got = got
        self.finish = finish


class Grid:
    def __init__(self):
        self.nf = lax.axis_size("fsdp")
        self.nc = lax.axis_size("context")
        self.n = self.nf * self.nc
        self.cbits = self.nc.bit_length() - 1
        self.fbits = self.nf.bit_length() - 1
        self.me = lax.axis_index("fsdp") * self.nc + lax.axis_index("context")
        self.my_slot = lax.axis_index("context")
        self.core = lax.axis_index("tensor")
        self.done = ()
        self.zm = 1
        self.xm = self.nc
        self.deep = list(range(1, self.cbits)) + list(range(self.cbits + 1, self.cbits + self.fbits))

    def bit(self, b):
        return (self.me >> b) & 1

    def fence(self, *xs):
        return lax.optimization_barrier(xs + self.done)[: len(xs)]

    def close(self, *xs):
        raw = lax.optimization_barrier(
            tuple(x.got if isinstance(x, Pending) else x for x in xs)
        )
        self.done = raw
        outs = [x.finish(r) if isinstance(x, Pending) else r for x, r in zip(xs, raw)]
        return outs[0] if len(outs) == 1 else outs

    def one(self, x, mask, pin=()):
        if pin:
            x = after(x, *pin)
        return lax.ppermute(x, BOTH, [(i, i ^ mask) for i in range(self.n)])

    def swap(self, x):
        return lax.ppermute(x, "tensor", [(0, 1), (1, 0)])

    def pair(self, b, mine, theirs, axis):
        low = self.bit(b) == 0
        return jnp.stack([jnp.where(low, mine, theirs), jnp.where(low, theirs, mine)], axis)

    def ordered(self, pieces, bits):
        if len(bits) == 0:
            return pieces[0]
        half = len(pieces) // 2
        low = self.ordered(pieces[:half], bits[:-1])
        high = self.ordered(pieces[half:], bits[:-1])
        return self.pair(bits[-1], low, high, 0)

    def fsdp_take(self, x, r):
        x = x.reshape(self.nf, -1, x.shape[1])
        return lax.dynamic_index_in_dim(x, lax.axis_index("fsdp") ^ r, 0, keepdims=False)

    def fsdp_far(self, x):
        far = self.fsdp_take(x, 3)
        cut = far.shape[0] // 2
        return far[:cut], far[cut:]

    def fsdp_near(self, x, by_y, by_x):
        px, py = self.fsdp_take(x, 1), self.fsdp_take(x, 2)
        cut = px.shape[0] // 2
        px = jnp.concatenate([px[:cut].astype(F32) + by_y.astype(F32), px[cut:].astype(F32)], 0)
        py = jnp.concatenate([py[:cut].astype(F32), py[cut:].astype(F32) + by_x.astype(F32)], 0)
        return px.astype(BF), py.astype(BF)

    def fsdp_end(self, x, rx, ry):
        return (self.fsdp_take(x, 0).astype(F32) + rx.astype(F32) + ry.astype(F32)).astype(BF)

    def over_x(self, x):
        return self.one(x, self.xm)

    def over_y(self, x):
        return self.one(x, 2 * self.xm)

    def over_z(self, x):
        return self.one(x, self.zm)

    def context_pick(self, x, r):
        x = x.reshape(self.nc, -1, x.shape[1])
        return lax.dynamic_index_in_dim(x, self.my_slot ^ r, 0, keepdims=False)

    def tokens_near(self, x, pin_x=(), pin_z=()):
        return self.one(x, self.xm, pin_x), self.one(x, self.zm, pin_z)

    def tokens_far(self, nears):
        cut = nears[0][0].shape[0] // 2
        by_z = self.one(jnp.concatenate([px[:cut] for px, _ in nears], 0), self.zm)
        by_x = self.one(jnp.concatenate([pz[cut:] for _, pz in nears], 0), self.xm)
        parts = []
        for k, (px, pz) in enumerate(nears):
            here = slice(k * cut, (k + 1) * cut)
            parts.append(jnp.concatenate([px, pz, by_z[here], by_x[here]], 0))
        return parts

    def tokens_split(self, part, other):
        rows = part.shape[0] // 4
        cut = rows // 2
        here = [slice(k * rows, (k + 1) * rows) for k in range(4)]
        own, px, pz, far = [part[k].astype(F32) + other[k].astype(F32) for k in here]
        return own, px, pz, far[:cut].astype(BF), far[cut:].astype(BF)

    def tokens_add(self, px, pz, by_z, by_x):
        cut = by_z.shape[0]
        px = jnp.concatenate([px[:cut] + by_z.astype(F32), px[cut:]], 0).astype(BF)
        pz = jnp.concatenate([pz[:cut], pz[cut:] + by_x.astype(F32)], 0).astype(BF)
        return px, pz

    def quarter_masks(self):
        return (0, self.zm, self.xm, self.xm + self.zm)

    def my_quarter(self):
        return 2 * self.bit(self.cbits) + self.bit(0)

    def quarter_groups(self):
        masks = (0, self.zm, self.xm, self.xm + self.zm)
        return [[i | m for m in masks] for i in range(self.n) if i & masks[3] == 0]

    def quarters_in(self, w):
        return lax.all_to_all(w, BOTH, 0, 0, axis_index_groups=self.quarter_groups())

    def quarters_out(self, g):
        return lax.all_to_all(g, BOTH, 0, 0, axis_index_groups=self.quarter_groups())

    def deepen(self, w, held, bits):
        for b in bits[:-1]:
            w = self.pair(b, w, self.one(w, 1 << b), sum(1 for h in held if h > b))
            held.append(b)
        b = bits[-1]
        axis = sum(1 for h in held if h > b)
        held.append(b)
        return Pending(self.one(w, 1 << b), lambda got: self.pair(b, w, got, axis))

    def fold(self, g, held, bits):
        def step(g, b):
            axis = held.index(b)
            held.remove(b)
            give = lax.dynamic_index_in_dim(g, 1 - self.bit(b), axis, keepdims=False)
            keep = lax.dynamic_index_in_dim(g, self.bit(b), axis, keepdims=False)
            finish = lambda got: (keep.astype(F32) + got.astype(F32)).astype(BF)
            return Pending(self.one(give, 1 << b), finish)

        for b in bits[:-1]:
            pending = step(g, b)
            g = pending.finish(pending.got)
        return step(g, bits[-1])


def on_device(
    tokens,
    block_order,
    norm_one,
    w_query,
    b_query,
    w_key,
    b_key,
    w_value,
    b_value,
    w_out,
    norm_two,
    w_gate,
    w_up,
    w_down,
    cotangent,
):
    grid = Grid()
    block_rows, width = tokens.shape
    shard = norm_one.shape[0]
    slot_count = grid.nc
    prompt_slots = slot_count // 2
    head_width = w_key.shape[1]
    query_width = w_query.shape[1]
    head_group = query_width // head_width
    score_scale = head_width ** (-0.5)
    cores = lax.axis_size("tensor")
    own_rows = block_rows // cores
    owners = block_order[0]
    my_block = lax.dynamic_index_in_dim(owners, grid.my_slot, 0, keepdims=False)
    query_anchor = locate(my_block, prompt_slots, block_rows)[1]
    query_pos = query_anchor + jnp.arange(block_rows)

    def own(x):
        return lax.dynamic_slice(x, (grid.core * own_rows, 0), (own_rows, x.shape[1]))

    def others(x):
        return lax.dynamic_slice(x, ((1 - grid.core) * own_rows, 0), (own_rows, x.shape[1]))

    def both(x):
        other = grid.swap(x)
        first = grid.core == 0
        return jnp.concatenate([jnp.where(first, x, other), jnp.where(first, other, x)], 0)

    def summed(part):
        give = lax.dynamic_slice(part, ((1 - grid.core) * own_rows, 0), (own_rows, width))
        return own(part) + grid.swap(give.astype(BF)).astype(F32)

    bias_shard = b_query.shape[1]
    small_bias = b_key.shape[1]
    vector = jnp.concatenate([norm_one[None], norm_two[None], b_query, b_key, b_value], axis=1)
    columns = query_width + 2 * head_width
    vector = jnp.pad(vector, ((0, 7), (0, columns - vector.shape[1])))
    packed = jnp.concatenate(
        [jnp.concatenate([w_query, w_key, w_value], axis=1), vector], axis=0
    )
    hidden = w_gate.shape[1]
    quarter = -(-hidden // (4 * LANES)) * LANES
    pad = ((0, 0), (0, 4 * quarter - hidden))
    w_out_t = lax.all_gather(w_out.T, BOTH, axis=0, tiled=True)

    context_deep = [b for b in grid.deep if b < grid.cbits]
    fsdp_deep = [b for b in grid.deep if b > grid.cbits]

    def quarters(w):
        return w.reshape(shard, 4, quarter).transpose(1, 0, 2)

    def deep_z(w):
        return grid.deepen(w, [0], context_deep)

    def give_y(w):
        return grid.one(w, 1 << fsdp_deep[0])

    def parts_of(*pieces):
        return tuple(x.reshape(grid.n // PARTS * shard, quarter) for x in pieces)

    side = grid.bit(fsdp_deep[0]).reshape(1)
    held = []
    gate_near = grid.quarters_in(quarters(jnp.pad(w_gate, pad)))
    packed = grid.deepen(packed, held, context_deep[::-1])
    gate_near, packed = grid.close(gate_near, packed)

    gate_near = gate_near.reshape(2, 2, shard, quarter)
    packed = grid.close(grid.deepen(packed, held, [0]))

    packed = packed.reshape(grid.nc * (shard + 8), columns)
    (gate_0,) = grid.fence(gate_near[0])
    gx, gy, gate_0 = grid.close(grid.over_x(packed), grid.over_y(packed), deep_z(gate_0))

    cut = gx.shape[0] // 2
    gate_1, up_in = grid.fence(gate_near[1], quarters(jnp.pad(w_up, pad)))
    by_y, by_x = grid.over_y(gx[:cut]), grid.over_x(gy[cut:])
    by_y, by_x, gate_1, up_near = grid.close(
        by_y, by_x, deep_z(gate_1), grid.quarters_in(up_in)
    )

    up_near = up_near.reshape(2, 2, shard, quarter)
    pieces = [packed, gx, gy, jnp.concatenate([by_y, by_x], 0)]
    pieces = [x.reshape(grid.nc, shard + 8, columns) for x in pieces]
    sources = [grid.cbits, grid.cbits + 1]
    w_qkv = grid.ordered([x[:, :shard] for x in pieces], sources)
    w_qkv = w_qkv.reshape(grid.n * shard, columns)
    vectors = grid.ordered([x[:, shard] for x in pieces], sources).reshape(grid.n, columns)
    gain_one = vectors[:, :shard].reshape(-1)
    gain_two = vectors[:, shard : 2 * shard].reshape(-1)
    start = 2 * shard
    bias = jnp.concatenate(
        [
            vectors[:, start : start + bias_shard].reshape(-1),
            vectors[:, start + bias_shard : start + bias_shard + small_bias].reshape(-1),
            vectors[
                :, start + bias_shard + small_bias : start + bias_shard + 2 * small_bias
            ].reshape(-1),
        ]
    ).astype(F32)

    inputs = tokens.astype(F32)
    inv_one = lax.rsqrt(jnp.mean(inputs * inputs, axis=-1, keepdims=True) + EPSILON)
    rows_one = inputs * inv_one
    normed_one = (rows_one * gain_one.astype(F32)).astype(BF)
    cosine, sine = tables(query_pos, head_width)
    grads_own, grads_other = own(cotangent), others(cotangent)
    gate_0, grads_pz = grid.fence(gate_0, grads_own)
    gate_2, grads_pz = give_y(gate_0), grid.over_z(grads_pz)
    qkv = dot_nn(normed_one, w_qkv) + bias
    keys = qkv[:, query_width : query_width + head_width]
    keys = keys * cosine + swap_halves(keys) * sine
    pair = jnp.concatenate([keys, qkv[:, query_width + head_width :]], axis=1).astype(BF)
    pair, qkv, gate_2, grads_pz = grid.close(pair, qkv, gate_2, grads_pz)

    gate_1, grads_px = grid.fence(gate_1, grads_own)
    met = [grid.one(pair, r) for r in range(1, slot_count)]
    gate_3, grads_px, *met = grid.close(give_y(gate_1), grid.over_x(grads_px), *met)
    pairs = [pair] + met

    piece_block = owners[grid.my_slot ^ jnp.arange(slot_count)]
    seen = ((piece_block < prompt_slots) & (piece_block < my_block)).astype(jnp.int32)
    up_0, down_in = grid.fence(up_near[0], quarters(jnp.pad(w_down.T, pad)))
    up_0, down_near = deep_z(up_0), grid.quarters_in(down_in)
    queries, attn_heads, out_low, log_total = attend(
        seen, qkv, cosine, sine, pairs, head_group, score_scale
    )
    out_low, up_0, down_near = grid.close(out_low, up_0, down_near)

    down_near = down_near.reshape(2, 2, shard, quarter)
    hidden_one = own(tokens).astype(F32) + summed(dot_nt(out_low, w_out_t))

    inv_two = lax.rsqrt(jnp.mean(hidden_one * hidden_one, axis=-1, keepdims=True) + EPSILON)
    rows_two = hidden_one * inv_two
    normed_two = (rows_two * gain_two.astype(F32)).astype(BF)
    normed_two = grid.close(normed_two)

    up_0, up_1 = grid.fence(up_0, up_near[1])
    px, pz, normed_other, up_1, up_2 = grid.close(
        grid.over_x(normed_two),
        grid.over_z(normed_two),
        grid.swap(normed_two),
        deep_z(up_1),
        give_y(up_0),
    )

    cut = px.shape[0] // 2
    (down_0,) = grid.fence(down_near[0])
    normed_near = jnp.concatenate([px, pz], 0)
    by_z, by_x, up_3, down_0, normed_swap = grid.close(
        grid.over_z(px[:cut]),
        grid.over_x(pz[cut:]),
        give_y(up_1),
        deep_z(down_0),
        grid.swap(normed_near),
    )

    normed_far = jnp.concatenate([by_z, by_x], 0)
    gate_full = parts_of(gate_0, gate_1, gate_2, gate_3)
    up_full = parts_of(up_0, up_1, up_2, up_3)
    far_swap, grads_swap = grid.close(
        grid.swap(normed_far), grid.swap(jnp.concatenate([grads_px, grads_pz], 0))
    )

    normed_in = jnp.concatenate(
        [normed_two, normed_near, normed_far, normed_other, normed_swap, far_swap], 0
    )
    far_z, far_x, down_0, down_1 = grid.fence(
        grads_px[:cut], grads_pz[cut:], down_0, down_near[1]
    )
    by_z, by_x = grid.over_z(far_z), grid.over_x(far_x)
    down_2, down_1 = give_y(down_0), deep_z(down_1)
    act, by_gate, by_up = hidden_units(side, normed_in, gate_full, up_full)
    act, by_z, by_x, down_2, down_1 = grid.close(act, by_z, by_x, down_2, down_1)

    grads_far = jnp.concatenate([by_z, by_x], 0)
    down_3 = give_y(down_1)
    grads_in = jnp.concatenate(
        [grads_own, grads_px, grads_pz, grads_far, grads_other, grads_swap, grid.swap(grads_far)],
        0,
    )
    grad_wdown = dot_tn(grads_in, act).astype(BF)
    grad_wdown, down_3 = grid.close(grad_wdown, down_3)
    down_full = parts_of(down_0, down_1, down_2, down_3)

    top = sorted(range(grid.cbits + grid.fbits), reverse=True)
    shape = (2,) * len(top) + (shard, quarter)
    y_back, z_back = fsdp_deep[::-1], context_deep[::-1]

    def half(grad, h):
        return lax.index_in_dim(grad.reshape(shape), h, top.index(grid.cbits), keepdims=False)

    def fold_y(grad):
        return grid.fold(grad, [b for b in top if b != grid.cbits], y_back)

    def fold_z(grad):
        return grid.fold(grad, [b for b in top if b not in fsdp_deep and b != grid.cbits], z_back)

    def joined(first, second):
        return jnp.stack([first, second], 0).reshape(4, shard, quarter)

    down_0 = fold_y(half(grad_wdown, 0))
    grad_gate, grad_up = hidden_grads(side, grads_in, down_full, by_gate, by_up)
    down_0, grad_gate, grad_up = grid.close(down_0, grad_gate, grad_up)

    (down_1,) = grid.fence(half(grad_wdown, 1))
    down_0, down_1 = fold_z(down_0), fold_y(down_1)
    part, give = hidden_back(side, (grad_gate, grad_up), (gate_full, up_full))
    down_0, down_1, part, give = grid.close(down_0, down_1, part, give)

    other = grid.swap(give)
    (up_in,) = grid.fence(grad_up)
    grad_wup = dot_tn(normed_in, up_in).astype(BF)
    other, grad_wup = grid.close(other, grad_wup)

    part_own, px, pz, far_z, far_x = grid.tokens_split(part, other)
    down_1, gate_in = grid.fence(down_1, grad_gate)
    by_z, by_x = grid.over_z(far_z), grid.over_x(far_x)
    down_1, up_0 = fold_z(down_1), fold_y(half(grad_wup, 0))
    grad_wgate = dot_tn(normed_in, gate_in).astype(BF)
    by_z, by_x, down_1, up_0, grad_wgate = grid.close(by_z, by_x, down_1, up_0, grad_wgate)

    px, pz = grid.tokens_add(px, pz, by_z, by_x)
    up_1, act_in = grid.fence(half(grad_wup, 1), act)
    px, pz = grid.over_x(px), grid.over_z(pz)
    up_0, up_1 = fold_z(up_0), fold_y(up_1)
    mlp_part, mlp_give = hidden_back(side, (act_in,), (down_full,))
    px, pz, up_0, up_1, mlp_part, mlp_give = grid.close(
        px, pz, up_0, up_1, mlp_part, mlp_give
    )

    (down_in,) = grid.fence(joined(down_0, down_1))
    grad_wdown = grid.quarters_out(down_in)
    mlp_other = grid.swap(mlp_give)
    grad_normed_two = part_own + px.astype(F32) + pz.astype(F32)
    grad_gain_two = jnp.sum(grad_normed_two * rows_two, axis=0)
    grad_hidden_one = own(cotangent).astype(F32) + norm_back(
        grad_normed_two, rows_two, inv_two, gain_two
    )
    grad_low = both(grad_hidden_one.astype(BF))
    grad_heads = dot_nn(grad_low, w_out_t).astype(BF)
    grad_heads, mlp_other, grad_wdown = grid.close(grad_heads, mlp_other, grad_wdown)

    mlp_own, mx, mz, far_z, far_x = grid.tokens_split(mlp_part, mlp_other)
    gate_0, up_1 = grid.fence(half(grad_wgate, 0), up_1)
    by_z, by_x = grid.over_z(far_z), grid.over_x(far_x)
    gate_0, up_1 = fold_y(gate_0), fold_z(up_1)
    grad_query, grad_pairs = attend_back(
        seen,
        queries,
        grad_heads,
        attn_heads,
        log_total,
        cosine,
        sine,
        pairs,
        head_group,
        score_scale,
    )
    by_z, by_x, gate_0, up_1, grad_query, *grad_pairs = grid.close(
        by_z, by_x, gate_0, up_1, grad_query, *grad_pairs
    )

    grad_got = [grid.one(x, r + 1) for r, x in enumerate(grad_pairs[1:])]
    mx, mz = grid.tokens_add(mx, mz, by_z, by_x)
    (gate_1,) = grid.fence(half(grad_wgate, 1))
    mx, gate_1 = grid.over_x(mx), fold_y(gate_1)
    grad_attn = products(normed_one, grad_query, grad_low, out_low)
    mx, gate_1, grad_attn, *grad_got = grid.close(mx, gate_1, grad_attn, *grad_got)

    far_y, far_x = grid.fsdp_far(grad_attn)
    mz, grad_query = grid.fence(mz, grad_query)
    by_y, by_x = grid.over_y(far_y), grid.over_x(far_x)
    gate_0, mz = fold_z(gate_0), grid.over_z(mz)
    grad_pair = grad_pairs[0]
    for x in grad_got:
        grad_pair = grad_pair + x.astype(F32)
    grad_keys = grad_pair[:, :head_width]
    grad_keys = grad_keys * cosine - swap_halves(grad_keys) * sine
    grad_kv = jnp.concatenate([grad_keys, grad_pair[:, head_width:]], axis=1).astype(BF)
    grad_qkv = jnp.concatenate([grad_query, grad_kv], axis=1)
    grad_bias = jnp.sum(grad_qkv.astype(F32), axis=0)
    grad_normed_one = summed(dot_nt(grad_qkv, w_qkv))
    rows_own = own(rows_one)
    inv_own = own(inv_one)
    grad_gain_one = jnp.sum(grad_normed_one * rows_own, axis=0)
    gains = jnp.concatenate(
        [grad_gain_one.reshape(-1, shard), grad_gain_two.reshape(-1, shard)], axis=1
    )
    gains = gains + grid.swap(gains)
    small = jnp.concatenate(
        [
            gains,
            grad_bias[:query_width].reshape(-1, bias_shard),
            grad_bias[query_width : query_width + head_width].reshape(-1, small_bias),
            grad_bias[query_width + head_width :].reshape(-1, small_bias),
        ],
        axis=1,
    )
    wide = 2 * head_width
    small = jnp.pad(small[:, None], ((0, 0), (0, 7), (0, max(wide - small.shape[1], 0))))
    grad_wkv = dot_tn(normed_one, grad_kv).reshape(grid.n, shard, wide)
    grad_wkv = jnp.concatenate([grad_wkv, small], axis=1).astype(BF)
    grad_wkv = grad_wkv.reshape(grid.n * (shard + 8), wide)
    by_y, by_x, gate_0, mz, grad_wkv, grad_normed_one = grid.close(
        by_y, by_x, gate_0, mz, grad_wkv, grad_normed_one
    )

    ax, ay = grid.fsdp_near(grad_attn, by_y, by_x)
    far_y, far_x = grid.fsdp_far(grad_wkv)
    (gate_1,) = grid.fence(gate_1)
    ax, ay = grid.over_x(ax), grid.over_y(ay)
    by_y, by_x, gate_1 = grid.over_y(far_y), grid.over_x(far_x), fold_z(gate_1)
    grad_inputs = grad_hidden_one + norm_back(grad_normed_one, rows_own, inv_own, gain_one)
    result = (hidden_one + mlp_own + mx.astype(F32) + mz.astype(F32)).astype(BF)
    ax, ay, by_y, by_x, gate_1, grad_tokens, result = grid.close(
        ax, ay, by_y, by_x, gate_1, grad_inputs.astype(BF), result
    )

    grad_attn = grid.fsdp_end(grad_attn, ax, ay)
    kx, ky = grid.fsdp_near(grad_wkv, by_y, by_x)
    (up_in,) = grid.fence(joined(up_0, up_1))
    kx, ky = grid.over_x(kx), grid.over_y(ky)
    parts = [grid.one(grid.context_pick(grad_attn, r), r) for r in range(1, grid.nc)]
    grad_wup = grid.quarters_out(up_in)
    grad_tokens, result = both(grad_tokens), both(result)
    kx, ky, grad_wup, grad_tokens, result, *parts = grid.close(
        kx, ky, grad_wup, grad_tokens, result, *parts
    )

    (gate_in,) = grid.fence(joined(gate_0, gate_1))
    grad_wgate = grid.quarters_out(gate_in)
    grad_wkv = grid.fsdp_end(grad_wkv, kx, ky)
    terms = [grid.one(grid.context_pick(grad_wkv, r), r) for r in range(1, grid.nc)]
    grad_attn = grid.context_pick(grad_attn, 0).astype(F32)
    for x in parts:
        grad_attn = grad_attn + x.astype(F32)
    grad_wkv = grid.context_pick(grad_wkv, 0).astype(F32)
    for x in terms:
        grad_wkv = grad_wkv + x.astype(F32)
    small = grad_wkv[shard : shard + 1]
    grad_wkv = grad_wkv[:shard]
    grad_wdown, grad_wup, grad_wgate = [
        g.transpose(1, 0, 2).reshape(shard, 4 * quarter).astype(F32)
        for g in (grad_wdown, grad_wup, grad_wgate)
    ]
    return (
        result,
        grad_tokens,
        small[0, :shard],
        grad_attn[:, :query_width],
        small[:, start : start + bias_shard],
        grad_wkv[:, :head_width],
        small[:, start + bias_shard : start + bias_shard + small_bias],
        grad_wkv[:, head_width:],
        small[:, start + bias_shard + small_bias : start + bias_shard + 2 * small_bias],
        grad_attn[:, query_width : 2 * query_width].T,
        small[0, shard : 2 * shard],
        grad_wgate[:, :hidden],
        grad_wup[:, :hidden],
        grad_wdown[:, :hidden].T,
    )


def solution(mesh):
    rows = P(("fsdp", "context"), None)
    split = P(("fsdp", "context"))
    into = P(("fsdp", "context"), "tensor")
    back = P("tensor", ("fsdp", "context"))
    return jax.shard_map(
        on_device,
        mesh=mesh,
        in_specs=(
            rows,
            P("fsdp", None),
            split,
            into,
            back,
            into,
            back,
            into,
            back,
            back,
            split,
            into,
            into,
            back,
            rows,
        ),
        out_specs=(
            rows,
            rows,
            split,
            into,
            back,
            into,
            back,
            into,
            back,
            back,
            split,
            into,
            into,
            back,
        ),
        check_vma=False,
    )
```

```python
import functools

import jax
import jax.numpy as jnp
from jax import lax
from jax.experimental import pallas as pl
from jax.experimental.pallas import tpu as pltpu
from jax.sharding import PartitionSpec as P

EPSILON = 1e-06
ROPE_BASE = 1000000.0
MASKED = -1e30
LANES = 128
PARTS = 4
BOTH = ("fsdp", "context")
KERNEL_BYTES = 56 << 20
BF = jnp.bfloat16
F32 = jnp.float32


def tables(positions, head_width):
    ladder = jnp.arange(head_width // 2, dtype=F32)
    inverse = jnp.exp(-jnp.log(ROPE_BASE) * 2.0 * ladder / head_width)
    angles = positions.astype(F32)[:, None] * inverse[None, :]
    cosine, sine = jnp.cos(angles), jnp.sin(angles)
    return (
        jnp.concatenate([cosine, cosine], axis=1),
        jnp.concatenate([-sine, sine], axis=1),
    )


def swap_halves(x):
    middle = x.shape[1] // 2
    return jnp.concatenate([x[:, middle:], x[:, :middle]], axis=1)


def locate(blocks, prompt_slots, block_rows):
    segment = jnp.where(blocks < prompt_slots, 0, blocks - prompt_slots + 1)
    anchor = jnp.where(blocks < prompt_slots, blocks * block_rows, prompt_slots * block_rows)
    return (segment, anchor)


def dot_nn(left, right):
    return lax.dot_general(left, right, (((1,), (0,)), ((), ())), preferred_element_type=F32)


def dot_tn(left, right):
    return lax.dot_general(left, right, (((0,), (0,)), ((), ())), preferred_element_type=F32)


def dot_nt(left, right):
    return lax.dot_general(left, right, (((1,), (1,)), ((), ())), preferred_element_type=F32)


def norm_back(grad_normed, rows_normed, inv_rms, gain):
    grad_rows = grad_normed * gain.astype(F32)
    return inv_rms * (
        grad_rows - rows_normed * jnp.mean(grad_rows * rows_normed, axis=-1, keepdims=True)
    )


def turn(x, cosine, sine):
    return x * cosine + pltpu.roll(x, x.shape[1] // 2, 1) * sine


def attend_kernel(count, scale, seen, lin_ref, cos_ref, sin_ref, *refs):
    pairs = refs[:count]
    q_ref, out_ref, low_ref, lse_ref, peak_ref, total_ref, sum_ref = refs[count:]
    wide = lin_ref.shape[1]
    query = turn(lin_ref[...], cos_ref[...], sin_ref[...]).astype(BF)
    q_ref[...] = query

    def piece(r):
        scores = dot_nt(pairs[r][:, :wide], query) * scale
        if r == 0:
            rows = lax.broadcasted_iota(jnp.int32, scores.shape, 0)
            columns = lax.broadcasted_iota(jnp.int32, scores.shape, 1)
            scores = jnp.where(rows <= columns, scores, MASKED)
            peak = jnp.max(scores, axis=0, keepdims=True)
        else:
            old = peak_ref[...]
            peak = jnp.maximum(old, jnp.max(scores, axis=0, keepdims=True))
        probs = jnp.exp(scores - peak)
        total = jnp.sum(probs, axis=0, keepdims=True)
        mixed = dot_tn(pairs[r][:, wide:], probs.astype(BF))
        if r:
            shrink = jnp.exp(old - peak)
            total = total + total_ref[...] * shrink
            mixed = mixed + sum_ref[...] * shrink
        peak_ref[...] = peak
        total_ref[...] = total
        sum_ref[...] = mixed

    piece(0)
    for r in range(1, count):
        pl.when(seen[r] != 0)(functools.partial(piece, r))
    total = total_ref[...]
    out = jnp.transpose(sum_ref[...] / total)
    out_ref[...] = out
    low_ref[...] = out.astype(BF)
    lse_ref[...] = (peak_ref[...] + jnp.log(total))[None]


def attend(seen, lin, cosine, sine, pairs, heads, scale):
    rows, wide = cosine.shape
    count = len(pairs)
    every = pl.BlockSpec((rows, wide), lambda h, seen: (0, 0))
    head = pl.BlockSpec((rows, wide), lambda h, seen: (0, h))
    whole = pl.BlockSpec(pairs[0].shape, lambda h, seen: (0, 0))
    return pl.pallas_call(
        functools.partial(attend_kernel, count, scale),
        grid_spec=pltpu.PrefetchScalarGridSpec(
            num_scalar_prefetch=1,
            grid=(heads,),
            in_specs=[head, every, every] + [whole] * count,
            out_specs=[head, head, head, pl.BlockSpec((1, 1, rows), lambda h, seen: (h, 0, 0))],
            scratch_shapes=[
                pltpu.VMEM((1, rows), F32),
                pltpu.VMEM((1, rows), F32),
                pltpu.VMEM((wide, rows), F32),
            ],
        ),
        out_shape=[
            jax.ShapeDtypeStruct((rows, heads * wide), BF),
            jax.ShapeDtypeStruct((rows, heads * wide), F32),
            jax.ShapeDtypeStruct((rows, heads * wide), BF),
            jax.ShapeDtypeStruct((heads, 1, rows), F32),
        ],
        compiler_params=pltpu.CompilerParams(vmem_limit_bytes=KERNEL_BYTES),
        cost_estimate=pl.CostEstimate(flops=1, bytes_accessed=1, transcendentals=0),
    )(seen, lin, cosine, sine, *pairs)


def attend_back_kernel(
    count, scale, seen, q_ref, g_ref, out_ref, lse_ref, cos_ref, sin_ref, *refs
):
    pairs = refs[:count]
    dq_ref = refs[count]
    grads = refs[count + 1 : 2 * count + 1]
    held, sum_ref = refs[2 * count + 1 :]
    wide = q_ref.shape[1]
    step = pl.program_id(0)
    query = q_ref[...]
    grad = g_ref[...]
    delta = jnp.sum(grad.astype(F32) * out_ref[...], axis=1, keepdims=True)
    delta = jnp.transpose(jnp.broadcast_to(delta, q_ref.shape))[:1]
    lse = lse_ref[0]

    @pl.when(step == 0)
    def _():
        held[...] = jnp.zeros_like(held)

    def piece(r):
        key = pairs[r][:, :wide]
        probs = jnp.exp(dot_nt(key, query) * scale - lse)
        if r == 0:
            rows = lax.broadcasted_iota(jnp.int32, probs.shape, 0)
            columns = lax.broadcasted_iota(jnp.int32, probs.shape, 1)
            probs = jnp.where(rows <= columns, probs, 0.0)
        grad_scores = (probs * (dot_nt(pairs[r][:, wide:], grad) - delta)).astype(BF)
        held[r, :, wide:] += dot_nn(probs.astype(BF), grad)
        held[r, :, :wide] += dot_nn(grad_scores, query) * scale
        term = dot_tn(key, grad_scores)
        sum_ref[...] = term if r == 0 else sum_ref[...] + term

    piece(0)
    for r in range(1, count):
        pl.when(seen[r] != 0)(functools.partial(piece, r))
    grad_query = jnp.transpose(sum_ref[...]) * scale
    dq_ref[...] = turn(grad_query, cos_ref[...], -sin_ref[...]).astype(BF)

    @pl.when(step == pl.num_programs(0) - 1)
    def _():
        for r in range(count):
            grads[r][...] = held[r].astype(grads[r].dtype)


def attend_back(seen, queries, grads, outs, lse, cosine, sine, pairs, heads, scale):
    rows = queries.shape[0]
    wide = queries.shape[1] // heads
    count = len(pairs)
    head = pl.BlockSpec((rows, wide), lambda h, seen: (0, h))
    whole = pl.BlockSpec(pairs[0].shape, lambda h, seen: (0, 0))
    results = pl.pallas_call(
        functools.partial(attend_back_kernel, count, scale),
        grid_spec=pltpu.PrefetchScalarGridSpec(
            num_scalar_prefetch=1,
            grid=(heads,),
            in_specs=[head] * 3
            + [pl.BlockSpec((1, 1, rows), lambda h, seen: (h, 0, 0))]
            + [pl.BlockSpec((rows, wide), lambda h, seen: (0, 0))] * 2
            + [whole] * count,
            out_specs=[head] + [whole] * count,
            scratch_shapes=[
                pltpu.VMEM((count,) + pairs[0].shape, F32),
                pltpu.VMEM((wide, rows), F32),
            ],
        ),
        out_shape=[jax.ShapeDtypeStruct(queries.shape, BF)]
        + [jax.ShapeDtypeStruct(pairs[0].shape, F32 if r == 0 else BF) for r in range(count)],
        compiler_params=pltpu.CompilerParams(vmem_limit_bytes=KERNEL_BYTES),
        cost_estimate=pl.CostEstimate(flops=1, bytes_accessed=1, transcendentals=0),
    )(seen, queries, grads, outs, lse, cosine, sine, *pairs)
    return results[0], results[1:]


def products_kernel(a_ref, b_ref, c_ref, d_ref, out_ref):
    wide = b_ref.shape[1]
    out_ref[:, :wide] = dot_tn(a_ref[...], b_ref[...]).astype(BF)
    out_ref[:, wide:] = dot_tn(c_ref[...], d_ref[...]).astype(BF)


def products(a, b, c, d):
    tokens, depth = a.shape
    tile = depth // 3 if depth % (3 * LANES) == 0 else depth
    left = pl.BlockSpec((tokens, tile), lambda m: (0, m))
    right = pl.BlockSpec(b.shape, lambda m: (0, 0))
    return pl.pallas_call(
        products_kernel,
        grid=(depth // tile,),
        in_specs=[left, right, left, right],
        out_specs=pl.BlockSpec((tile, 2 * b.shape[1]), lambda m: (m, 0)),
        out_shape=jax.ShapeDtypeStruct((depth, 2 * b.shape[1]), BF),
        compiler_params=pltpu.CompilerParams(vmem_limit_bytes=KERNEL_BYTES),
        cost_estimate=pl.CostEstimate(flops=1, bytes_accessed=1, transcendentals=0),
    )(a, b, c, d)


def fetch(side, parts, held, sems):
    @pl.when(pl.program_id(0) == 0)
    def _():
        copies = []
        for k, dst in enumerate(held):
            for p in range(PARTS):
                src = parts[PARTS * k + p]
                rows = src.shape[0]
                high = side[0] if p < 2 else 1 - side[0]
                first = pl.multiple_of((2 * high + p % 2) * rows, rows)
                copies.append(
                    pltpu.make_async_copy(src, dst.at[pl.ds(first, rows)], sems.at[k, p])
                )
        for copy in copies:
            copy.start()
        for copy in copies:
            copy.wait()


def with_weights(body, grid, in_specs, weights, out_specs, out_shape):
    rows, units = weights[0][0].shape
    count = len(weights)
    first = 1 + len(in_specs)
    last = first + PARTS * count

    def kernel(*refs):
        held, sems = refs[-count - 1 : -1], refs[-1]
        fetch(refs[0], refs[first:last], held, sems)
        body(*refs[1:first], *held, *refs[last : -count - 1])

    return pl.pallas_call(
        kernel,
        grid=grid,
        in_specs=[pl.BlockSpec(memory_space=pltpu.SMEM)]
        + in_specs
        + [pl.BlockSpec(memory_space=pl.ANY)] * (PARTS * count),
        out_specs=out_specs,
        out_shape=out_shape,
        scratch_shapes=[pltpu.VMEM((PARTS * rows, units), BF)] * count
        + [pltpu.SemaphoreType.DMA((count, PARTS))],
        compiler_params=pltpu.CompilerParams(vmem_limit_bytes=KERNEL_BYTES),
        cost_estimate=pl.CostEstimate(flops=1, bytes_accessed=1, transcendentals=0),
    )


def hidden_kernel(n_ref, wg_ref, wu_ref, act_ref, by_gate_ref, by_up_ref):
    gate = dot_nn(n_ref[...], wg_ref[...])
    up = dot_nn(n_ref[...], wu_ref[...])
    sigmoid = jax.nn.sigmoid(gate)
    silu = gate * sigmoid
    act_ref[...] = (silu * up).astype(BF)
    by_gate_ref[...] = (up * (sigmoid + silu * (1.0 - sigmoid))).astype(BF)
    by_up_ref[...] = silu.astype(BF)


def hidden_units(side, normed, gate_w, up_w):
    tokens, depth = normed.shape
    units = gate_w[0].shape[1]
    tm = min(tokens, 256)
    rows = pl.BlockSpec((tm, depth), lambda m: (m, 0))
    out = pl.BlockSpec((tm, units), lambda m: (m, 0))
    shape = jax.ShapeDtypeStruct((tokens, units), BF)
    call = with_weights(
        hidden_kernel, (tokens // tm,), [rows], (gate_w, up_w), [out] * 3, [shape] * 3
    )
    return call(side, normed, *gate_w, *up_w)


def hidden_grad_kernel(d_ref, by_gate_ref, by_up_ref, wd_ref, dg_ref, du_ref):
    grad = dot_nn(d_ref[...], wd_ref[...])
    dg_ref[...] = (grad * by_gate_ref[...].astype(F32)).astype(BF)
    du_ref[...] = (grad * by_up_ref[...].astype(F32)).astype(BF)


def hidden_grads(side, grads, down_w, by_gate, by_up):
    tokens, depth = grads.shape
    units = down_w[0].shape[1]
    tm = min(tokens, 256)
    rows = pl.BlockSpec((tm, depth), lambda m: (m, 0))
    out = pl.BlockSpec((tm, units), lambda m: (m, 0))
    shape = jax.ShapeDtypeStruct((tokens, units), BF)
    call = with_weights(
        hidden_grad_kernel, (tokens // tm,), [rows, out, out], (down_w,), [out] * 2, [shape] * 2
    )
    return call(side, grads, by_gate, by_up, *down_w)


def back_kernel(count, half, *refs):
    lefts, rights = refs[:count], refs[count : 2 * count]
    first, second = refs[2 * count :]
    total = dot_nt(lefts[0][...], rights[0][...])
    for left, right in zip(lefts[1:], rights[1:]):
        total = total + dot_nt(left[...], right[...])
    step = pl.program_id(0)

    @pl.when(step < half)
    def _():
        first[...] = total.astype(BF)

    @pl.when(step >= half)
    def _():
        second[...] = total.astype(BF)


def hidden_back(side, lefts, rights):
    tokens, units = lefts[0].shape
    depth = PARTS * rights[0][0].shape[0]
    count = len(lefts)
    tm = min(tokens // 2, 512)
    half = tokens // 2 // tm
    rows = pl.BlockSpec((tm, units), lambda m: (m, 0))
    out_specs = [
        pl.BlockSpec((tm, depth), lambda m: (jnp.minimum(m, half - 1), 0)),
        pl.BlockSpec((tm, depth), lambda m: (jnp.maximum(m - half, 0), 0)),
    ]
    call = with_weights(
        functools.partial(back_kernel, count, half),
        (tokens // tm,),
        [rows] * count,
        rights,
        out_specs,
        [jax.ShapeDtypeStruct((tokens // 2, depth), BF)] * 2,
    )
    return call(side, *lefts, *[x for w in rights for x in w])


def after(x, *earlier):
    return lax.optimization_barrier((x,) + earlier)[0]


class Pending:
    def __init__(self, got, finish):
        self.got = got
        self.finish = finish


class Grid:
    def __init__(self):
        self.nf = lax.axis_size("fsdp")
        self.nc = lax.axis_size("context")
        self.n = self.nf * self.nc
        self.cbits = self.nc.bit_length() - 1
        self.fbits = self.nf.bit_length() - 1
        self.me = lax.axis_index("fsdp") * self.nc + lax.axis_index("context")
        self.my_slot = lax.axis_index("context")
        self.core = lax.axis_index("tensor")
        self.done = ()
        self.zm = 1
        self.xm = self.nc
        self.deep = list(range(1, self.cbits)) + list(range(self.cbits + 1, self.cbits + self.fbits))

    def bit(self, b):
        return (self.me >> b) & 1

    def fence(self, *xs):
        return lax.optimization_barrier(xs + self.done)[: len(xs)]

    def close(self, *xs):
        raw = lax.optimization_barrier(
            tuple(x.got if isinstance(x, Pending) else x for x in xs)
        )
        self.done = raw
        outs = [x.finish(r) if isinstance(x, Pending) else r for x, r in zip(xs, raw)]
        return outs[0] if len(outs) == 1 else outs

    def one(self, x, mask, pin=()):
        if pin:
            x = after(x, *pin)
        return lax.ppermute(x, BOTH, [(i, i ^ mask) for i in range(self.n)])

    def swap(self, x):
        return lax.ppermute(x, "tensor", [(0, 1), (1, 0)])

    def pair(self, b, mine, theirs, axis):
        low = self.bit(b) == 0
        return jnp.stack([jnp.where(low, mine, theirs), jnp.where(low, theirs, mine)], axis)

    def ordered(self, pieces, bits):
        if len(bits) == 0:
            return pieces[0]
        half = len(pieces) // 2
        low = self.ordered(pieces[:half], bits[:-1])
        high = self.ordered(pieces[half:], bits[:-1])
        return self.pair(bits[-1], low, high, 0)

    def fsdp_take(self, x, r):
        x = x.reshape(self.nf, -1, x.shape[1])
        return lax.dynamic_index_in_dim(x, lax.axis_index("fsdp") ^ r, 0, keepdims=False)

    def fsdp_far(self, x):
        far = self.fsdp_take(x, 3)
        cut = far.shape[0] // 2
        return far[:cut], far[cut:]

    def fsdp_near(self, x, by_y, by_x):
        px, py = self.fsdp_take(x, 1), self.fsdp_take(x, 2)
        cut = px.shape[0] // 2
        px = jnp.concatenate([px[:cut].astype(F32) + by_y.astype(F32), px[cut:].astype(F32)], 0)
        py = jnp.concatenate([py[:cut].astype(F32), py[cut:].astype(F32) + by_x.astype(F32)], 0)
        return px.astype(BF), py.astype(BF)

    def fsdp_end(self, x, rx, ry):
        return (self.fsdp_take(x, 0).astype(F32) + rx.astype(F32) + ry.astype(F32)).astype(BF)

    def over_x(self, x):
        return self.one(x, self.xm)

    def over_y(self, x):
        return self.one(x, 2 * self.xm)

    def over_z(self, x):
        return self.one(x, self.zm)

    def context_pick(self, x, r):
        x = x.reshape(self.nc, -1, x.shape[1])
        return lax.dynamic_index_in_dim(x, self.my_slot ^ r, 0, keepdims=False)

    def tokens_near(self, x, pin_x=(), pin_z=()):
        return self.one(x, self.xm, pin_x), self.one(x, self.zm, pin_z)

    def tokens_far(self, nears):
        cut = nears[0][0].shape[0] // 2
        by_z = self.one(jnp.concatenate([px[:cut] for px, _ in nears], 0), self.zm)
        by_x = self.one(jnp.concatenate([pz[cut:] for _, pz in nears], 0), self.xm)
        parts = []
        for k, (px, pz) in enumerate(nears):
            here = slice(k * cut, (k + 1) * cut)
            parts.append(jnp.concatenate([px, pz, by_z[here], by_x[here]], 0))
        return parts

    def tokens_split(self, part, other):
        rows = part.shape[0] // 4
        cut = rows // 2
        here = [slice(k * rows, (k + 1) * rows) for k in range(4)]
        own, px, pz, far = [part[k].astype(F32) + other[k].astype(F32) for k in here]
        return own, px, pz, far[:cut].astype(BF), far[cut:].astype(BF)

    def tokens_add(self, px, pz, by_z, by_x):
        cut = by_z.shape[0]
        px = jnp.concatenate([px[:cut] + by_z.astype(F32), px[cut:]], 0).astype(BF)
        pz = jnp.concatenate([pz[:cut], pz[cut:] + by_x.astype(F32)], 0).astype(BF)
        return px, pz

    def quarter_masks(self):
        return (0, self.zm, self.xm, self.xm + self.zm)

    def my_quarter(self):
        return 2 * self.bit(self.cbits) + self.bit(0)

    def quarter_groups(self):
        masks = (0, self.zm, self.xm, self.xm + self.zm)
        return [[i | m for m in masks] for i in range(self.n) if i & masks[3] == 0]

    def quarters_in(self, w):
        return lax.all_to_all(w, BOTH, 0, 0, axis_index_groups=self.quarter_groups())

    def quarters_out(self, g):
        return lax.all_to_all(g, BOTH, 0, 0, axis_index_groups=self.quarter_groups())

    def deepen(self, w, held, bits):
        for b in bits[:-1]:
            w = self.pair(b, w, self.one(w, 1 << b), sum(1 for h in held if h > b))
            held.append(b)
        b = bits[-1]
        axis = sum(1 for h in held if h > b)
        held.append(b)
        return Pending(self.one(w, 1 << b), lambda got: self.pair(b, w, got, axis))

    def fold(self, g, held, bits):
        def step(g, b):
            axis = held.index(b)
            held.remove(b)
            give = lax.dynamic_index_in_dim(g, 1 - self.bit(b), axis, keepdims=False)
            keep = lax.dynamic_index_in_dim(g, self.bit(b), axis, keepdims=False)
            finish = lambda got: (keep.astype(F32) + got.astype(F32)).astype(BF)
            return Pending(self.one(give, 1 << b), finish)

        for b in bits[:-1]:
            pending = step(g, b)
            g = pending.finish(pending.got)
        return step(g, bits[-1])


def on_device(
    tokens,
    block_order,
    norm_one,
    w_query,
    b_query,
    w_key,
    b_key,
    w_value,
    b_value,
    w_out,
    norm_two,
    w_gate,
    w_up,
    w_down,
    cotangent,
):
    grid = Grid()
    block_rows, width = tokens.shape
    shard = norm_one.shape[0]
    slot_count = grid.nc
    prompt_slots = slot_count // 2
    head_width = w_key.shape[1]
    query_width = w_query.shape[1]
    head_group = query_width // head_width
    score_scale = head_width ** (-0.5)
    cores = lax.axis_size("tensor")
    own_rows = block_rows // cores
    owners = block_order[0]
    my_block = lax.dynamic_index_in_dim(owners, grid.my_slot, 0, keepdims=False)
    query_anchor = locate(my_block, prompt_slots, block_rows)[1]
    query_pos = query_anchor + jnp.arange(block_rows)

    def own(x):
        return lax.dynamic_slice(x, (grid.core * own_rows, 0), (own_rows, x.shape[1]))

    def others(x):
        return lax.dynamic_slice(x, ((1 - grid.core) * own_rows, 0), (own_rows, x.shape[1]))

    def both(x):
        other = grid.swap(x)
        first = grid.core == 0
        return jnp.concatenate([jnp.where(first, x, other), jnp.where(first, other, x)], 0)

    def summed(part):
        give = lax.dynamic_slice(part, ((1 - grid.core) * own_rows, 0), (own_rows, width))
        return own(part) + grid.swap(give.astype(BF)).astype(F32)

    bias_shard = b_query.shape[1]
    small_bias = b_key.shape[1]
    vector = jnp.concatenate([norm_one[None], norm_two[None], b_query, b_key, b_value], axis=1)
    columns = query_width + 2 * head_width
    vector = jnp.pad(vector, ((0, 7), (0, columns - vector.shape[1])))
    packed = jnp.concatenate(
        [jnp.concatenate([w_query, w_key, w_value], axis=1), vector], axis=0
    )
    hidden = w_gate.shape[1]
    quarter = -(-hidden // (4 * LANES)) * LANES
    pad = ((0, 0), (0, 4 * quarter - hidden))
    w_out_t = lax.all_gather(w_out.T, BOTH, axis=0, tiled=True)

    context_deep = [b for b in grid.deep if b < grid.cbits]
    fsdp_deep = [b for b in grid.deep if b > grid.cbits]

    def quarters(w):
        return w.reshape(shard, 4, quarter).transpose(1, 0, 2)

    def deep_z(w):
        return grid.deepen(w, [0], context_deep)

    def give_y(w):
        return grid.one(w, 1 << fsdp_deep[0])

    def parts_of(*pieces):
        return tuple(x.reshape(grid.n // PARTS * shard, quarter) for x in pieces)

    side = grid.bit(fsdp_deep[0]).reshape(1)
    held = []
    gate_near = grid.quarters_in(quarters(jnp.pad(w_gate, pad)))
    packed = grid.deepen(packed, held, context_deep[::-1])
    gate_near, packed = grid.close(gate_near, packed)

    gate_near = gate_near.reshape(2, 2, shard, quarter)
    packed = grid.close(grid.deepen(packed, held, [0]))

    packed = packed.reshape(grid.nc * (shard + 8), columns)
    (gate_0,) = grid.fence(gate_near[0])
    gx, gy, gate_0 = grid.close(grid.over_x(packed), grid.over_y(packed), deep_z(gate_0))

    cut = gx.shape[0] // 2
    gate_1, up_in = grid.fence(gate_near[1], quarters(jnp.pad(w_up, pad)))
    by_y, by_x = grid.over_y(gx[:cut]), grid.over_x(gy[cut:])
    by_y, by_x, gate_1, up_near = grid.close(
        by_y, by_x, deep_z(gate_1), grid.quarters_in(up_in)
    )

    up_near = up_near.reshape(2, 2, shard, quarter)
    pieces = [packed, gx, gy, jnp.concatenate([by_y, by_x], 0)]
    pieces = [x.reshape(grid.nc, shard + 8, columns) for x in pieces]
    sources = [grid.cbits, grid.cbits + 1]
    w_qkv = grid.ordered([x[:, :shard] for x in pieces], sources)
    w_qkv = w_qkv.reshape(grid.n * shard, columns)
    vectors = grid.ordered([x[:, shard] for x in pieces], sources).reshape(grid.n, columns)
    gain_one = vectors[:, :shard].reshape(-1)
    gain_two = vectors[:, shard : 2 * shard].reshape(-1)
    start = 2 * shard
    bias = jnp.concatenate(
        [
            vectors[:, start : start + bias_shard].reshape(-1),
            vectors[:, start + bias_shard : start + bias_shard + small_bias].reshape(-1),
            vectors[
                :, start + bias_shard + small_bias : start + bias_shard + 2 * small_bias
            ].reshape(-1),
        ]
    ).astype(F32)

    inputs = tokens.astype(F32)
    inv_one = lax.rsqrt(jnp.mean(inputs * inputs, axis=-1, keepdims=True) + EPSILON)
    rows_one = inputs * inv_one
    normed_one = (rows_one * gain_one.astype(F32)).astype(BF)
    cosine, sine = tables(query_pos, head_width)
    grads_own, grads_other = own(cotangent), others(cotangent)
    gate_0, grads_pz = grid.fence(gate_0, grads_own)
    gate_2, grads_pz = give_y(gate_0), grid.over_z(grads_pz)
    qkv = dot_nn(normed_one, w_qkv) + bias
    keys = qkv[:, query_width : query_width + head_width]
    keys = keys * cosine + swap_halves(keys) * sine
    pair = jnp.concatenate([keys, qkv[:, query_width + head_width :]], axis=1).astype(BF)
    pair, qkv, gate_2, grads_pz = grid.close(pair, qkv, gate_2, grads_pz)

    gate_1, grads_px = grid.fence(gate_1, grads_own)
    met = [grid.one(pair, r) for r in range(1, slot_count)]
    gate_3, grads_px, *met = grid.close(give_y(gate_1), grid.over_x(grads_px), *met)
    pairs = [pair] + met

    piece_block = owners[grid.my_slot ^ jnp.arange(slot_count)]
    seen = ((piece_block < prompt_slots) & (piece_block < my_block)).astype(jnp.int32)
    up_0, down_in = grid.fence(up_near[0], quarters(jnp.pad(w_down.T, pad)))
    up_0, down_near = deep_z(up_0), grid.quarters_in(down_in)
    queries, attn_heads, out_low, log_total = attend(
        seen, qkv, cosine, sine, pairs, head_group, score_scale
    )
    out_low, up_0, down_near = grid.close(out_low, up_0, down_near)

    down_near = down_near.reshape(2, 2, shard, quarter)
    hidden_one = own(tokens).astype(F32) + summed(dot_nt(out_low, w_out_t))

    inv_two = lax.rsqrt(jnp.mean(hidden_one * hidden_one, axis=-1, keepdims=True) + EPSILON)
    rows_two = hidden_one * inv_two
    normed_two = (rows_two * gain_two.astype(F32)).astype(BF)
    normed_two = grid.close(normed_two)

    up_0, up_1 = grid.fence(up_0, up_near[1])
    px, pz, normed_other, up_1, up_2 = grid.close(
        grid.over_x(normed_two),
        grid.over_z(normed_two),
        grid.swap(normed_two),
        deep_z(up_1),
        give_y(up_0),
    )

    cut = px.shape[0] // 2
    (down_0,) = grid.fence(down_near[0])
    normed_near = jnp.concatenate([px, pz], 0)
    by_z, by_x, up_3, down_0, normed_swap = grid.close(
        grid.over_z(px[:cut]),
        grid.over_x(pz[cut:]),
        give_y(up_1),
        deep_z(down_0),
        grid.swap(normed_near),
    )

    normed_far = jnp.concatenate([by_z, by_x], 0)
    gate_full = parts_of(gate_0, gate_1, gate_2, gate_3)
    up_full = parts_of(up_0, up_1, up_2, up_3)
    far_swap, grads_swap = grid.close(
        grid.swap(normed_far), grid.swap(jnp.concatenate([grads_px, grads_pz], 0))
    )

    normed_in = jnp.concatenate(
        [normed_two, normed_near, normed_far, normed_other, normed_swap, far_swap], 0
    )
    far_z, far_x, down_0, down_1 = grid.fence(
        grads_px[:cut], grads_pz[cut:], down_0, down_near[1]
    )
    by_z, by_x = grid.over_z(far_z), grid.over_x(far_x)
    down_2, down_1 = give_y(down_0), deep_z(down_1)
    act, by_gate, by_up = hidden_units(side, normed_in, gate_full, up_full)
    act, by_z, by_x, down_2, down_1 = grid.close(act, by_z, by_x, down_2, down_1)

    grads_far = jnp.concatenate([by_z, by_x], 0)
    down_3 = give_y(down_1)
    grads_in = jnp.concatenate(
        [grads_own, grads_px, grads_pz, grads_far, grads_other, grads_swap, grid.swap(grads_far)],
        0,
    )
    grad_wdown = dot_tn(grads_in, act).astype(BF)
    grad_wdown, down_3 = grid.close(grad_wdown, down_3)
    down_full = parts_of(down_0, down_1, down_2, down_3)

    top = sorted(range(grid.cbits + grid.fbits), reverse=True)
    shape = (2,) * len(top) + (shard, quarter)
    y_back, z_back = fsdp_deep[::-1], context_deep[::-1]

    def half(grad, h):
        return lax.index_in_dim(grad.reshape(shape), h, top.index(grid.cbits), keepdims=False)

    def fold_y(grad):
        return grid.fold(grad, [b for b in top if b != grid.cbits], y_back)

    def fold_z(grad):
        return grid.fold(grad, [b for b in top if b not in fsdp_deep and b != grid.cbits], z_back)

    def joined(first, second):
        return jnp.stack([first, second], 0).reshape(4, shard, quarter)

    down_0 = fold_y(half(grad_wdown, 0))
    grad_gate, grad_up = hidden_grads(side, grads_in, down_full, by_gate, by_up)
    down_0, grad_gate, grad_up = grid.close(down_0, grad_gate, grad_up)

    (grad_wdown,) = grid.fence(grad_wdown)
    down_0, down_1 = fold_z(down_0), fold_y(half(grad_wdown, 1))
    part, give = hidden_back(side, (grad_gate, grad_up), (gate_full, up_full))
    down_0, down_1, part, give = grid.close(down_0, down_1, part, give)

    other = grid.swap(give)
    (up_in,) = grid.fence(grad_up)
    grad_wup = dot_tn(normed_in, up_in).astype(BF)
    other, grad_wup = grid.close(other, grad_wup)

    part_own, px, pz, far_z, far_x = grid.tokens_split(part, other)
    down_1, gate_in = grid.fence(down_1, grad_gate)
    by_z, by_x = grid.over_z(far_z), grid.over_x(far_x)
    down_1, up_0 = fold_z(down_1), fold_y(half(grad_wup, 0))
    grad_wgate = dot_tn(normed_in, gate_in).astype(BF)
    by_z, by_x, down_1, up_0, grad_wgate = grid.close(by_z, by_x, down_1, up_0, grad_wgate)

    px, pz = grid.tokens_add(px, pz, by_z, by_x)
    grad_wup, act_in = grid.fence(grad_wup, act)
    px, pz = grid.over_x(px), grid.over_z(pz)
    up_0, up_1 = fold_z(up_0), fold_y(half(grad_wup, 1))
    mlp_part, mlp_give = hidden_back(side, (act_in,), (down_full,))
    px, pz, up_0, up_1, mlp_part, mlp_give = grid.close(
        px, pz, up_0, up_1, mlp_part, mlp_give
    )

    (down_in,) = grid.fence(joined(down_0, down_1))
    grad_wdown = grid.quarters_out(down_in)
    mlp_other = grid.swap(mlp_give)
    grad_normed_two = part_own + px.astype(F32) + pz.astype(F32)
    grad_gain_two = jnp.sum(grad_normed_two * rows_two, axis=0)
    grad_hidden_one = own(cotangent).astype(F32) + norm_back(
        grad_normed_two, rows_two, inv_two, gain_two
    )
    grad_low = both(grad_hidden_one.astype(BF))
    grad_heads = dot_nn(grad_low, w_out_t).astype(BF)
    grad_heads, mlp_other, grad_wdown = grid.close(grad_heads, mlp_other, grad_wdown)

    mlp_own, mx, mz, far_z, far_x = grid.tokens_split(mlp_part, mlp_other)
    grad_wgate, up_1 = grid.fence(grad_wgate, up_1)
    by_z, by_x = grid.over_z(far_z), grid.over_x(far_x)
    gate_0, up_1 = fold_y(half(grad_wgate, 0)), fold_z(up_1)
    grad_query, grad_pairs = attend_back(
        seen,
        queries,
        grad_heads,
        attn_heads,
        log_total,
        cosine,
        sine,
        pairs,
        head_group,
        score_scale,
    )
    by_z, by_x, gate_0, up_1, grad_query, *grad_pairs = grid.close(
        by_z, by_x, gate_0, up_1, grad_query, *grad_pairs
    )

    grad_got = [grid.one(x, r + 1) for r, x in enumerate(grad_pairs[1:])]
    mx, mz = grid.tokens_add(mx, mz, by_z, by_x)
    (grad_wgate,) = grid.fence(grad_wgate)
    mx, gate_1 = grid.over_x(mx), fold_y(half(grad_wgate, 1))
    grad_attn = products(normed_one, grad_query, grad_low, out_low)
    mx, gate_1, grad_attn, *grad_got = grid.close(mx, gate_1, grad_attn, *grad_got)

    far_y, far_x = grid.fsdp_far(grad_attn)
    mz, grad_query = grid.fence(mz, grad_query)
    by_y, by_x = grid.over_y(far_y), grid.over_x(far_x)
    gate_0, mz = fold_z(gate_0), grid.over_z(mz)
    grad_pair = grad_pairs[0]
    for x in grad_got:
        grad_pair = grad_pair + x.astype(F32)
    grad_keys = grad_pair[:, :head_width]
    grad_keys = grad_keys * cosine - swap_halves(grad_keys) * sine
    grad_kv = jnp.concatenate([grad_keys, grad_pair[:, head_width:]], axis=1).astype(BF)
    grad_qkv = jnp.concatenate([grad_query, grad_kv], axis=1)
    grad_bias = jnp.sum(grad_qkv.astype(F32), axis=0)
    grad_normed_one = summed(dot_nt(grad_qkv, w_qkv))
    rows_own = own(rows_one)
    inv_own = own(inv_one)
    grad_gain_one = jnp.sum(grad_normed_one * rows_own, axis=0)
    gains = jnp.concatenate(
        [grad_gain_one.reshape(-1, shard), grad_gain_two.reshape(-1, shard)], axis=1
    )
    gains = gains + grid.swap(gains)
    small = jnp.concatenate(
        [
            gains,
            grad_bias[:query_width].reshape(-1, bias_shard),
            grad_bias[query_width : query_width + head_width].reshape(-1, small_bias),
            grad_bias[query_width + head_width :].reshape(-1, small_bias),
        ],
        axis=1,
    )
    wide = 2 * head_width
    small = jnp.pad(small[:, None], ((0, 0), (0, 7), (0, max(wide - small.shape[1], 0))))
    grad_wkv = dot_tn(normed_one, grad_kv).reshape(grid.n, shard, wide)
    grad_wkv = jnp.concatenate([grad_wkv, small], axis=1).astype(BF)
    grad_wkv = grad_wkv.reshape(grid.n * (shard + 8), wide)
    by_y, by_x, gate_0, mz, grad_wkv, grad_normed_one = grid.close(
        by_y, by_x, gate_0, mz, grad_wkv, grad_normed_one
    )

    ax, ay = grid.fsdp_near(grad_attn, by_y, by_x)
    far_y, far_x = grid.fsdp_far(grad_wkv)
    (gate_1,) = grid.fence(gate_1)
    ax, ay = grid.over_x(ax), grid.over_y(ay)
    by_y, by_x, gate_1 = grid.over_y(far_y), grid.over_x(far_x), fold_z(gate_1)
    grad_inputs = grad_hidden_one + norm_back(grad_normed_one, rows_own, inv_own, gain_one)
    result = (hidden_one + mlp_own + mx.astype(F32) + mz.astype(F32)).astype(BF)
    ax, ay, by_y, by_x, gate_1, grad_tokens, result = grid.close(
        ax, ay, by_y, by_x, gate_1, grad_inputs.astype(BF), result
    )

    grad_attn = grid.fsdp_end(grad_attn, ax, ay)
    kx, ky = grid.fsdp_near(grad_wkv, by_y, by_x)
    (up_in,) = grid.fence(joined(up_0, up_1))
    kx, ky = grid.over_x(kx), grid.over_y(ky)
    parts = [grid.one(grid.context_pick(grad_attn, r), r) for r in range(1, grid.nc)]
    grad_wup = grid.quarters_out(up_in)
    grad_tokens, result = both(grad_tokens), both(result)
    kx, ky, grad_wup, grad_tokens, result, *parts = grid.close(
        kx, ky, grad_wup, grad_tokens, result, *parts
    )

    (gate_in,) = grid.fence(joined(gate_0, gate_1))
    grad_wgate = grid.quarters_out(gate_in)
    grad_wkv = grid.fsdp_end(grad_wkv, kx, ky)
    terms = [grid.one(grid.context_pick(grad_wkv, r), r) for r in range(1, grid.nc)]
    grad_attn = grid.context_pick(grad_attn, 0).astype(F32)
    for x in parts:
        grad_attn = grad_attn + x.astype(F32)
    grad_wkv = grid.context_pick(grad_wkv, 0).astype(F32)
    for x in terms:
        grad_wkv = grad_wkv + x.astype(F32)
    small = grad_wkv[shard : shard + 1]
    grad_wkv = grad_wkv[:shard]
    grad_wdown, grad_wup, grad_wgate = [
        g.transpose(1, 0, 2).reshape(shard, 4 * quarter).astype(F32)
        for g in (grad_wdown, grad_wup, grad_wgate)
    ]
    return (
        result,
        grad_tokens,
        small[0, :shard],
        grad_attn[:, :query_width],
        small[:, start : start + bias_shard],
        grad_wkv[:, :head_width],
        small[:, start + bias_shard : start + bias_shard + small_bias],
        grad_wkv[:, head_width:],
        small[:, start + bias_shard + small_bias : start + bias_shard + 2 * small_bias],
        grad_attn[:, query_width : 2 * query_width].T,
        small[0, shard : 2 * shard],
        grad_wgate[:, :hidden],
        grad_wup[:, :hidden],
        grad_wdown[:, :hidden].T,
    )


def solution(mesh):
    rows = P(("fsdp", "context"), None)
    split = P(("fsdp", "context"))
    into = P(("fsdp", "context"), "tensor")
    back = P("tensor", ("fsdp", "context"))
    return jax.shard_map(
        on_device,
        mesh=mesh,
        in_specs=(
            rows,
            P("fsdp", None),
            split,
            into,
            back,
            into,
            back,
            into,
            back,
            back,
            split,
            into,
            into,
            back,
            rows,
        ),
        out_specs=(
            rows,
            rows,
            split,
            into,
            back,
            into,
            back,
            into,
            back,
            back,
            split,
            into,
            into,
            back,
        ),
        check_vma=False,
    )
```

```python
import functools

import jax
import jax.numpy as jnp
from jax import lax
from jax.experimental import pallas as pl
from jax.experimental.pallas import tpu as pltpu
from jax.sharding import PartitionSpec as P

EPSILON = 1e-06
ROPE_BASE = 1000000.0
MASKED = -1e30
LANES = 128
PARTS = 4
BOTH = ("fsdp", "context")
KERNEL_BYTES = 56 << 20
BF = jnp.bfloat16
F32 = jnp.float32


def tables(positions, head_width):
    ladder = jnp.arange(head_width // 2, dtype=F32)
    inverse = jnp.exp(-jnp.log(ROPE_BASE) * 2.0 * ladder / head_width)
    angles = positions.astype(F32)[:, None] * inverse[None, :]
    cosine, sine = jnp.cos(angles), jnp.sin(angles)
    return (
        jnp.concatenate([cosine, cosine], axis=1),
        jnp.concatenate([-sine, sine], axis=1),
    )


def swap_halves(x):
    middle = x.shape[1] // 2
    return jnp.concatenate([x[:, middle:], x[:, :middle]], axis=1)


def locate(blocks, prompt_slots, block_rows):
    segment = jnp.where(blocks < prompt_slots, 0, blocks - prompt_slots + 1)
    anchor = jnp.where(blocks < prompt_slots, blocks * block_rows, prompt_slots * block_rows)
    return (segment, anchor)


def dot_nn(left, right):
    return lax.dot_general(left, right, (((1,), (0,)), ((), ())), preferred_element_type=F32)


def dot_tn(left, right):
    return lax.dot_general(left, right, (((0,), (0,)), ((), ())), preferred_element_type=F32)


def dot_nt(left, right):
    return lax.dot_general(left, right, (((1,), (1,)), ((), ())), preferred_element_type=F32)


def norm_back(grad_normed, rows_normed, inv_rms, gain):
    grad_rows = grad_normed * gain.astype(F32)
    return inv_rms * (
        grad_rows - rows_normed * jnp.mean(grad_rows * rows_normed, axis=-1, keepdims=True)
    )


def turn(x, cosine, sine):
    return x * cosine + pltpu.roll(x, x.shape[1] // 2, 1) * sine


def attend_kernel(count, scale, seen, lin_ref, cos_ref, sin_ref, *refs):
    pairs = refs[:count]
    q_ref, out_ref, low_ref, lse_ref, peak_ref, total_ref, sum_ref = refs[count:]
    wide = lin_ref.shape[1]
    query = turn(lin_ref[...], cos_ref[...], sin_ref[...]).astype(BF)
    q_ref[...] = query

    def piece(r):
        scores = dot_nt(pairs[r][:, :wide], query) * scale
        if r == 0:
            rows = lax.broadcasted_iota(jnp.int32, scores.shape, 0)
            columns = lax.broadcasted_iota(jnp.int32, scores.shape, 1)
            scores = jnp.where(rows <= columns, scores, MASKED)
            peak = jnp.max(scores, axis=0, keepdims=True)
        else:
            old = peak_ref[...]
            peak = jnp.maximum(old, jnp.max(scores, axis=0, keepdims=True))
        probs = jnp.exp(scores - peak)
        total = jnp.sum(probs, axis=0, keepdims=True)
        mixed = dot_tn(pairs[r][:, wide:], probs.astype(BF))
        if r:
            shrink = jnp.exp(old - peak)
            total = total + total_ref[...] * shrink
            mixed = mixed + sum_ref[...] * shrink
        peak_ref[...] = peak
        total_ref[...] = total
        sum_ref[...] = mixed

    piece(0)
    for r in range(1, count):
        pl.when(seen[r] != 0)(functools.partial(piece, r))
    total = total_ref[...]
    out = jnp.transpose(sum_ref[...] / total)
    out_ref[...] = out
    low_ref[...] = out.astype(BF)
    lse_ref[...] = (peak_ref[...] + jnp.log(total))[None]


def attend(seen, lin, cosine, sine, pairs, heads, scale):
    rows, wide = cosine.shape
    count = len(pairs)
    every = pl.BlockSpec((rows, wide), lambda h, seen: (0, 0))
    head = pl.BlockSpec((rows, wide), lambda h, seen: (0, h))
    whole = pl.BlockSpec(pairs[0].shape, lambda h, seen: (0, 0))
    return pl.pallas_call(
        functools.partial(attend_kernel, count, scale),
        grid_spec=pltpu.PrefetchScalarGridSpec(
            num_scalar_prefetch=1,
            grid=(heads,),
            in_specs=[head, every, every] + [whole] * count,
            out_specs=[head, head, head, pl.BlockSpec((1, 1, rows), lambda h, seen: (h, 0, 0))],
            scratch_shapes=[
                pltpu.VMEM((1, rows), F32),
                pltpu.VMEM((1, rows), F32),
                pltpu.VMEM((wide, rows), F32),
            ],
        ),
        out_shape=[
            jax.ShapeDtypeStruct((rows, heads * wide), BF),
            jax.ShapeDtypeStruct((rows, heads * wide), F32),
            jax.ShapeDtypeStruct((rows, heads * wide), BF),
            jax.ShapeDtypeStruct((heads, 1, rows), F32),
        ],
        compiler_params=pltpu.CompilerParams(vmem_limit_bytes=KERNEL_BYTES),
        cost_estimate=pl.CostEstimate(flops=1, bytes_accessed=1, transcendentals=0),
    )(seen, lin, cosine, sine, *pairs)


def attend_back_kernel(
    count, scale, seen, q_ref, g_ref, out_ref, lse_ref, cos_ref, sin_ref, *refs
):
    pairs = refs[:count]
    dq_ref = refs[count]
    grads = refs[count + 1 : 2 * count + 1]
    held, sum_ref = refs[2 * count + 1 :]
    wide = q_ref.shape[1]
    step = pl.program_id(0)
    query = q_ref[...]
    grad = g_ref[...]
    delta = jnp.sum(grad.astype(F32) * out_ref[...], axis=1, keepdims=True)
    delta = jnp.transpose(jnp.broadcast_to(delta, q_ref.shape))[:1]
    lse = lse_ref[0]

    @pl.when(step == 0)
    def _():
        held[...] = jnp.zeros_like(held)

    def piece(r):
        key = pairs[r][:, :wide]
        probs = jnp.exp(dot_nt(key, query) * scale - lse)
        if r == 0:
            rows = lax.broadcasted_iota(jnp.int32, probs.shape, 0)
            columns = lax.broadcasted_iota(jnp.int32, probs.shape, 1)
            probs = jnp.where(rows <= columns, probs, 0.0)
        grad_scores = (probs * (dot_nt(pairs[r][:, wide:], grad) - delta)).astype(BF)
        held[r, :, wide:] += dot_nn(probs.astype(BF), grad)
        held[r, :, :wide] += dot_nn(grad_scores, query) * scale
        term = dot_tn(key, grad_scores)
        sum_ref[...] = term if r == 0 else sum_ref[...] + term

    piece(0)
    for r in range(1, count):
        pl.when(seen[r] != 0)(functools.partial(piece, r))
    grad_query = jnp.transpose(sum_ref[...]) * scale
    dq_ref[...] = turn(grad_query, cos_ref[...], -sin_ref[...]).astype(BF)

    @pl.when(step == pl.num_programs(0) - 1)
    def _():
        for r in range(count):
            grads[r][...] = held[r].astype(grads[r].dtype)


def attend_back(seen, queries, grads, outs, lse, cosine, sine, pairs, heads, scale):
    rows = queries.shape[0]
    wide = queries.shape[1] // heads
    count = len(pairs)
    head = pl.BlockSpec((rows, wide), lambda h, seen: (0, h))
    whole = pl.BlockSpec(pairs[0].shape, lambda h, seen: (0, 0))
    results = pl.pallas_call(
        functools.partial(attend_back_kernel, count, scale),
        grid_spec=pltpu.PrefetchScalarGridSpec(
            num_scalar_prefetch=1,
            grid=(heads,),
            in_specs=[head] * 3
            + [pl.BlockSpec((1, 1, rows), lambda h, seen: (h, 0, 0))]
            + [pl.BlockSpec((rows, wide), lambda h, seen: (0, 0))] * 2
            + [whole] * count,
            out_specs=[head] + [whole] * count,
            scratch_shapes=[
                pltpu.VMEM((count,) + pairs[0].shape, F32),
                pltpu.VMEM((wide, rows), F32),
            ],
        ),
        out_shape=[jax.ShapeDtypeStruct(queries.shape, BF)]
        + [jax.ShapeDtypeStruct(pairs[0].shape, F32 if r == 0 else BF) for r in range(count)],
        compiler_params=pltpu.CompilerParams(vmem_limit_bytes=KERNEL_BYTES),
        cost_estimate=pl.CostEstimate(flops=1, bytes_accessed=1, transcendentals=0),
    )(seen, queries, grads, outs, lse, cosine, sine, *pairs)
    return results[0], results[1:]


def products_kernel(a_ref, b_ref, c_ref, d_ref, out_ref):
    wide = b_ref.shape[1]
    out_ref[:, :wide] = dot_tn(a_ref[...], b_ref[...]).astype(BF)
    out_ref[:, wide:] = dot_tn(c_ref[...], d_ref[...]).astype(BF)


def products(a, b, c, d):
    tokens, depth = a.shape
    tile = depth // 3 if depth % (3 * LANES) == 0 else depth
    left = pl.BlockSpec((tokens, tile), lambda m: (0, m))
    right = pl.BlockSpec(b.shape, lambda m: (0, 0))
    return pl.pallas_call(
        products_kernel,
        grid=(depth // tile,),
        in_specs=[left, right, left, right],
        out_specs=pl.BlockSpec((tile, 2 * b.shape[1]), lambda m: (m, 0)),
        out_shape=jax.ShapeDtypeStruct((depth, 2 * b.shape[1]), BF),
        compiler_params=pltpu.CompilerParams(vmem_limit_bytes=KERNEL_BYTES),
        cost_estimate=pl.CostEstimate(flops=1, bytes_accessed=1, transcendentals=0),
    )(a, b, c, d)


def fetch(side, parts, held, sems):
    @pl.when(pl.program_id(0) == 0)
    def _():
        copies = []
        for k, dst in enumerate(held):
            for p in range(PARTS):
                src = parts[PARTS * k + p]
                rows = src.shape[0]
                high = side[0] if p < 2 else 1 - side[0]
                first = pl.multiple_of((2 * high + p % 2) * rows, rows)
                copies.append(
                    pltpu.make_async_copy(src, dst.at[pl.ds(first, rows)], sems.at[k, p])
                )
        for copy in copies:
            copy.start()
        for copy in copies:
            copy.wait()


def with_weights(body, grid, in_specs, weights, out_specs, out_shape):
    rows, units = weights[0][0].shape
    count = len(weights)
    first = 1 + len(in_specs)
    last = first + PARTS * count

    def kernel(*refs):
        held, sems = refs[-count - 1 : -1], refs[-1]
        fetch(refs[0], refs[first:last], held, sems)
        body(*refs[1:first], *held, *refs[last : -count - 1])

    return pl.pallas_call(
        kernel,
        grid=grid,
        in_specs=[pl.BlockSpec(memory_space=pltpu.SMEM)]
        + in_specs
        + [pl.BlockSpec(memory_space=pl.ANY)] * (PARTS * count),
        out_specs=out_specs,
        out_shape=out_shape,
        scratch_shapes=[pltpu.VMEM((PARTS * rows, units), BF)] * count
        + [pltpu.SemaphoreType.DMA((count, PARTS))],
        compiler_params=pltpu.CompilerParams(vmem_limit_bytes=KERNEL_BYTES),
        cost_estimate=pl.CostEstimate(flops=1, bytes_accessed=1, transcendentals=0),
    )


def hidden_kernel(n_ref, wg_ref, wu_ref, act_ref, by_gate_ref, by_up_ref):
    gate = dot_nn(n_ref[...], wg_ref[...])
    up = dot_nn(n_ref[...], wu_ref[...])
    sigmoid = jax.nn.sigmoid(gate)
    silu = gate * sigmoid
    act_ref[...] = (silu * up).astype(BF)
    by_gate_ref[...] = (up * (sigmoid + silu * (1.0 - sigmoid))).astype(BF)
    by_up_ref[...] = silu.astype(BF)


def hidden_units(side, normed, gate_w, up_w):
    tokens, depth = normed.shape
    units = gate_w[0].shape[1]
    tm = min(tokens, 256)
    rows = pl.BlockSpec((tm, depth), lambda m: (m, 0))
    out = pl.BlockSpec((tm, units), lambda m: (m, 0))
    shape = jax.ShapeDtypeStruct((tokens, units), BF)
    call = with_weights(
        hidden_kernel, (tokens // tm,), [rows], (gate_w, up_w), [out] * 3, [shape] * 3
    )
    return call(side, normed, *gate_w, *up_w)


def hidden_grad_kernel(d_ref, by_gate_ref, by_up_ref, wd_ref, dg_ref, du_ref):
    grad = dot_nn(d_ref[...], wd_ref[...])
    dg_ref[...] = (grad * by_gate_ref[...].astype(F32)).astype(BF)
    du_ref[...] = (grad * by_up_ref[...].astype(F32)).astype(BF)


def hidden_grads(side, grads, down_w, by_gate, by_up):
    tokens, depth = grads.shape
    units = down_w[0].shape[1]
    tm = min(tokens, 256)
    rows = pl.BlockSpec((tm, depth), lambda m: (m, 0))
    out = pl.BlockSpec((tm, units), lambda m: (m, 0))
    shape = jax.ShapeDtypeStruct((tokens, units), BF)
    call = with_weights(
        hidden_grad_kernel, (tokens // tm,), [rows, out, out], (down_w,), [out] * 2, [shape] * 2
    )
    return call(side, grads, by_gate, by_up, *down_w)


def back_kernel(count, half, *refs):
    lefts, rights = refs[:count], refs[count : 2 * count]
    first, second = refs[2 * count :]
    total = dot_nt(lefts[0][...], rights[0][...])
    for left, right in zip(lefts[1:], rights[1:]):
        total = total + dot_nt(left[...], right[...])
    step = pl.program_id(0)

    @pl.when(step < half)
    def _():
        first[...] = total.astype(BF)

    @pl.when(step >= half)
    def _():
        second[...] = total.astype(BF)


def hidden_back(side, lefts, rights):
    tokens, units = lefts[0].shape
    depth = PARTS * rights[0][0].shape[0]
    count = len(lefts)
    tm = min(tokens // 2, 512)
    half = tokens // 2 // tm
    rows = pl.BlockSpec((tm, units), lambda m: (m, 0))
    out_specs = [
        pl.BlockSpec((tm, depth), lambda m: (jnp.minimum(m, half - 1), 0)),
        pl.BlockSpec((tm, depth), lambda m: (jnp.maximum(m - half, 0), 0)),
    ]
    call = with_weights(
        functools.partial(back_kernel, count, half),
        (tokens // tm,),
        [rows] * count,
        rights,
        out_specs,
        [jax.ShapeDtypeStruct((tokens // 2, depth), BF)] * 2,
    )
    return call(side, *lefts, *[x for w in rights for x in w])


def after(x, *earlier):
    return lax.optimization_barrier((x,) + earlier)[0]


class Pending:
    def __init__(self, got, finish):
        self.got = got
        self.finish = finish


class Grid:
    def __init__(self):
        self.nf = lax.axis_size("fsdp")
        self.nc = lax.axis_size("context")
        self.n = self.nf * self.nc
        self.cbits = self.nc.bit_length() - 1
        self.fbits = self.nf.bit_length() - 1
        self.me = lax.axis_index("fsdp") * self.nc + lax.axis_index("context")
        self.my_slot = lax.axis_index("context")
        self.core = lax.axis_index("tensor")
        self.done = ()
        self.zm = 1
        self.xm = self.nc
        self.deep = list(range(1, self.cbits)) + list(range(self.cbits + 1, self.cbits + self.fbits))

    def bit(self, b):
        return (self.me >> b) & 1

    def fence(self, *xs):
        return lax.optimization_barrier(xs + self.done)[: len(xs)]

    def close(self, *xs):
        raw = lax.optimization_barrier(
            tuple(x.got if isinstance(x, Pending) else x for x in xs)
        )
        self.done = raw
        outs = [x.finish(r) if isinstance(x, Pending) else r for x, r in zip(xs, raw)]
        return outs[0] if len(outs) == 1 else outs

    def one(self, x, mask, pin=()):
        if pin:
            x = after(x, *pin)
        return lax.ppermute(x, BOTH, [(i, i ^ mask) for i in range(self.n)])

    def swap(self, x):
        return lax.ppermute(x, "tensor", [(0, 1), (1, 0)])

    def pair(self, b, mine, theirs, axis):
        low = self.bit(b) == 0
        return jnp.stack([jnp.where(low, mine, theirs), jnp.where(low, theirs, mine)], axis)

    def ordered(self, pieces, bits):
        if len(bits) == 0:
            return pieces[0]
        half = len(pieces) // 2
        low = self.ordered(pieces[:half], bits[:-1])
        high = self.ordered(pieces[half:], bits[:-1])
        return self.pair(bits[-1], low, high, 0)

    def fsdp_take(self, x, r):
        x = x.reshape(self.nf, -1, x.shape[1])
        return lax.dynamic_index_in_dim(x, lax.axis_index("fsdp") ^ r, 0, keepdims=False)

    def fsdp_far(self, x):
        far = self.fsdp_take(x, 3)
        cut = far.shape[0] // 2
        return far[:cut], far[cut:]

    def fsdp_near(self, x, by_y, by_x):
        px, py = self.fsdp_take(x, 1), self.fsdp_take(x, 2)
        cut = px.shape[0] // 2
        px = jnp.concatenate([px[:cut].astype(F32) + by_y.astype(F32), px[cut:].astype(F32)], 0)
        py = jnp.concatenate([py[:cut].astype(F32), py[cut:].astype(F32) + by_x.astype(F32)], 0)
        return px.astype(BF), py.astype(BF)

    def fsdp_end(self, x, rx, ry):
        return (self.fsdp_take(x, 0).astype(F32) + rx.astype(F32) + ry.astype(F32)).astype(BF)

    def over_x(self, x):
        return self.one(x, self.xm)

    def over_y(self, x):
        return self.one(x, 2 * self.xm)

    def over_z(self, x):
        return self.one(x, self.zm)

    def context_pick(self, x, r):
        x = x.reshape(self.nc, -1, x.shape[1])
        return lax.dynamic_index_in_dim(x, self.my_slot ^ r, 0, keepdims=False)

    def tokens_near(self, x, pin_x=(), pin_z=()):
        return self.one(x, self.xm, pin_x), self.one(x, self.zm, pin_z)

    def tokens_far(self, nears):
        cut = nears[0][0].shape[0] // 2
        by_z = self.one(jnp.concatenate([px[:cut] for px, _ in nears], 0), self.zm)
        by_x = self.one(jnp.concatenate([pz[cut:] for _, pz in nears], 0), self.xm)
        parts = []
        for k, (px, pz) in enumerate(nears):
            here = slice(k * cut, (k + 1) * cut)
            parts.append(jnp.concatenate([px, pz, by_z[here], by_x[here]], 0))
        return parts

    def tokens_split(self, part, other):
        rows = part.shape[0] // 4
        cut = rows // 2
        here = [slice(k * rows, (k + 1) * rows) for k in range(4)]
        own, px, pz, far = [part[k].astype(F32) + other[k].astype(F32) for k in here]
        return own, px, pz, far[:cut].astype(BF), far[cut:].astype(BF)

    def tokens_add(self, px, pz, by_z, by_x):
        cut = by_z.shape[0]
        px = jnp.concatenate([px[:cut] + by_z.astype(F32), px[cut:]], 0).astype(BF)
        pz = jnp.concatenate([pz[:cut], pz[cut:] + by_x.astype(F32)], 0).astype(BF)
        return px, pz

    def quarter_masks(self):
        return (0, self.zm, self.xm, self.xm + self.zm)

    def my_quarter(self):
        return 2 * self.bit(self.cbits) + self.bit(0)

    def quarter_groups(self):
        masks = (0, self.zm, self.xm, self.xm + self.zm)
        return [[i | m for m in masks] for i in range(self.n) if i & masks[3] == 0]

    def quarters_in(self, w):
        return lax.all_to_all(w, BOTH, 0, 0, axis_index_groups=self.quarter_groups())

    def quarters_out(self, g):
        return lax.all_to_all(g, BOTH, 0, 0, axis_index_groups=self.quarter_groups())

    def deepen(self, w, held, bits):
        for b in bits[:-1]:
            w = self.pair(b, w, self.one(w, 1 << b), sum(1 for h in held if h > b))
            held.append(b)
        b = bits[-1]
        axis = sum(1 for h in held if h > b)
        held.append(b)
        return Pending(self.one(w, 1 << b), lambda got: self.pair(b, w, got, axis))

    def fold(self, g, held, bits):
        def step(g, b):
            axis = held.index(b)
            held.remove(b)
            give = lax.dynamic_index_in_dim(g, 1 - self.bit(b), axis, keepdims=False)
            keep = lax.dynamic_index_in_dim(g, self.bit(b), axis, keepdims=False)
            finish = lambda got: (keep.astype(F32) + got.astype(F32)).astype(BF)
            return Pending(self.one(give, 1 << b), finish)

        for b in bits[:-1]:
            pending = step(g, b)
            g = pending.finish(pending.got)
        return step(g, bits[-1])


def on_device(
    tokens,
    block_order,
    norm_one,
    w_query,
    b_query,
    w_key,
    b_key,
    w_value,
    b_value,
    w_out,
    norm_two,
    w_gate,
    w_up,
    w_down,
    cotangent,
):
    grid = Grid()
    block_rows, width = tokens.shape
    shard = norm_one.shape[0]
    slot_count = grid.nc
    prompt_slots = slot_count // 2
    head_width = w_key.shape[1]
    query_width = w_query.shape[1]
    head_group = query_width // head_width
    score_scale = head_width ** (-0.5)
    cores = lax.axis_size("tensor")
    own_rows = block_rows // cores
    owners = block_order[0]
    my_block = lax.dynamic_index_in_dim(owners, grid.my_slot, 0, keepdims=False)
    query_anchor = locate(my_block, prompt_slots, block_rows)[1]
    query_pos = query_anchor + jnp.arange(block_rows)

    def own(x):
        return lax.dynamic_slice(x, (grid.core * own_rows, 0), (own_rows, x.shape[1]))

    def others(x):
        return lax.dynamic_slice(x, ((1 - grid.core) * own_rows, 0), (own_rows, x.shape[1]))

    def both(x):
        other = grid.swap(x)
        first = grid.core == 0
        return jnp.concatenate([jnp.where(first, x, other), jnp.where(first, other, x)], 0)

    def summed(part):
        give = lax.dynamic_slice(part, ((1 - grid.core) * own_rows, 0), (own_rows, width))
        return own(part) + grid.swap(give.astype(BF)).astype(F32)

    bias_shard = b_query.shape[1]
    small_bias = b_key.shape[1]
    vector = jnp.concatenate([norm_one[None], norm_two[None], b_query, b_key, b_value], axis=1)
    columns = query_width + 2 * head_width
    vector = jnp.pad(vector, ((0, 7), (0, columns - vector.shape[1])))
    packed = jnp.concatenate(
        [jnp.concatenate([w_query, w_key, w_value], axis=1), vector], axis=0
    )
    hidden = w_gate.shape[1]
    quarter = -(-hidden // (4 * LANES)) * LANES
    pad = ((0, 0), (0, 4 * quarter - hidden))
    w_out_t = lax.all_gather(w_out.T, BOTH, axis=0, tiled=True)

    context_deep = [b for b in grid.deep if b < grid.cbits]
    fsdp_deep = [b for b in grid.deep if b > grid.cbits]

    def quarters(w):
        return w.reshape(shard, 4, quarter).transpose(1, 0, 2)

    def deep_z(w):
        return grid.deepen(w, [0], context_deep)

    def give_y(w):
        return grid.one(w, 1 << fsdp_deep[0])

    def parts_of(*pieces):
        return tuple(x.reshape(grid.n // PARTS * shard, quarter) for x in pieces)

    side = grid.bit(fsdp_deep[0]).reshape(1)
    held = []
    gate_near = grid.quarters_in(quarters(jnp.pad(w_gate, pad)))
    packed = grid.deepen(packed, held, context_deep[::-1])
    gate_near, packed = grid.close(gate_near, packed)

    gate_near = gate_near.reshape(2, 2, shard, quarter)
    packed = grid.close(grid.deepen(packed, held, [0]))

    packed = packed.reshape(grid.nc * (shard + 8), columns)
    (gate_0,) = grid.fence(gate_near[0])
    gx, gy, gate_0 = grid.close(grid.over_x(packed), grid.over_y(packed), deep_z(gate_0))

    cut = gx.shape[0] // 2
    gate_1, up_in = grid.fence(gate_near[1], quarters(jnp.pad(w_up, pad)))
    by_y, by_x = grid.over_y(gx[:cut]), grid.over_x(gy[cut:])
    by_y, by_x, gate_1, up_near = grid.close(
        by_y, by_x, deep_z(gate_1), grid.quarters_in(up_in)
    )

    up_near = up_near.reshape(2, 2, shard, quarter)
    pieces = [packed, gx, gy, jnp.concatenate([by_y, by_x], 0)]
    pieces = [x.reshape(grid.nc, shard + 8, columns) for x in pieces]
    sources = [grid.cbits, grid.cbits + 1]
    w_qkv = grid.ordered([x[:, :shard] for x in pieces], sources)
    w_qkv = w_qkv.reshape(grid.n * shard, columns)
    vectors = grid.ordered([x[:, shard] for x in pieces], sources).reshape(grid.n, columns)
    gain_one = vectors[:, :shard].reshape(-1)
    gain_two = vectors[:, shard : 2 * shard].reshape(-1)
    start = 2 * shard
    bias = jnp.concatenate(
        [
            vectors[:, start : start + bias_shard].reshape(-1),
            vectors[:, start + bias_shard : start + bias_shard + small_bias].reshape(-1),
            vectors[
                :, start + bias_shard + small_bias : start + bias_shard + 2 * small_bias
            ].reshape(-1),
        ]
    ).astype(F32)

    inputs = tokens.astype(F32)
    inv_one = lax.rsqrt(jnp.mean(inputs * inputs, axis=-1, keepdims=True) + EPSILON)
    rows_one = inputs * inv_one
    normed_one = (rows_one * gain_one.astype(F32)).astype(BF)
    cosine, sine = tables(query_pos, head_width)
    grads_own, grads_other = own(cotangent), others(cotangent)
    gate_0, grads_pz = grid.fence(gate_0, grads_own)
    gate_2, grads_pz = give_y(gate_0), grid.over_z(grads_pz)
    qkv = dot_nn(normed_one, w_qkv) + bias
    keys = qkv[:, query_width : query_width + head_width]
    keys = keys * cosine + swap_halves(keys) * sine
    pair = jnp.concatenate([keys, qkv[:, query_width + head_width :]], axis=1).astype(BF)
    pair, qkv, gate_2, grads_pz = grid.close(pair, qkv, gate_2, grads_pz)

    gate_1, grads_px = grid.fence(gate_1, grads_own)
    met = [grid.one(pair, r) for r in range(1, slot_count)]
    gate_3, grads_px, *met = grid.close(give_y(gate_1), grid.over_x(grads_px), *met)
    pairs = [pair] + met

    piece_block = owners[grid.my_slot ^ jnp.arange(slot_count)]
    seen = ((piece_block < prompt_slots) & (piece_block < my_block)).astype(jnp.int32)
    up_0, down_in = grid.fence(up_near[0], quarters(jnp.pad(w_down.T, pad)))
    up_0, down_near = deep_z(up_0), grid.quarters_in(down_in)
    queries, attn_heads, out_low, log_total = attend(
        seen, qkv, cosine, sine, pairs, head_group, score_scale
    )
    out_low, up_0, down_near = grid.close(out_low, up_0, down_near)

    down_near = down_near.reshape(2, 2, shard, quarter)
    hidden_one = own(tokens).astype(F32) + summed(dot_nt(out_low, w_out_t))

    inv_two = lax.rsqrt(jnp.mean(hidden_one * hidden_one, axis=-1, keepdims=True) + EPSILON)
    rows_two = hidden_one * inv_two
    normed_two = (rows_two * gain_two.astype(F32)).astype(BF)
    normed_two = grid.close(normed_two)

    up_0, up_1 = grid.fence(up_0, up_near[1])
    px, pz, normed_other, up_1, up_2 = grid.close(
        grid.over_x(normed_two),
        grid.over_z(normed_two),
        grid.swap(normed_two),
        deep_z(up_1),
        give_y(up_0),
    )

    cut = px.shape[0] // 2
    (down_0,) = grid.fence(down_near[0])
    normed_near = jnp.concatenate([px, pz], 0)
    by_z, by_x, up_3, down_0, normed_swap = grid.close(
        grid.over_z(px[:cut]),
        grid.over_x(pz[cut:]),
        give_y(up_1),
        deep_z(down_0),
        grid.swap(normed_near),
    )

    normed_far = jnp.concatenate([by_z, by_x], 0)
    gate_full = parts_of(gate_0, gate_1, gate_2, gate_3)
    up_full = parts_of(up_0, up_1, up_2, up_3)
    far_swap, grads_swap = grid.close(
        grid.swap(normed_far), grid.swap(jnp.concatenate([grads_px, grads_pz], 0))
    )

    normed_in = jnp.concatenate(
        [normed_two, normed_near, normed_far, normed_other, normed_swap, far_swap], 0
    )
    far_z, far_x, down_0, down_1 = grid.fence(
        grads_px[:cut], grads_pz[cut:], down_0, down_near[1]
    )
    by_z, by_x = grid.over_z(far_z), grid.over_x(far_x)
    down_2, down_1 = give_y(down_0), deep_z(down_1)
    act, by_gate, by_up = hidden_units(side, normed_in, gate_full, up_full)
    act, by_z, by_x, down_2, down_1 = grid.close(act, by_z, by_x, down_2, down_1)

    grads_far = jnp.concatenate([by_z, by_x], 0)
    down_3 = give_y(down_1)
    grads_in = jnp.concatenate(
        [grads_own, grads_px, grads_pz, grads_far, grads_other, grads_swap, grid.swap(grads_far)],
        0,
    )
    grad_wdown = dot_tn(grads_in, act).astype(BF)
    grad_wdown, down_3 = grid.close(grad_wdown, down_3)
    down_full = parts_of(down_0, down_1, down_2, down_3)

    top = sorted(range(grid.cbits + grid.fbits), reverse=True)
    shape = (2,) * len(top) + (shard, quarter)
    y_back, z_back = fsdp_deep[::-1], context_deep[::-1]

    def half(grad, h):
        return lax.index_in_dim(grad.reshape(shape), h, top.index(grid.cbits), keepdims=False)

    def fold_y(grad):
        return grid.fold(grad, [b for b in top if b != grid.cbits], y_back)

    def fold_z(grad):
        return grid.fold(grad, [b for b in top if b not in fsdp_deep and b != grid.cbits], z_back)

    def joined(first, second):
        return jnp.stack([first, second], 0).reshape(4, shard, quarter)

    down_0 = fold_y(half(grad_wdown, 0))
    grad_gate, grad_up = hidden_grads(side, grads_in, down_full, by_gate, by_up)
    down_0, grad_gate, grad_up = grid.close(down_0, grad_gate, grad_up)

    (grad_wdown,) = grid.fence(grad_wdown)
    down_0, down_1 = fold_z(down_0), fold_y(half(grad_wdown, 1))
    part, give = hidden_back(side, (grad_gate, grad_up), (gate_full, up_full))
    down_0, down_1, part, give = grid.close(down_0, down_1, part, give)

    other = grid.swap(give)
    (up_in,) = grid.fence(grad_up)
    grad_wup = dot_tn(normed_in, up_in).astype(BF)
    other, grad_wup = grid.close(other, grad_wup)

    part_own, px, pz, far_z, far_x = grid.tokens_split(part, other)
    down_1, gate_in = grid.fence(down_1, grad_gate)
    by_z, by_x = grid.over_z(far_z), grid.over_x(far_x)
    down_1, up_0 = fold_z(down_1), fold_y(half(grad_wup, 0))
    grad_wgate = dot_tn(normed_in, gate_in).astype(BF)
    by_z, by_x, down_1, up_0, grad_wgate = grid.close(by_z, by_x, down_1, up_0, grad_wgate)

    px, pz = grid.tokens_add(px, pz, by_z, by_x)
    grad_wup, act_in = grid.fence(grad_wup, act)
    px, pz = grid.over_x(px), grid.over_z(pz)
    up_0, up_1 = fold_z(up_0), fold_y(half(grad_wup, 1))
    mlp_part, mlp_give = hidden_back(side, (act_in,), (down_full,))
    px, pz, up_0, up_1, mlp_part, mlp_give = grid.close(
        px, pz, up_0, up_1, mlp_part, mlp_give
    )

    (down_in,) = grid.fence(joined(down_0, down_1))
    grad_wdown = grid.quarters_out(down_in)
    mlp_other = grid.swap(mlp_give)
    grad_normed_two = part_own + px.astype(F32) + pz.astype(F32)
    grad_gain_two = jnp.sum(grad_normed_two * rows_two, axis=0)
    grad_hidden_one = own(cotangent).astype(F32) + norm_back(
        grad_normed_two, rows_two, inv_two, gain_two
    )
    grad_low = both(grad_hidden_one.astype(BF))
    grad_heads = dot_nn(grad_low, w_out_t).astype(BF)
    grad_heads, mlp_other, grad_wdown = grid.close(grad_heads, mlp_other, grad_wdown)

    mlp_own, mx, mz, far_z, far_x = grid.tokens_split(mlp_part, mlp_other)
    grad_wgate, up_1 = grid.fence(grad_wgate, up_1)
    by_z, by_x = grid.over_z(far_z), grid.over_x(far_x)
    gate_0, up_1 = fold_y(half(grad_wgate, 0)), fold_z(up_1)
    grad_query, grad_pairs = attend_back(
        seen,
        queries,
        grad_heads,
        attn_heads,
        log_total,
        cosine,
        sine,
        pairs,
        head_group,
        score_scale,
    )
    by_z, by_x, gate_0, up_1, grad_query, *grad_pairs = grid.close(
        by_z, by_x, gate_0, up_1, grad_query, *grad_pairs
    )

    grad_got = [grid.one(x, r + 1) for r, x in enumerate(grad_pairs[1:])]
    mx, mz = grid.tokens_add(mx, mz, by_z, by_x)
    (grad_wgate,) = grid.fence(grad_wgate)
    mx, gate_1 = grid.over_x(mx), fold_y(half(grad_wgate, 1))
    grad_attn = products(normed_one, grad_query, grad_low, out_low)
    mx, gate_1, grad_attn, *grad_got = grid.close(mx, gate_1, grad_attn, *grad_got)

    far_y, far_x = grid.fsdp_far(grad_attn)
    mz, grad_query, up_in = grid.fence(mz, grad_query, joined(up_0, up_1))
    grad_wup = grid.quarters_out(up_in)
    by_y, by_x = grid.over_y(far_y), grid.over_x(far_x)
    gate_0, mz = fold_z(gate_0), grid.over_z(mz)
    grad_pair = grad_pairs[0]
    for x in grad_got:
        grad_pair = grad_pair + x.astype(F32)
    grad_keys = grad_pair[:, :head_width]
    grad_keys = grad_keys * cosine - swap_halves(grad_keys) * sine
    grad_kv = jnp.concatenate([grad_keys, grad_pair[:, head_width:]], axis=1).astype(BF)
    grad_qkv = jnp.concatenate([grad_query, grad_kv], axis=1)
    grad_bias = jnp.sum(grad_qkv.astype(F32), axis=0)
    grad_normed_one = summed(dot_nt(grad_qkv, w_qkv))
    rows_own = own(rows_one)
    inv_own = own(inv_one)
    grad_gain_one = jnp.sum(grad_normed_one * rows_own, axis=0)
    gains = jnp.concatenate(
        [grad_gain_one.reshape(-1, shard), grad_gain_two.reshape(-1, shard)], axis=1
    )
    gains = gains + grid.swap(gains)
    small = jnp.concatenate(
        [
            gains,
            grad_bias[:query_width].reshape(-1, bias_shard),
            grad_bias[query_width : query_width + head_width].reshape(-1, small_bias),
            grad_bias[query_width + head_width :].reshape(-1, small_bias),
        ],
        axis=1,
    )
    wide = 2 * head_width
    small = jnp.pad(small[:, None], ((0, 0), (0, 7), (0, max(wide - small.shape[1], 0))))
    grad_wkv = dot_tn(normed_one, grad_kv).reshape(grid.n, shard, wide)
    grad_wkv = jnp.concatenate([grad_wkv, small], axis=1).astype(BF)
    grad_wkv = grad_wkv.reshape(grid.n * (shard + 8), wide)
    by_y, by_x, gate_0, mz, grad_wup, grad_wkv, grad_normed_one = grid.close(
        by_y, by_x, gate_0, mz, grad_wup, grad_wkv, grad_normed_one
    )

    ax, ay = grid.fsdp_near(grad_attn, by_y, by_x)
    far_y, far_x = grid.fsdp_far(grad_wkv)
    (gate_1,) = grid.fence(gate_1)
    ax, ay = grid.over_x(ax), grid.over_y(ay)
    by_y, by_x, gate_1 = grid.over_y(far_y), grid.over_x(far_x), fold_z(gate_1)
    grad_inputs = grad_hidden_one + norm_back(grad_normed_one, rows_own, inv_own, gain_one)
    result = (hidden_one + mlp_own + mx.astype(F32) + mz.astype(F32)).astype(BF)
    ax, ay, by_y, by_x, gate_1, grad_tokens, result = grid.close(
        ax, ay, by_y, by_x, gate_1, grad_inputs.astype(BF), result
    )

    grad_attn = grid.fsdp_end(grad_attn, ax, ay)
    kx, ky = grid.fsdp_near(grad_wkv, by_y, by_x)
    (gate_in,) = grid.fence(joined(gate_0, gate_1))
    kx, ky = grid.over_x(kx), grid.over_y(ky)
    parts = [grid.one(grid.context_pick(grad_attn, r), r) for r in range(1, grid.nc)]
    grad_wgate = grid.quarters_out(gate_in)
    grad_tokens, result = both(grad_tokens), both(result)
    kx, ky, grad_wgate, grad_tokens, result, *parts = grid.close(
        kx, ky, grad_wgate, grad_tokens, result, *parts
    )

    grad_wkv = grid.fsdp_end(grad_wkv, kx, ky)
    terms = [grid.one(grid.context_pick(grad_wkv, r), r) for r in range(1, grid.nc)]
    grad_attn = grid.context_pick(grad_attn, 0).astype(F32)
    for x in parts:
        grad_attn = grad_attn + x.astype(F32)
    grad_wkv = grid.context_pick(grad_wkv, 0).astype(F32)
    for x in terms:
        grad_wkv = grad_wkv + x.astype(F32)
    small = grad_wkv[shard : shard + 1]
    grad_wkv = grad_wkv[:shard]
    grad_wdown, grad_wup, grad_wgate = [
        g.transpose(1, 0, 2).reshape(shard, 4 * quarter).astype(F32)
        for g in (grad_wdown, grad_wup, grad_wgate)
    ]
    return (
        result,
        grad_tokens,
        small[0, :shard],
        grad_attn[:, :query_width],
        small[:, start : start + bias_shard],
        grad_wkv[:, :head_width],
        small[:, start + bias_shard : start + bias_shard + small_bias],
        grad_wkv[:, head_width:],
        small[:, start + bias_shard + small_bias : start + bias_shard + 2 * small_bias],
        grad_attn[:, query_width : 2 * query_width].T,
        small[0, shard : 2 * shard],
        grad_wgate[:, :hidden],
        grad_wup[:, :hidden],
        grad_wdown[:, :hidden].T,
    )


def solution(mesh):
    rows = P(("fsdp", "context"), None)
    split = P(("fsdp", "context"))
    into = P(("fsdp", "context"), "tensor")
    back = P("tensor", ("fsdp", "context"))
    return jax.shard_map(
        on_device,
        mesh=mesh,
        in_specs=(
            rows,
            P("fsdp", None),
            split,
            into,
            back,
            into,
            back,
            into,
            back,
            back,
            split,
            into,
            into,
            back,
            rows,
        ),
        out_specs=(
            rows,
            rows,
            split,
            into,
            back,
            into,
            back,
            into,
            back,
            back,
            split,
            into,
            into,
            back,
        ),
        check_vma=False,
    )
```
